32 devices in a mesh: dp: 4 (over y, x), seq: 8 (over z, core).
Axes of the slice: x: 2, y: 2, z: 4, core: 2. Of those that a mesh axis runs over, the one named last changes fastest.
Arguments:
- hidden: float32 [4, 2048, 768], P('dp', 'seq'), may hold values from -6 to 6
- cotangent: float32 [4, 2048, 768], P('dp', 'seq'), may hold values from -6 to 6
- lengths: int32 [4], P('dp'), may hold values from 1024 to 2048, as said below
- norm_gain: float32 [2, 768], P(None, 'dp'), may hold values from 0.5 to 1.5
- gate_weight: float32 [2, 768, 1536], P(None, 'dp'), may hold values from -0.21875 to 0.21875
- mix_weight: float32 [2, 768, 1792], P(None, 'dp'), may hold values from -0.21875 to 0.21875
- step_weight: float32 [2, 768, 24], P(None, 'dp'), may hold values from -0.21875 to 0.21875
- conv_kernel: float32 [2, 4, 1792], P(None, None, 'dp'), may hold values from -0.5 to 0.5
- conv_bias: float32 [2, 1792], P(None, 'dp'), may hold values from -0.5 to 0.5
- gated_gain: float32 [2, 1536], P(None, 'dp'), may hold values from 0.5 to 1.5
- out_weight: float32 [2, 1536, 768], P(None, 'dp'), may hold values from -0.15625 to 0.15625
- skip_gain: float32 [2, 24], replicated, may hold values from 0.5 to 1.5
- log_rate: float32 [2, 24], replicated, may hold values from -4 to 1
- step_bias: float32 [2, 24], replicated, may hold values from -9 to -4
Outputs:
- result: float32 [4, 2048, 768], P('dp', 'seq')
- hidden_grad: float32 [4, 2048, 768], P('dp', 'seq')
- norm_gain_grad: float32 [2, 768], P(None, 'dp')
- gate_weight_grad: float32 [2, 768, 1536], P(None, 'dp')
- mix_weight_grad: float32 [2, 768, 1792], P(None, 'dp')
- step_weight_grad: float32 [2, 768, 24], P(None, 'dp')
- conv_kernel_grad: float32 [2, 4, 1792], P(None, None, 'dp')
- conv_bias_grad: float32 [2, 1792], P(None, 'dp')
- gated_gain_grad: float32 [2, 1536], P(None, 'dp')
- out_weight_grad: float32 [2, 1536, 768], P(None, 'dp')
- skip_gain_grad: float32 [2, 24], replicated
The draws below stay inside these ranges and needn't reach their ends.
Inputs may be any that keep to these rules, and one draw needn't show every extreme that they name: `lengths`: positions at or past a slot's length are padding; some slot has length 2048 and some slot the least length.
All inputs are finite; a program needn't handle non-finite values.
Results may differ from the reference program's by a relative error of at most 0.0003.
Values sent between devices are 32-bit elements; how exact they have to be, the bound alone decides.
A program may use at most 192 MiB of HBM per device.

```python
import jax
import jax.numpy as jnp
from jax import lax

D = 768
DI = 1536
H = 24
P_SIZE = 64
NS = 128
K = 4
GROUP = 256
LAYERS = 2
LEN_MIN = 1024
CW = 1792
SLOTS = 4
SEQ_LEN = 2048


def draw_lengths(key, part):
    floor_len = min(LEN_MIN, SEQ_LEN)
    key_draw, key_long, key_short = jax.random.split(key, 3)
    values = jax.random.randint(key_draw, (SLOTS,), floor_len, SEQ_LEN + 1)
    longest = jax.random.randint(key_long, (), 0, SLOTS)
    shortest = (longest + 1 + jax.random.randint(key_short, (), 0, SLOTS - 1)) % SLOTS
    slot_index = jnp.arange(SLOTS)
    values = jnp.where(slot_index == longest, SEQ_LEN, values)
    values = jnp.where(slot_index == shortest, floor_len, values)
    return values.astype(jnp.int32)


def block_levels(own_key, dims, cuts, smallest, top_value):
    loudness, own = 1.0, jax.random.fold_in(own_key, 6)
    for dim, parts in cuts:
        steps = jnp.exp(jax.random.uniform(jax.random.fold_in(own, dim), (parts,), jnp.float32, smallest / len(cuts), top_value / len(cuts)))
        loudness = loudness * jnp.repeat(steps, dims[dim] // parts).reshape([-1 if axis == dim else 1 for axis in range(len(dims))])
    return loudness


def bell_draw(key, shape, scale, bound, cuts=(), kind=jnp.bfloat16):
    drawn = jax.random.normal(key, shape, jnp.float32) * scale
    if len(cuts) > 0:
        drawn = block_levels(key, shape, cuts, -0.22, 0.18) * drawn
    return jnp.clip(drawn, min=-bound, max=bound).astype(kind)


def setup_inputs(seed: int = 0) -> dict:
    streams_of = jax.random.split(jax.random.key(seed), 15)
    return {
        "hidden": bell_draw(streams_of[0], (SLOTS, SEQ_LEN, D), 1.0, 6.0, ((0, 4), (1, 8)), jnp.float32),
        "cotangent": bell_draw(streams_of[1], (SLOTS, SEQ_LEN, D), 1.0, 6.0, ((0, 4), (1, 8)), jnp.float32),
        "lengths": draw_lengths(jax.random.fold_in(streams_of[14], 71), 0),
        "norm_gain": jnp.clip(1.0 + 0.1 * jax.random.normal(streams_of[3], (LAYERS, D), jnp.float32), 0.5, 1.5),
        "gate_weight": bell_draw(streams_of[4], (LAYERS, D, DI), D ** -0.5, 0.21875, ((1, 4),), jnp.float32),
        "mix_weight": bell_draw(streams_of[5], (LAYERS, D, CW), D ** -0.5, 0.21875, ((1, 4),), jnp.float32),
        "step_weight": bell_draw(streams_of[6], (LAYERS, D, H), D ** -0.5, 0.21875, ((1, 4),), jnp.float32),
        "conv_kernel": jnp.clip(jax.random.uniform(streams_of[7], (LAYERS, K, CW), jnp.float32, -0.5, 0.5) * block_levels(streams_of[7], (LAYERS, K, CW), ((2, 4),), -0.4, 0.0), -0.5, 0.5),
        "conv_bias": jnp.clip(jax.random.uniform(streams_of[8], (LAYERS, CW), jnp.float32, -0.5, 0.5) * block_levels(streams_of[8], (LAYERS, CW), ((1, 4),), -0.4, 0.0), -0.5, 0.5),
        "gated_gain": jnp.clip(1.0 + 0.1 * jax.random.normal(streams_of[9], (LAYERS, DI), jnp.float32), 0.5, 1.5),
        "out_weight": bell_draw(streams_of[10], (LAYERS, DI, D), DI ** -0.5, 0.15625, ((1, 4),), jnp.float32),
        "skip_gain": jnp.clip(jax.random.uniform(streams_of[11], (LAYERS, H), jnp.float32, 0.5, 1.5), 0.5, 1.5),
        "log_rate": jnp.clip(jax.random.uniform(streams_of[12], (LAYERS, H), jnp.float32, -4.0, 1.0), -4.0, 1.0),
        "step_bias": jnp.clip(jax.random.uniform(streams_of[13], (LAYERS, H), jnp.float32, -9.0, -4.0), -9.0, -4.0),
    }


@jax.custom_vjp
def low(v):
    return lax.optimization_barrier(v.astype(jnp.bfloat16)).astype(jnp.float32)

@jax.custom_vjp
def low_back(v):
    return v

def low_keep(v):
    return (low(v), None)

def low_pass(kept, grad):
    return (grad,)

def back_keep(v):
    return (v, None)

def back_low(kept, grad):
    return (low(grad),)
low.defvjp(low_keep, low_pass)
low_back.defvjp(back_keep, back_low)
EPSILON = 1e-05
HIGHEST = lax.Precision.HIGHEST

def rms_scale(values):
    return lax.rsqrt(lax.optimization_barrier(jnp.mean(values * values, axis=-1, keepdims=True)) + EPSILON)

def block_step(state_in, pieces, rates):
    heads_in, step_size, input_map, output_map = pieces
    log_decay = jnp.cumsum(-rates * step_size, axis=0)
    scaled_in = heads_in * step_size[:, :, None]
    position = lax.iota(jnp.int32, GROUP)
    causal = (position[:, None] >= position[None, :])[:, :, None]
    gaps = log_decay[:, None, :] - log_decay[None, :, :]
    decays = jnp.where(causal, jnp.exp(jnp.where(causal, gaps, 0.0)), 0.0)
    intersection = jnp.dot(output_map, input_map.T, precision=HIGHEST)
    mixing = intersection[:, :, None] * decays
    diag_out = jnp.einsum('tsh,shp->thp', mixing, scaled_in, precision=HIGHEST)
    off_out = jnp.exp(log_decay)[:, :, None] * jnp.einsum('tn,hpn->thp', output_map, state_in, precision=HIGHEST)
    end_weight = jnp.exp(log_decay[-1:, :] - log_decay)
    state_local = jnp.einsum('shp,sn->hpn', scaled_in * end_weight[:, :, None], input_map, precision=HIGHEST)
    state_next = jnp.exp(log_decay[-1, :])[:, None, None] * state_in + state_local
    return (state_next, diag_out + off_out)

def mamba_layer(stream, params, fixed, layer_index):
    norm_gain, gate_weight, mix_weight, step_weight, conv_kernel, conv_bias, gated_gain, out_weight, skip_gain = [array[layer_index] for array in params]
    log_rate = fixed[0][layer_index]
    step_bias = fixed[1][layer_index]
    normed = stream * rms_scale(stream) * norm_gain
    gate_pre = jnp.dot(normed, gate_weight, precision=HIGHEST)
    mixed_raw = jnp.dot(normed, mix_weight, precision=HIGHEST)
    step_raw = jnp.dot(normed, step_weight, precision=HIGHEST)
    padded = jnp.concatenate([jnp.zeros((K - 1, CW), jnp.float32), mixed_raw], axis=0)
    conv_pre = conv_bias
    for tap_index in range(K):
        conv_pre = conv_pre + conv_kernel[tap_index] * padded[tap_index:tap_index + SEQ_LEN]
    mixed = jax.nn.silu(conv_pre)
    heads_in = mixed[:, :DI].reshape(SEQ_LEN, H, P_SIZE)
    input_map = mixed[:, DI:DI + NS]
    output_map = mixed[:, DI + NS:]
    step_size = jax.nn.softplus(step_raw + step_bias)
    blocks = SEQ_LEN // GROUP
    pieces = (heads_in.reshape(blocks, GROUP, H, P_SIZE), step_size.reshape(blocks, GROUP, H), input_map.reshape(blocks, GROUP, NS), output_map.reshape(blocks, GROUP, NS))
    rates = jnp.exp(log_rate)

    def advance(state_in, piece):
        return block_step(state_in, piece, rates)
    unused, outputs = lax.scan(jax.checkpoint(advance), jnp.zeros((H, P_SIZE, NS), jnp.float32), pieces)
    mixed_out = outputs.reshape(SEQ_LEN, H, P_SIZE) + skip_gain[:, None] * heads_in
    gated = mixed_out.reshape(SEQ_LEN, DI) * jax.nn.silu(gate_pre)
    normed_out = gated * rms_scale(gated) * gated_gain
    return stream + jnp.dot(normed_out, out_weight, precision=HIGHEST)

def reference(hidden, cotangent, lengths, norm_gain, gate_weight, mix_weight, step_weight, conv_kernel, conv_bias, gated_gain, out_weight, skip_gain, log_rate, step_bias):
    params = (norm_gain, gate_weight, mix_weight, step_weight, conv_kernel, conv_bias, gated_gain, out_weight, skip_gain)
    fixed = (log_rate, step_bias)
    position = jnp.arange(SEQ_LEN).astype(jnp.int32)

    def per_slot(running, slot_items):
        seq_in, seq_cot, length = slot_items
        mask = (position < length).astype(jnp.float32)[:, None]

        def forward(stream, *weights):
            for layer_index in range(LAYERS):
                stream = mamba_layer(stream, weights, fixed, layer_index)
            return stream * mask
        result, pullback = jax.vjp(forward, seq_in, *params)
        gradients = pullback(seq_cot)
        running = tuple((total + update for total, update in zip(running, gradients[1:])))
        return (running, (result, gradients[0]))
    initial = tuple((jnp.zeros_like(array) for array in params))
    running, (results, input_grads) = lax.scan(per_slot, initial, (hidden, cotangent, lengths))
    return (results, input_grads) + running
```

```python
import functools

import jax
import jax.numpy as jnp
from jax import lax
from jax.experimental import pallas as pl
from jax.experimental.pallas import tpu as pltpu
from jax.sharding import PartitionSpec as P

EPSILON = 1e-05
HIGH = lax.Precision.HIGH
MESH = pl.DeviceIdType.MESH
LANES = 128
F32 = jnp.float32


def mm(left, right, contract=((1,), (0,))):
    return lax.dot_general(left, right, (contract, ((), ())), precision=HIGH, preferred_element_type=F32)


NN = ((1,), (0,))
NT = ((1,), (1,))
TN = ((0,), (0,))


def split(value):
    high = value.astype(jnp.bfloat16)
    return high, (value - high.astype(F32)).astype(jnp.bfloat16)


def split3(value):
    first = value.astype(jnp.bfloat16)
    rest = value - first.astype(F32)
    second = rest.astype(jnp.bfloat16)
    third = (rest - second.astype(F32)).astype(jnp.bfloat16)
    return first, second, third


def exact(select, value, contract=((1,), (0,))):
    total = None
    for part in split3(value):
        term = lax.dot_general(select, part, (contract, ((), ())), preferred_element_type=F32)
        total = term if total is None else total + term
    return total


def exact_right(value, select, contract=((1,), (0,))):
    total = None
    for part in split3(value):
        term = lax.dot_general(part, select, (contract, ((), ())), preferred_element_type=F32)
        total = term if total is None else total + term
    return total


def iota(shape, axis):
    return lax.broadcasted_iota(jnp.int32, shape, axis)


def head_matrix(heads_padded, width, head_size, start=0):
    head = iota((heads_padded, width), 0)
    channel = iota((heads_padded, width), 1) + start
    inside = jnp.logical_and(channel >= head * head_size, channel < (head + 1) * head_size)
    return jnp.where(inside, 1.0, 0.0).astype(jnp.bfloat16)


def tri(size):
    return jnp.where(iota((size, size), 0) >= iota((size, size), 1), 1.0, 0.0)


def sigmoid(v):
    return jax.nn.sigmoid(v)


def softplus(v):
    return jnp.maximum(v, 0.0) + jnp.log1p(jnp.exp(-jnp.abs(v)))


def tiles(count, body):
    lax.fori_loop(0, count, lambda i, c: (body(i), c)[1], 0)


def lanes(i, width):
    return pl.ds(pl.multiple_of(i * width, width), width)


class Place:
    def __init__(self, dp_count, seq_count):
        self.n_dp, self.n_seq = dp_count, seq_count
        self.dp = lax.axis_index("dp")
        self.seq = lax.axis_index("seq")
        self.core = self.seq % 2
        self.z = self.seq // 2
        self.sib = self.z * 2 + (1 - self.core)
        self.parity = self.z % 2
        self.pair = (self.z + 1 - 2 * self.parity) * 2 + self.core
        y, x = self.dp // 2, self.dp % 2
        self.dpx = 2 * y + (1 - x)
        self.dpy = 2 * (1 - y) + x
        self.dpd = 2 * (1 - y) + (1 - x)


def remote(src, dst, send, recv, dp, seq):
    return pltpu.make_async_remote_copy(
        src_ref=src, dst_ref=dst, send_sem=send, recv_sem=recv, device_id=(dp, seq), device_id_type=MESH
    )


def entry_barrier(place):
    barrier = pltpu.get_barrier_semaphore()

    def greet(dp, seq):
        pl.semaphore_signal(barrier, inc=1, device_id=(dp, seq), device_id_type=MESH)

    for step in range(1, place.n_dp):
        greet((place.dp + step) % place.n_dp, place.seq)
    greet(place.dp, place.sib)
    greet(place.dp, place.pair)

    @pl.when(jnp.logical_and(place.core == 1, place.seq < place.n_seq - 1))
    def _():
        greet(place.dp, place.seq + 1)

    @pl.when(jnp.logical_and(place.core == 0, place.seq > 0))
    def _():
        greet(place.dp, place.seq - 1)

    outer = jnp.logical_or(place.seq == 0, place.seq == place.n_seq - 1)

    @pl.when(outer)
    def _():
        pl.semaphore_wait(barrier, place.n_dp + 1)

    @pl.when(jnp.logical_not(outer))
    def _():
        pl.semaphore_wait(barrier, place.n_dp + 2)


def full_barrier(place):
    barrier = pltpu.get_barrier_semaphore()
    for step in range(1, place.n_dp):
        peer = (place.dp + step) % place.n_dp
        pl.semaphore_signal(barrier, inc=1, device_id=(peer, place.seq), device_id_type=MESH)
    for step in range(1, place.n_seq):
        peer = (place.seq + step) % place.n_seq
        pl.semaphore_signal(barrier, inc=1, device_id=(place.dp, peer), device_id_type=MESH)
    pl.semaphore_wait(barrier, place.n_dp + place.n_seq - 2)


class Gather:
    def __init__(self, place, own, dest, stride, row_of, columns, half, sems, index):
        self.p, self.own, self.dest = place, own, dest
        self.stride, self.row_of, self.columns = stride, row_of, columns
        self.send, self.recv = sems
        self.index = index
        self.half = half
        self.third = half // 3
        self.wide = place.n_dp == 4 and half % 24 == 0 and place.n_seq % 4 == 0

    def at(self, owner, core, offset, count):
        start = owner * self.stride + self.row_of(core) + offset
        return self.dest.at[pl.ds(pl.multiple_of(start, 8), count), self.columns]

    def copy(self, kind, src, dst, dp, seq):
        return remote(src, dst, self.send.at[self.index, kind], self.recv.at[self.index, kind], dp, seq)

    def own_part(self, offset, count):
        start = self.row_of(self.p.core) + offset
        return self.own.at[pl.ds(pl.multiple_of(start, 8), count), self.columns]

    def get(self, kind):
        p, t = self.p, self.third
        if not self.wide:
            if kind < p.n_dp:
                peer = (p.dp + kind) % p.n_dp
                return self.copy(
                    kind, self.own_part(0, self.half), self.at(p.dp, p.core, 0, self.half), peer, p.seq
                )
            owner = (p.dp + 2 * p.n_dp - 1 - kind) % p.n_dp
            part = self.at(owner, p.core, 0, self.half)
            return self.copy(kind, part, part, p.dp, p.sib)
        first = p.parity * t
        only = 2 * t * p.parity
        miss = 2 * t * (1 - p.parity)
        if kind < 2:
            return self.copy(
                kind, self.own_part(first, 2 * t), self.at(p.dp, p.core, first, 2 * t),
                p.dpx if kind == 0 else p.dpy, p.seq,
            )
        owner, offset, count, dp, seq = {
            2: (p.dpx, first, t, p.dpy, p.seq),
            3: (p.dpy, first + t, t, p.dpx, p.seq),
            4: (p.dpx, only, t, p.dp, p.pair),
            5: (p.dpy, only, t, p.dp, p.pair),
            6: (p.dpd, only, t, p.dp, p.pair),
            7: (p.dpx, first, 2 * t, p.dp, p.sib),
            8: (p.dpy, first, 2 * t, p.dp, p.sib),
            9: (p.dpd, first, 2 * t, p.dp, p.sib),
            10: (p.dpx, miss, t, p.dp, p.sib),
            11: (p.dpy, miss, t, p.dp, p.sib),
            12: (p.dpd, miss, t, p.dp, p.sib),
        }[kind]
        part = self.at(owner, p.core, offset, count)
        return self.copy(kind, part, part, dp, seq)

    def stage(self, number):
        n = self.p.n_dp
        if not self.wide:
            if number == 0:
                for kind in range(1, n):
                    self.get(kind).start()
            elif number == 1:
                for kind in range(1, n):
                    self.get(kind).wait_recv()
                    self.get(n - 1 + kind).start()
            elif number == 4:
                for kind in range(n, 2 * n - 1):
                    self.get(kind).wait_recv()
            elif number == 5:
                for kind in range(1, 2 * n - 1):
                    self.get(kind).wait_send()
            return
        if number == 0:
            self.get(0).start()
            self.get(1).start()
        elif number == 1:
            self.get(0).wait_recv()
            for kind in (2, 4, 7):
                self.get(kind).start()
            self.get(1).wait_recv()
            for kind in (3, 5, 8):
                self.get(kind).start()
        elif number == 2:
            self.get(2).wait_recv()
            self.get(3).wait_recv()
            for kind in (6, 9):
                self.get(kind).start()
        elif number == 3:
            for kind in (4, 5, 6):
                self.get(kind).wait_recv()
                self.get(kind + 6).start()
        elif number == 4:
            for kind in range(7, 13):
                self.get(kind).wait_recv()
        else:
            for kind in range(13):
                self.get(kind).wait_send()


GATHER_OFFSETS = (0, 2, 4, 6, 7, 9)
PIECE = 384


def kinds_of(n_dp):
    return max(13, 2 * n_dp)


def forward_kernel(n_dp, n_seq, dims, *refs):
    (
        x_hbm, mask_ref, conv_ref, head_ref, wm_own, wg_own, wo_own,
        result_ref, conv_full, xs_out, gate_out, ext_out, step_out, mo_out, sin_out, sout_out, wm_out, wg_out, wo_out,
        WM, WG, WO, xs, gate, ext, step, mo, sin, sout, conv_in, mixed, diag, ldE, dtE, ldT, gm,
        g_send, g_recv, g_local, c_send, c_recv, e_send, e_recv, r_send, r_recv, o_sem,
    ) = refs
    T, D, DI, CW, H, PS, N, K = dims
    layers = 2
    place = Place(n_dp, n_seq)
    h = D // n_dp // 2
    mix_pieces, gate_pieces, across = (CW + LANES) // PIECE, DI // PIECE, D // PIECE
    out_pieces = 2 * across
    per_layer = mix_pieces + gate_pieces + out_pieces
    early = mix_pieces + gate_pieces
    done_at = GATHER_OFFSETS[4]

    def tick(t):
        for number in reversed(range(len(GATHER_OFFSETS))):
            job = t - GATHER_OFFSETS[number]
            layer, q = job // per_layer, job % per_layer
            inside = jnp.logical_and(job >= 0, job < 2 * per_layer)

            def run(own, dest, stride, row_of, column, number=number, job=job, layer=layer):
                piece = Gather(
                    place, own.at[layer], dest.at[layer], stride, row_of, lanes(column, PIECE), h, (g_send, g_recv), job
                )
                piece.stage(number)

            @pl.when(jnp.logical_and(inside, q < mix_pieces))
            def _():
                run(wm_own, WM, 2 * h, lambda core: core * h, q)

            @pl.when(jnp.logical_and(inside, jnp.logical_and(q >= mix_pieces, q < early)))
            def _():
                run(wg_own, WG, 2 * h, lambda core: core * h, q - mix_pieces)

            @pl.when(jnp.logical_and(inside, q >= early))
            def _():
                part = (q - early) // across
                run(wo_own, WO, 4 * h, lambda core: core * 2 * h + part * h, (q - early) % across)

    def own_copy(kind, layer):
        own, dest = ((wm_own, WM), (wg_own, WG), (wo_own, WO))[kind]
        rows = own.shape[1]
        start = pl.multiple_of(place.dp * rows, 8)
        return pltpu.make_async_copy(own.at[layer], dest.at[layer, pl.ds(start, rows)], g_local.at[layer * 3 + kind])

    first_in = pltpu.make_async_copy(x_hbm, xs.at[0], o_sem.at[0])
    first_in.start()
    ext[0, 0:8, :] = jnp.zeros((8, CW), F32)
    ext[1, 0:8, :] = jnp.zeros((8, CW), F32)
    entry_barrier(place)
    tick(0)
    for layer in range(layers):
        for kind in range(3):
            own_copy(kind, layer).start()

    def conv_copy(step_index):
        peer = (place.dp + step_index) % n_dp
        return remote(
            conv_ref, conv_in.at[place.dp], c_send.at[step_index - 1], c_recv.at[step_index - 1], peer, place.seq
        )

    for s in range(1, n_dp):
        conv_copy(s).start()
    conv_in[place.dp] = conv_ref[...]
    first_in.wait()
    tiles(done_at, lambda i: tick(i + 1))
    per_body = mix_pieces + 4 + H // 4 + gate_pieces + across
    ti, tj = iota((T, T), 0), iota((T, T), 1)
    lane_low = iota((T, LANES), 1) < PS
    CHUNK = 256
    chunks = DI // CHUNK

    def saved_copies(layer):
        saved = (
            (gate, gate_out), (ext, ext_out), (step, step_out), (mo, mo_out), (sin, sin_out), (sout, sout_out),
            (WM, wm_out), (WG, wg_out), (WO, wo_out),
        )
        return [
            pltpu.make_async_copy(a.at[layer], b.at[layer], o_sem.at[layer * 9 + k + 1])
            for k, (a, b) in enumerate(saved)
        ]

    def layer_body(layer, carry):
        x_all = xs[layer]
        inv = lax.rsqrt(jnp.mean(x_all * x_all, axis=-1, keepdims=True) + EPSILON)
        diag[:, 0:D] = x_all * inv
        head = head_ref[layer]
        base = done_at + 1 + layer * per_body
        own_copy(0, layer).wait()

        def project_mix(i):
            ext[layer, 8 : T + 8, lanes(i, PIECE)] = mm(diag[:, 0:D], WM[layer, :, lanes(i, PIECE)])
            tick(base + i)

        tiles(mix_pieces - 1, project_mix)
        last = (mix_pieces - 1) * PIECE
        value = mm(diag[:, 0:D], WM[layer, :, last : last + PIECE])
        ext[layer, 8 : T + 8, last:CW] = value[:, 0 : CW - last]
        raw = value[:, CW - last :]
        edge = remote(
            ext.at[layer, pl.ds(T, 8)], ext.at[layer, pl.ds(0, 8)], e_send.at[layer], e_recv.at[layer],
            place.dp, place.seq + 1,
        )

        @pl.when(place.seq < n_seq - 1)
        def _():
            edge.start()

        step[layer] = raw
        tick(base + mix_pieces - 1)
        dt = softplus(raw + head[1:2, :])
        rate = -jnp.exp(head[0:1, :]) * dt
        ld = exact(tri(T).astype(jnp.bfloat16), rate)
        ldT[...] = ld.T
        tick(base + mix_pieces)

        def expand(i):
            select = head_matrix(LANES, 256, PS, i * 256)
            ldE[:, lanes(i, 256)] = exact_right(ld, select)
            dtE[:, lanes(i, 256)] = exact_right(dt, select)

        tiles(DI // 256, expand)
        tick(base + mix_pieces + 1)

        @pl.when(layer == 0)
        def _():
            for s in range(1, n_dp):
                conv_copy(s).wait_recv()

            def sum_taps(i):
                at = lanes(i, 256)
                taps = conv_in[0, :, at]
                for s in range(1, n_dp):
                    taps = taps + conv_in[s, :, at]
                conv_full[:, at] = taps

            tiles(CW // 256, sum_taps)

        @pl.when(place.seq > 0)
        def _():
            edge.wait_recv()

        def conv(i):
            at = lanes(i, 256)
            taps = conv_full[pl.ds(pl.multiple_of(layer * 8, 8), 8), at]
            total = taps[K : K + 1, :]
            for k in range(K):
                total = total + taps[k : k + 1, :] * ext[layer, 8 - K + 1 + k : 8 - K + 1 + k + T, at]
            mixed[:, at] = total * sigmoid(total)

        tiles(CW // 256, conv)
        tick(base + mix_pieces + 2)
        b_map = mixed[:, DI : DI + N]
        c_map = mixed[:, DI + N : DI + 2 * N]
        gm[...] = jnp.where(ti >= tj, mm(c_map, b_map, NT), 0.0)

        def local_state(i):
            at = lanes(i, 256)
            l_tile = ldE[:, at]
            weighted = mixed[:, at] * dtE[:, at] * jnp.exp(l_tile[T - 1 : T, :] - l_tile)
            sout[layer, :, at] = mm(b_map, weighted, TN)

        tiles(DI // 256, local_state)
        tick(base + mix_pieces + 3)

        def relay_copy(chunk):
            at = lanes(chunk, CHUNK)
            return remote(
                sout.at[layer, :, at], sin.at[layer, :, at], r_send.at[layer, chunk], r_recv.at[layer, chunk],
                place.dp, place.seq + 1,
            )

        def relay(chunk):
            at = lanes(chunk, CHUNK)

            @pl.when(place.seq > 0)
            def _():
                relay_copy(chunk).wait_recv()
                total = jnp.exp(ldE[T - 1 : T, at])
                sout[layer, :, at] = sout[layer, :, at] + total * sin[layer, :, at]

            @pl.when(place.seq == 0)
            def _():
                sin[layer, :, at] = jnp.zeros((N, CHUNK), F32)

            @pl.when(place.seq < n_seq - 1)
            def _():
                relay_copy(chunk).start()

        pairs = H // 2

        def diagonal(i):
            @pl.when(i == place.seq * pairs // n_seq)
            def _():
                tiles(chunks, relay)

            at = lanes(i, LANES)
            scaled = mixed[:, at] * dtE[:, at]
            l_tile = ldE[:, at]
            parts = []
            for side in range(2):
                column = l_tile[:, side * PS : side * PS + 1]
                row = ldT[pl.ds(2 * i + side, 1), :]
                weights = gm[...] * jnp.exp(jnp.minimum(column - row, 0.0))
                parts.append(mm(weights, scaled))
            diag[:, at] = jnp.where(lane_low, parts[0], parts[1])

            @pl.when(i % 2 == 1)
            def _():
                tick(base + mix_pieces + 4 + i // 2)

        tiles(pairs, diagonal)

        def skip_row(i):
            return exact_right(head[2:3, :], head_matrix(LANES, 256, PS, i * 256))

        def gate_proj(i):
            at = lanes(i, PIECE)
            gate[layer, :, at] = mm(xs[layer] * inv, WG[layer, :, at])
            tick(base + mix_pieces + 4 + H // 4 + i)

        def off(i):
            at = lanes(i, 256)
            lift = jnp.exp(ldE[:, at])
            out = diag[:, at] + lift * mm(c_map, sin[layer, :, at]) + skip_row(i) * mixed[:, at]
            mo[layer, :, at] = out

        tiles(DI // 256, off)
        own_copy(1, layer).wait()
        tiles(gate_pieces, gate_proj)

        def gating(i, squares):
            at = lanes(i, LANES)
            pre = gate[layer, :, at]
            gated = mo[layer, :, at] * (pre * sigmoid(pre))
            diag[:, at] = gated
            return squares + gated * gated

        squares = lax.fori_loop(0, DI // LANES, gating, jnp.zeros((T, LANES), F32))
        inv_out = lax.rsqrt(jnp.sum(squares, axis=-1, keepdims=True) / DI + EPSILON)
        own_copy(2, layer).wait()

        def project_out(i):
            at = lanes(i, PIECE)
            tick(base + mix_pieces + 4 + H // 4 + gate_pieces + i)
            branch = mm(diag[...] * inv_out, WO[layer, :, at])
            nxt = xs[layer, :, at] + branch
            xs[layer + 1, :, at] = nxt

        tiles(across, project_out)
        for copy in saved_copies(layer):
            copy.start()
        @pl.when(place.seq < n_seq - 1)
        def _():
            edge.wait_send()
            tiles(chunks, lambda c: relay_copy(c).wait_send())

        return carry

    lax.fori_loop(0, layers, layer_body, 0)
    done = done_at + 1 + layers * per_body
    left = layers * per_layer + GATHER_OFFSETS[5] - done
    if left > 0:
        tiles(left, lambda i: tick(done + i))
    result_ref[...] = xs[layers] * mask_ref[...]
    last = pltpu.make_async_copy(xs.at[1], xs_out, o_sem.at[0])
    last.start()
    for s in range(1, n_dp):
        conv_copy(s).wait_send()
    for layer in range(layers):
        for copy in saved_copies(layer):
            copy.wait()
    last.wait()


def forward(x, mask, conv, head, wm, wg, wo, n_dp, n_seq, dims):
    T, D, DI, CW, H, PS, N, K = dims
    any_spec = pl.BlockSpec(memory_space=pl.ANY)
    vmem = pl.BlockSpec(memory_space=pltpu.VMEM)
    CX = CW + LANES
    kinds = kinds_of(n_dp)
    PIECES = 2 * ((CW + LANES) // PIECE + DI // PIECE + 2 * (D // PIECE))
    sd = lambda *s: jax.ShapeDtypeStruct(s, F32)
    v = lambda *s: pltpu.VMEM(s, F32)
    dma = pltpu.SemaphoreType.DMA
    return pl.pallas_call(
        functools.partial(forward_kernel, n_dp, n_seq, dims),
        out_shape=(
            sd(T, D), sd(16, CW), sd(T, D), sd(2, T, DI), sd(2, T + 8, CW), sd(2, T, LANES), sd(2, T, DI), sd(2, N, DI),
            sd(2, N, DI), sd(2, D, CX), sd(2, D, DI), sd(2, DI, D),
        ),
        in_specs=[any_spec, vmem, vmem, vmem, any_spec, any_spec, any_spec],
        out_specs=(vmem, vmem) + (any_spec,) * 10,
        scratch_shapes=[
            v(2, D, CX), v(2, D, DI), v(2, DI, D), v(3, T, D), v(2, T, DI), v(2, T + 8, CW), v(2, T, LANES),
            v(2, T, DI), v(2, N, DI), v(2, N, DI), v(n_dp, 16, CW), v(T, CW), v(T, DI), v(T, DI), v(T, DI),
            v(LANES, T), v(T, T),
            dma((PIECES, kinds)), dma((PIECES, kinds)), dma((6,)), dma((n_dp - 1,)), dma((n_dp - 1,)), dma((2,)), dma((2,)),
            dma((2, DI // 256)), dma((2, DI // 256)), dma((19,)),
        ],
        compiler_params=pltpu.CompilerParams(
            collective_id=0, has_side_effects=True, vmem_limit_bytes=61 << 20
        ),
        name="forward",
    )(x, mask, conv, head, wm, wg, wo)


def prepare(hidden, lengths, norm_gain, gate_weight, mix_weight, step_weight, conv_kernel, conv_bias, gated_gain,
            out_weight, skip_gain, log_rate, step_bias, n_dp):
    T = hidden.shape[1]
    H = skip_gain.shape[1]
    shard = conv_bias.shape[1]
    CW = shard * n_dp
    position = lax.axis_index("seq") * T + lax.iota(jnp.int32, T)
    mask = (position < lengths[0]).astype(F32)[:, None]
    gain = norm_gain[:, :, None]
    step_pad = jnp.pad(step_weight, ((0, 0), (0, 0), (0, LANES - H)))
    wm = jnp.concatenate([mix_weight, step_pad], axis=2) * gain
    wg = gate_weight * gain
    wo = out_weight * gated_gain[:, :, None]
    head = jnp.pad(jnp.stack([log_rate, step_bias, skip_gain], axis=1), ((0, 0), (0, 5), (0, LANES - H)))
    own = jnp.concatenate([conv_kernel, conv_bias[:, None, :]], axis=1)
    own = jnp.pad(own, ((0, 0), (0, 8 - own.shape[1]), (0, 0))).reshape(16, shard)
    conv = lax.dynamic_update_slice(jnp.zeros((16, CW), F32), own, (0, lax.axis_index("dp") * shard))
    return mask, conv, head, wm, wg, wo
CHUNK_N = 384


class Plan:
    def __init__(self, n_dp, n_seq, dims):
        T, D, DI, CW, H, PS, N, K = dims
        self.n_dp, self.n_seq = n_dp, n_seq
        self.n_z = n_seq // 2
        self.h = D // n_dp // 2
        self.out_jobs = 2 * (D // CHUNK_N)
        self.gate_jobs = DI // CHUNK_N
        self.mix_jobs = (CW + LANES) // CHUNK_N
        self.lead, self.bubbles = 2, 3
        self.per_layer = self.out_jobs + self.gate_jobs + self.mix_jobs
        self.early = self.out_jobs + self.gate_jobs
        self.slots = self.lead + self.per_layer + self.bubbles
        self.blocks = 2 * self.mix_jobs
        self.blocks_per_job = self.h // 8
        self.conv_jobs = -(-self.blocks // self.blocks_per_job)
        self.jobs = 2 * self.per_layer + self.conv_jobs
        self.total_slots = 2 * self.slots + self.conv_jobs
        self.wide = n_dp == 4 and self.n_z == 4 and self.h % 32 == 0
        self.rounds = self.n_z.bit_length() - 1
        self.offsets = (0, 1, 2, 4, 6, 8, 10, 12, 14, 15)
        self.o_ring = self.offsets[4] + 1
        self.f_ring = max(self.offsets) + 1
        self.s_ring = self.offsets[2] + 1
        self.kinds = 12 if self.wide else n_dp - 1 + self.rounds + 2
        self.sibling_kind = self.kinds - 1

    def job_of(self, slot):
        layer = slot // self.slots
        q = slot % self.slots - self.lead
        early = jnp.logical_and(q >= 0, q < self.early)
        late = q >= self.early + self.bubbles
        inside = jnp.logical_and(slot >= 0, slot < 2 * self.slots)
        valid = jnp.logical_and(inside, jnp.logical_or(early, late))
        job = layer * self.per_layer + q - jnp.where(early, 0, self.bubbles)
        conv = jnp.logical_and(slot >= 2 * self.slots, slot < self.total_slots)
        job = jnp.where(slot >= 2 * self.slots, 2 * self.per_layer + slot - 2 * self.slots, job)
        return jnp.logical_or(valid, conv), job


class Reducer:
    def __init__(self, place, plan, refs, outs):
        self.p, self.plan = place, plan
        self.S, self.O, self.R, self.rx, self.ry, self.r2x, self.r2y, self.z1, self.z2, self.G, self.F, self.send, self.recv, self.loc, self.fin = refs
        self.outs = outs

    def copy(self, job, kind, src, dst, dp, seq):
        return remote(src, dst, self.send.at[job, kind], self.recv.at[job, kind], dp, seq)

    def own(self, job, owner, start, count):
        ring = lax.rem(job, self.plan.o_ring)
        if not isinstance(start, int):
            start = pl.multiple_of(start, 8)
        return self.O.at[ring, owner, pl.ds(start, count)]

    def mine(self, job, start, count):
        return self.own(job, self.p.dp, start, count)

    def summed(self, job, start, count):
        ring = lax.rem(job, self.plan.f_ring)
        if not isinstance(start, int):
            start = pl.multiple_of(start, 8)
        return self.G.at[ring, pl.ds(start, count)]

    def to_sibling(self, job):
        ring = lax.rem(job, self.plan.s_ring)
        kind = self.plan.kinds - 2
        return self.copy(job, kind, self.S.at[ring], self.R.at[job], self.p.dp, self.p.sib)

    def load(self, job):
        ring = lax.rem(job, self.plan.s_ring)
        return pltpu.make_async_copy(self.R.at[job], self.S.at[ring], self.loc.at[ring])

    def z_peer(self, step):
        return lax.rem(self.p.z + step, self.plan.n_z) * 2 + self.p.core

    def xy(self, job, kind):
        p, half = self.p, self.plan.h // 2
        low, high = (0, half), (half, half)
        return {
            0: lambda: self.copy(job, 0, self.own(job, p.dpx, *low), self.rx.at[job, 0], p.dpx, p.seq),
            1: lambda: self.copy(job, 1, self.own(job, p.dpd, *low), self.rx.at[job, 1], p.dpx, p.seq),
            2: lambda: self.copy(job, 2, self.own(job, p.dpy, *high), self.ry.at[job, 0], p.dpy, p.seq),
            3: lambda: self.copy(job, 3, self.own(job, p.dpd, *high), self.ry.at[job, 1], p.dpy, p.seq),
            4: lambda: self.copy(job, 4, self.own(job, p.dpy, *low), self.r2y.at[job], p.dpy, p.seq),
            5: lambda: self.copy(job, 5, self.own(job, p.dpx, *high), self.r2x.at[job], p.dpx, p.seq),
        }[kind]()

    def keep(self):
        return self.p.parity * (self.plan.h // 2)

    def quarter(self):
        return self.keep() + (self.p.z // 2) * (self.plan.h // 4)

    def zed(self, job, kind):
        p, h = self.p, self.plan.h
        if kind == 6:
            return self.copy(job, 6, self.summed(job, (1 - p.parity) * (h // 2), h // 2), self.z1.at[job], p.dp, p.pair)
        if kind == 7:
            start = self.keep() + (1 - p.z // 2) * (h // 4)
            return self.copy(job, 7, self.summed(job, start, h // 4), self.z2.at[job], p.dp, self.z_peer(2))
        if kind == 8:
            part = self.whole(job, self.quarter(), h // 4)
            return self.copy(job, 8, part, part, p.dp, self.z_peer(2))
        part = self.whole(job, self.keep(), h // 2)
        return self.copy(job, 9, part, part, p.dp, p.pair)

    def whole(self, job, start, count):
        ring = lax.rem(job, self.plan.f_ring)
        return self.F.at[ring, pl.ds(pl.multiple_of(start, 8), count)]

    def direct(self, job, step):
        p, h = self.p, self.plan.h
        peer = lax.rem(p.dp + step, p.n_dp)
        return self.copy(job, step - 1, self.own(job, peer, 0, h), self.rx.at[job, step - 1], peer, p.seq)

    def butterfly(self, job, rnd):
        p, h = self.p, self.plan.h
        bit = (p.z // (1 << rnd)) % 2
        peer = (p.z + (1 << rnd) - 2 * bit * (1 << rnd)) * 2 + p.core
        kind = p.n_dp - 1 + rnd
        return self.copy(job, kind, self.summed(job, 0, h), self.z1.at[job, rnd], p.dp, peer)

    def add(self, dst, src):
        dst[...] = dst[...] + src[...]

    def stage(self, number, job):
        plan, p = self.plan, self.p
        h = plan.h
        half = h // 2
        if number == 0:
            self.to_sibling(job).start()
        elif number == 1:
            copy = self.to_sibling(job)
            copy.wait_recv()
            copy.wait_send()
            self.load(job).start()
        elif number == 2:
            self.load(job).wait()
            ring = lax.rem(job, plan.s_ring)
            o_ring = lax.rem(job, plan.o_ring)

            def add_owner(o):
                self.O[o_ring, o] = self.O[o_ring, o] + self.S[ring, o]

            tiles(plan.n_dp, add_owner)
            if plan.wide:
                for kind in range(4):
                    self.xy(job, kind).start()
            else:
                for step in range(1, plan.n_dp):
                    self.direct(job, step).start()
        elif number == 3:
            if plan.wide:
                self.xy(job, 0).wait_recv()
                self.xy(job, 1).wait_recv()
                self.add(self.own(job, p.dpy, 0, half), self.rx.at[job, 1])
                self.xy(job, 4).start()
                self.add(self.mine(job, 0, half), self.rx.at[job, 0])
                self.xy(job, 2).wait_recv()
                self.xy(job, 3).wait_recv()
                self.add(self.own(job, p.dpx, half, half), self.ry.at[job, 1])
                self.xy(job, 5).start()
                self.add(self.mine(job, half, half), self.ry.at[job, 0])
            else:
                for step in range(1, plan.n_dp):
                    self.direct(job, step).wait_recv()
                    self.add(self.mine(job, 0, h), self.rx.at[job, step - 1])
        elif number == 4:
            if plan.wide:
                self.xy(job, 4).wait_recv()
                self.summed(job, 0, half)[...] = self.mine(job, 0, half)[...] + self.r2y[job]
                self.xy(job, 5).wait_recv()
                self.summed(job, half, half)[...] = self.mine(job, half, half)[...] + self.r2x[job]
                self.zed(job, 6).start()
                for kind in range(6):
                    self.xy(job, kind).wait_send()
            else:
                self.summed(job, 0, h)[...] = self.mine(job, 0, h)[...]
                for step in range(1, plan.n_dp):
                    self.direct(job, step).wait_send()
                if plan.rounds > 0:
                    self.butterfly(job, 0).start()
        elif number == 5:
            if plan.wide:
                self.zed(job, 6).wait_recv()
                self.add(self.summed(job, self.keep(), half), self.z1.at[job])
                self.zed(job, 7).start()
            else:
                self.exchange(job, 0)
        elif number == 6:
            if plan.wide:
                self.zed(job, 7).wait_recv()
                total = self.summed(job, self.quarter(), h // 4)
                self.whole(job, self.quarter(), h // 4)[...] = total[...] + self.z2[job]
                self.zed(job, 8).start()
            else:
                self.exchange(job, 1)
        elif number == 7:
            if plan.wide:
                self.zed(job, 8).wait_recv()
                self.zed(job, 9).start()
        elif number == 8:
            if plan.wide:
                self.zed(job, 9).wait_recv()
            else:
                for rnd in range(2, max(plan.rounds, 3)):
                    self.exchange(job, rnd)
            self.final(job, "start")
        else:
            self.final(job, "wait")
            if plan.wide:
                for kind in range(6, 10):
                    self.zed(job, kind).wait_send()

    def exchange(self, job, rnd):
        if rnd >= self.plan.rounds:
            return
        copy = self.butterfly(job, rnd)
        copy.wait_recv()
        copy.wait_send()
        self.add(self.summed(job, 0, self.plan.h), self.z1.at[job, rnd])
        if rnd + 1 < self.plan.rounds:
            self.butterfly(job, rnd + 1).start()

    def final(self, job, what):
        plan, p = self.plan, self.p
        h = plan.h
        gm, gg, go, gc = self.outs
        layer = 1 - job // plan.per_layer
        q = lax.rem(job, plan.per_layer)
        normal = job < 2 * plan.per_layer
        src = self.whole(job, 0, h) if plan.wide else self.summed(job, 0, h)

        def put(core):
            def rows(start):
                return pl.ds(pl.multiple_of(start, 8), h)

            per_row = plan.out_jobs // 2
            return (
                (
                    jnp.logical_and(normal, q < plan.out_jobs),
                    lambda: go.at[layer, rows(core * 2 * h + (q // per_row) * h), lanes(lax.rem(q, per_row), CHUNK_N)],
                ),
                (
                    jnp.logical_and(normal, jnp.logical_and(q >= plan.out_jobs, q < plan.early)),
                    lambda: gg.at[layer, rows(core * h), lanes(q - plan.out_jobs, CHUNK_N)],
                ),
                (
                    jnp.logical_and(normal, q >= plan.early),
                    lambda: gm.at[layer, rows(core * h), lanes(q - plan.early, CHUNK_N)],
                ),
                (jnp.logical_not(normal), lambda: gc.at[job - 2 * plan.per_layer, core]),
            )

        def go_for(make, which):
            local = pltpu.make_async_copy(src, make(), self.fin.at[lax.rem(job, plan.f_ring)])
            away = self.copy(job, plan.sibling_kind, src, make(), p.dp, p.sib)
            if which == "start":
                local.start()
                away.start()
            else:
                local.wait()
                away.wait_send()

        for when, make in put(p.core):
            pl.when(when)(functools.partial(go_for, make, what))
        if what == "wait":
            for when, make in put(1 - p.core):

                def arrived(make=make):
                    self.copy(job, plan.sibling_kind, src, make(), p.dp, p.sib).wait_recv()

                pl.when(when)(arrived)

    def tick(self, t):
        for number in reversed(range(len(self.plan.offsets))):
            valid, job = self.plan.job_of(t - self.plan.offsets[number])

            @pl.when(valid)
            def _():
                self.stage(number, job)


def backward_kernel(n_dp, n_seq, dims, *refs):
    T, D, DI, CW, H, PS, N, K = dims
    plan = Plan(n_dp, n_seq, dims)
    (
        cot_ref, mask_ref, conv_ref, head_ref, x0_hbm, x1_hbm, gate_hbm, ext_hbm, step_hbm, mo_hbm, sin_hbm,
        sout_hbm, wm_hbm, wg_hbm, wo_hbm,
        hg_ref, gm, gg, go, gc, R,
        grad, x, gate, ext, step, mo, sin, sout, wrow, wcol, U, V, mixed, ldE, dtE, ldT, gmT, dgT, PG, raw, nT, gnT,
        NG, dS, dSin, maps, heads, convg, rows,
        S, O, rx, ry, r2x, r2y, z1, z2, G, F, edge_in,
        j_send, j_recv, s_loc, f_loc, l_sem, w_sem, v_sem, e_send, e_recv, r_send, r_recv,
    ) = refs
    place = Place(n_dp, n_seq)
    h = plan.h
    red = Reducer(
        place, plan, (S, O, R, rx, ry, r2x, r2y, z1, z2, G, F, j_send, j_recv, s_loc, f_loc), (gm, gg, go, gc)
    )
    CX = CW + LANES
    CHUNK = 256
    chunks = DI // CHUNK
    pairs = H // 2

    def loads(layer, is_second):
        items = ((mo_hbm, mo), (gate_hbm, gate), (step_hbm, step), (ext_hbm, ext), (sin_hbm, sin), (sout_hbm, sout))
        return [pltpu.make_async_copy(a.at[layer], b, l_sem.at[k]) for k, (a, b) in enumerate(items)]

    def load_x(layer_value, action):
        @pl.when(layer_value == 1)
        def _():
            getattr(pltpu.make_async_copy(x1_hbm, x, l_sem.at[6]), action)()

        @pl.when(layer_value == 0)
        def _():
            getattr(pltpu.make_async_copy(x0_hbm, x, l_sem.at[6]), action)()

    grad[...] = cot_ref[...] * mask_ref[...]
    PG[T : T + 8, :] = jnp.zeros((8, CW), F32)
    full_barrier(place)
    ti, tj = iota((T, T), 0), iota((T, T), 1)
    lane_low = iota((T, LANES), 1) < PS

    def produce(job, lhs, stride, offset_of, rhs):
        ring_s = lax.rem(job, plan.s_ring)
        ring_o = lax.rem(job, plan.o_ring)
        for target, buffer, ring in ((1 - place.core, S, ring_s), (place.core, O, ring_o)):
            left = jnp.concatenate(
                [lhs[pl.ds(pl.multiple_of(o * stride + offset_of(target), 8), h), :] for o in range(n_dp)], axis=0
            )
            result = mm(left, rhs)
            for o in range(n_dp):
                buffer[ring, o] = result[o * h : (o + 1) * h]

    def column_stream(hbm, count, layer, body):
        def fetch(i, slot):
            return pltpu.make_async_copy(hbm.at[layer, :, lanes(i, CHUNK_N)], wcol.at[slot], w_sem.at[slot])

        fetch(0, 0).start()

        def run(i):
            slot = lax.rem(i, 2)
            fetch(i, slot).wait()

            @pl.when(i + 1 < count)
            def _():
                fetch(i + 1, 1 - slot).start()

            body(i, slot)

        tiles(count, run)

    def layer_body(li, carry):
        layer = 1 - li
        base = li * plan.slots
        first_job = li * plan.per_layer
        head = head_ref[layer]
        items = loads(layer, li)
        for copy in items:
            copy.start()
        load_x(layer, "start")

        def fetch_row(i, slot):
            return pltpu.make_async_copy(wo_hbm.at[layer, lanes(i, 256)], wrow.at[slot], v_sem.at[slot])

        fetch_row(0, 0).start()
        items[0].wait()
        items[1].wait()

        def regate(i, squares):
            at = lanes(i, LANES)
            pre = gate[:, at]
            gated = mo[:, at] * (pre * sigmoid(pre))
            U[:, at] = gated
            return squares + gated * gated

        squares = lax.fori_loop(0, DI // LANES, regate, jnp.zeros((T, LANES), F32))
        inv_out = lax.rsqrt(jnp.sum(squares, axis=-1, keepdims=True) / DI + EPSILON)
        red.tick(base)

        def back_out(i, sums):
            slot = lax.rem(i, 2)
            fetch_row(i, slot).wait()

            @pl.when(i + 1 < DI // 256)
            def _():
                fetch_row(i + 1, 1 - slot).start()

            at = lanes(i, 256)
            q = mm(grad[...], wrow[slot], NT)
            V[:, at] = q
            gated = U[:, at]
            gnT[at, :] = (gated * inv_out).T
            product = q * gated
            return sums + product[:, 0:LANES] + product[:, LANES:256]

        sums = lax.fori_loop(0, DI // 256, back_out, jnp.zeros((T, LANES), F32))
        pull = jnp.sum(sums, axis=-1, keepdims=True) / DI * (inv_out * inv_out * inv_out)

        red.tick(base + 1)

        def out_job(i):
            per_row = plan.out_jobs // 2
            part = i // per_row
            rhs = grad[:, lanes(i % per_row, CHUNK_N)]
            produce(first_job + i, gnT, 4 * h, lambda target: target * 2 * h + part * h, rhs)
            red.tick(base + plan.lead + i)

        def degate(i):
            at = lanes(i, LANES)
            pre = gate[:, at]
            sig = sigmoid(pre)
            gated_grad = inv_out * V[:, at] - U[:, at] * pull
            gate[:, at] = gated_grad * mo[:, at] * (sig * (1.0 + pre * (1.0 - sig)))
            V[:, at] = gated_grad * (pre * sig)

        tiles(DI // LANES, degate)
        out_job(0)
        load_x(layer, "wait")
        inv_in = lax.rsqrt(jnp.mean(x[...] * x[...], axis=-1, keepdims=True) + EPSILON)
        for copy in items[2:]:
            copy.wait()
        raw_step = step[...]
        dt = softplus(raw_step + head[1:2, :])
        ld = exact(tri(T).astype(jnp.bfloat16), -jnp.exp(head[0:1, :]) * dt)
        ldT[...] = ld.T

        def expand(i):
            select = head_matrix(LANES, 256, PS, i * 256)
            ldE[:, lanes(i, 256)] = exact_right(ld, select)
            dtE[:, lanes(i, 256)] = exact_right(dt, select)

        tiles(DI // 256, expand)

        def conv_value(at):
            taps = conv_ref[pl.ds(pl.multiple_of(layer * 8, 8), 8), at]
            total = taps[K : K + 1, :]
            for k in range(K):
                total = total + taps[k : k + 1, :] * ext[8 - K + 1 + k : 8 - K + 1 + k + T, at]
            return taps, total

        def conv(i):
            at = lanes(i, 256)
            total = conv_value(at)[1]
            mixed[:, at] = total * sigmoid(total)

        tiles(CW // 256, conv)
        out_job(1)
        b_map = mixed[:, DI : DI + N]
        c_map = mixed[:, DI + N : DI + 2 * N]
        gmT[...] = jnp.where(ti <= tj, mm(b_map, c_map, NT), 0.0)
        dgT[...] = jnp.zeros((T, T), F32)
        maps[...] = jnp.zeros((T, 2 * N), F32)

        def back_state(i):
            at = lanes(i, 256)
            lifted = V[:, at] * jnp.exp(ldE[:, at])
            dSin[:, at] = mm(c_map, lifted, TN)
            maps[:, N:] = maps[:, N:] + mm(lifted, sin[:, at], NT)

        tiles(DI // 256, back_state)

        def relay_copy(chunk):
            at = lanes(chunk, CHUNK)
            return remote(
                dSin.at[:, at], dS.at[li, :, at], r_send.at[li, chunk], r_recv.at[li, chunk], place.dp, place.seq - 1
            )

        def relay(chunk):
            at = lanes(chunk, CHUNK)

            @pl.when(place.seq < n_seq - 1)
            def _():
                relay_copy(chunk).wait_recv()
                dSin[:, at] = dSin[:, at] + jnp.exp(ldE[T - 1 : T, at]) * dS[li, :, at]

            @pl.when(place.seq == n_seq - 1)
            def _():
                dS[li, :, at] = jnp.zeros((N, CHUNK), F32)

            @pl.when(place.seq > 0)
            def _():
                relay_copy(chunk).start()

        @pl.when(place.seq == n_seq - 1)
        def _():
            tiles(chunks, relay)

        out_job(2)
        nT[...] = (x[...] * inv_in).T
        NG[...] = jnp.zeros((T, D), F32)

        def back_gate(i, slot):
            NG[...] = NG[...] + mm(gate[:, lanes(i, CHUNK_N)], wcol[slot], NT)

        column_stream(wg_hbm, plan.gate_jobs, layer, back_gate)
        out_job(3)

        def gate_job(i):
            produce(first_job + plan.out_jobs + i, nT, 2 * h, lambda target: target * h, gate[:, lanes(i, CHUNK_N)])

        def diagonal(i):
            @pl.when(jnp.logical_and(place.seq < n_seq - 1, i == (n_seq - 1 - place.seq) * pairs // n_seq))
            def _():
                tiles(chunks, relay)

            at = lanes(i, LANES)
            scaled = mixed[:, at] * dtE[:, at]
            out_grad = V[:, at]
            l_tile = ldE[:, at]
            parts = []
            for side in range(2):
                column = l_tile[:, side * PS : side * PS + 1]
                row = ldT[pl.ds(2 * i + side, 1), :]
                decay = jnp.exp(jnp.minimum(row - column, 0.0))
                own_lanes = lane_low if side == 0 else jnp.logical_not(lane_low)
                pairing = mm(jnp.where(own_lanes, scaled, 0.0), out_grad, NT)
                dgT[...] = dgT[...] + decay * pairing
                parts.append(mm(gmT[...] * decay, out_grad))
            U[:, at] = jnp.where(lane_low, parts[0], parts[1])
            number = i // 2

            @pl.when(jnp.logical_and(i % 2 == 1, number < plan.gate_jobs))
            def _():
                gate_job(number)

            @pl.when(i % 2 == 1)
            def _():
                red.tick(base + plan.lead + plan.out_jobs + number)

        tiles(pairs, diagonal)
        masked = jnp.where(ti <= tj, dgT[...], 0.0)
        maps[:, 0:N] = mm(masked, c_map)
        maps[:, N:] = maps[:, N:] + mm(masked, b_map, TN)
        heads[...] = jnp.zeros((2, T, LANES), F32)
        rows[...] = jnp.zeros((8, LANES), F32)

        def back_heads(i):
            at = lanes(i, 256)
            select = head_matrix(LANES, 256, PS, i * 256)
            select32 = select.astype(F32)
            l_tile = ldE[:, at]
            heads_in = mixed[:, at]
            dt_tile = dtE[:, at]
            scaled = heads_in * dt_tile
            end_weight = jnp.exp(l_tile[T - 1 : T, :] - l_tile)
            skip = exact_right(head[2:3, :], select)
            out_grad = V[:, at]
            scaled_grad = U[:, at] + end_weight * mm(b_map, dS[li, :, at])
            maps[:, 0:N] = maps[:, 0:N] + mm(scaled * end_weight, dS[li, :, at], NT)
            decay = out_grad * (mo[:, at] - skip * heads_in) - scaled * scaled_grad
            heads[0] = heads[0] + mm(decay, select32, NT)
            heads[1] = heads[1] + mm(scaled_grad * heads_in, select32, NT)
            skip_sum = jnp.sum(out_grad * heads_in, axis=0, keepdims=True)
            end_sum = jnp.sum(dS[li, :, at] * sout[:, at], axis=0, keepdims=True)
            both = jnp.concatenate([skip_sum, end_sum, jnp.zeros((6, 256), F32)], axis=0)
            rows[...] = rows[...] + mm(both, select32, NT)
            U[:, at] = skip * out_grad + scaled_grad * dt_tile

        tiles(DI // 256, back_heads)
        red.tick(base + plan.lead + plan.early + plan.bubbles - 1)
        last_row = iota((T, LANES), 0) == T - 1
        decay_grad = heads[0] + jnp.where(last_row, rows[1:2, :], 0.0)
        rate_grad = exact(tri(T).astype(jnp.bfloat16), decay_grad, TN)
        step_grad = heads[1] - jnp.exp(head[0:1, :]) * rate_grad
        raw[:, CW:CX] = step_grad * sigmoid(raw_step + head[1:2, :])

        def back_conv(i):
            at = lanes(i, 256)
            taps, total = conv_value(at)
            sig = sigmoid(total)
            slope = sig * (1.0 + total * (1.0 - sig))

            def finish(upstream):
                pre = upstream * slope
                PG[0:T, at] = pre
                parts = [
                    jnp.sum(pre * ext[8 - K + 1 + k : 8 - K + 1 + k + T, at], axis=0, keepdims=True) for k in range(K)
                ]
                parts.append(jnp.sum(pre, axis=0, keepdims=True))
                parts.append(jnp.zeros((8 - K - 1, 256), F32))
                convg[li, :, at] = jnp.concatenate(parts, axis=0)

            @pl.when(i < DI // 256)
            def _():
                finish(U[:, lanes(jnp.minimum(i, DI // 256 - 1), 256)])

            @pl.when(i >= DI // 256)
            def _():
                finish(maps[...])

        tiles(CW // 256, back_conv)
        convg[li, :, CW:CX] = jnp.where(iota((8, LANES), 0) == 0, rows[0:1, :], 0.0)
        edge = remote(
            PG.at[pl.ds(0, 8)], edge_in.at[li], e_send.at[li], e_recv.at[li], place.dp, place.seq - 1
        )

        @pl.when(place.seq > 0)
        def _():
            edge.start()

        @pl.when(place.seq < n_seq - 1)
        def _():
            edge.wait_recv()
            PG[T : T + 8, :] = edge_in[li]

        def back_raw(i):
            at = lanes(i, 256)
            taps = conv_ref[pl.ds(pl.multiple_of(layer * 8, 8), 8), at]
            total = taps[K - 1 : K, :] * PG[0:T, at]
            for k in range(K - 1):
                total = total + taps[k : k + 1, :] * PG[K - 1 - k : K - 1 - k + T, at]
            raw[:, at] = total

        tiles(CW // 256, back_raw)

        def mix_job(i):
            produce(first_job + plan.early + i, nT, 2 * h, lambda target: target * h, raw[:, lanes(i, CHUNK_N)])
            red.tick(base + plan.lead + plan.early + plan.bubbles + i)

        def back_mix(i, slot):
            mix_job(i)
            NG[...] = NG[...] + mm(raw[:, lanes(i, CHUNK_N)], wcol[slot], NT)

        column_stream(wm_hbm, plan.mix_jobs, layer, back_mix)
        inner = jnp.sum(NG[...] * x[...], axis=-1, keepdims=True) / D
        grad[...] = grad[...] + inv_in * NG[...] - x[...] * (inner * (inv_in * inv_in * inv_in))

        @pl.when(place.seq > 0)
        def _():
            edge.wait_send()
            tiles(chunks, lambda c: relay_copy(c).wait_send())

        return carry

    lax.fori_loop(0, 2, layer_body, 0)
    hg_ref[...] = grad[...]
    base = 2 * plan.slots
    for e in range(plan.conv_jobs):
        job = 2 * plan.per_layer + e
        for block in range(plan.blocks_per_job):
            number = e * plan.blocks_per_job + block
            at = pl.ds(block * 8, 8)
            for o in range(n_dp):
                if number < plan.blocks:
                    li, c = divmod(number, plan.mix_jobs)
                    value = convg[li, :, c * CHUNK_N : (c + 1) * CHUNK_N]
                else:
                    value = jnp.zeros((8, CHUNK_N), F32)
                S[job % plan.s_ring, o, at] = value
                O[job % plan.o_ring, o, at] = value
        red.tick(base + e)
    tiles(max(plan.offsets), lambda i: red.tick(base + plan.conv_jobs + i))


def backward(cot, mask, conv, head, saved, n_dp, n_seq, dims):
    T, D, DI, CW, H, PS, N, K = dims
    plan = Plan(n_dp, n_seq, dims)
    any_spec = pl.BlockSpec(memory_space=pl.ANY)
    vmem = pl.BlockSpec(memory_space=pltpu.VMEM)
    CX = CW + LANES
    h, J = plan.h, plan.jobs
    sd = lambda *s: jax.ShapeDtypeStruct(s, F32)
    v = lambda *s: pltpu.VMEM(s, F32)
    dma = pltpu.SemaphoreType.DMA
    if plan.wide:
        received = [v(J, 2, h // 2, CHUNK_N), v(J, 2, h // 2, CHUNK_N), v(J, h // 2, CHUNK_N), v(J, h // 2, CHUNK_N),
                    v(J, h // 2, CHUNK_N), v(J, h // 4, CHUNK_N)]
    else:
        none = v(8, LANES)
        received = [v(J, n_dp - 1, h, CHUNK_N), none, none, none, v(J, max(plan.rounds, 1), h, CHUNK_N), none]
    return pl.pallas_call(
        functools.partial(backward_kernel, n_dp, n_seq, dims),
        out_shape=(
            sd(T, D), sd(2, 2 * h, CX), sd(2, 2 * h, DI), sd(2, 4 * h, D), sd(plan.conv_jobs, 2, h, CHUNK_N),
            sd(J, n_dp, h, CHUNK_N),
        ),
        in_specs=[vmem] * 4 + [any_spec] * 11,
        out_specs=(vmem,) + (any_spec,) * 5,
        scratch_shapes=[
            v(T, D), v(T, D), v(T, DI), v(T + 8, CW), v(T, LANES), v(T, DI), v(N, DI), v(N, DI),
            v(2, 256, D), v(2, D, CHUNK_N), v(T, DI), v(T, DI), v(T, CW), v(T, DI), v(T, DI), v(LANES, T), v(T, T),
            v(T, T), v(T + 8, CW), v(T, CX), v(D, T), v(DI, T), v(T, D), v(2, N, DI), v(N, DI), v(T, 2 * N),
            v(2, T, LANES), v(2, 8, CX), v(8, LANES),
            v(plan.s_ring, n_dp, h, CHUNK_N), v(plan.o_ring, n_dp, h, CHUNK_N), *received,
            v(plan.f_ring, h, CHUNK_N), v(plan.f_ring, h, CHUNK_N) if plan.wide else v(8, LANES), v(2, 8, CW),
            dma((J, plan.kinds + 1)), dma((J, plan.kinds + 1)), dma((plan.s_ring,)), dma((plan.f_ring,)), dma((7,)),
            dma((2,)), dma((2,)), dma((2,)), dma((2,)), dma((2, DI // 256)), dma((2, DI // 256)),
        ],
        compiler_params=pltpu.CompilerParams(
            collective_id=1, has_side_effects=True, vmem_limit_bytes=61 << 20
        ),
        name="backward",
    )(cot, mask, conv, head, *saved)


def on_device(hidden, cotangent, lengths, norm_gain, gate_weight, mix_weight, step_weight, conv_kernel, conv_bias,
              gated_gain, out_weight, skip_gain, log_rate, step_bias):
    n_dp, n_seq = lax.axis_size("dp"), lax.axis_size("seq")
    slots, T, D = hidden.shape
    DI, CW, H, K = gate_weight.shape[2], mix_weight.shape[2], skip_gain.shape[1], conv_kernel.shape[1]
    dims = (T, D, DI, CW, H, DI // H, (CW - DI) // 2, K)
    plan = Plan(n_dp, n_seq, dims)
    mask, conv, head, wm, wg, wo = prepare(
        hidden, lengths, norm_gain, gate_weight, mix_weight, step_weight, conv_kernel, conv_bias, gated_gain,
        out_weight, skip_gain, log_rate, step_bias, n_dp,
    )
    x = hidden[0]
    result, conv_full, *saved = forward(x, mask, conv, head, wm, wg, wo, n_dp, n_seq, dims)
    hidden_grad, gm, gg, go, gc, _ = backward(
        cotangent[0], mask, conv_full, head, (x, *saved), n_dp, n_seq, dims
    )
    gain = norm_gain[:, :, None]
    mix_grad = gm[:, :, :CW]
    step_grad = gm[:, :, CW : CW + H]
    norm_gain_grad = (
        jnp.sum(mix_grad * mix_weight, axis=2)
        + jnp.sum(gg * gate_weight, axis=2)
        + jnp.sum(step_grad * step_weight, axis=2)
    )
    gated_gain_grad = jnp.sum(go * out_weight, axis=2)
    blocks = gc[:, 0].reshape(-1, 8, CHUNK_N)[: plan.blocks]
    blocks = blocks.reshape(2, plan.mix_jobs, 8, CHUNK_N).transpose(0, 2, 1, 3).reshape(2, 8, CW + LANES)[::-1]
    shard = conv_bias.shape[1]
    own = lax.dynamic_slice(blocks, (0, 0, lax.axis_index("dp") * shard), (2, 8, shard))
    skip_grad = blocks[:, 0, CW : CW + H]
    return (
        result[None], hidden_grad[None], norm_gain_grad, gg * gain, mix_grad * gain, step_grad * gain, own[:, :K],
        own[:, K], gated_gain_grad, go * gated_gain[:, :, None], skip_grad,
    )


def solution(mesh):
    return jax.shard_map(
        on_device,
        mesh=mesh,
        in_specs=(
            P("dp", "seq", None), P("dp", "seq", None), P("dp"), P(None, "dp"), P(None, "dp", None),
            P(None, "dp", None), P(None, "dp", None), P(None, None, "dp"), P(None, "dp"), P(None, "dp"),
            P(None, "dp", None), P(), P(), P(),
        ),
        out_specs=(
            P("dp", "seq", None), P("dp", "seq", None), P(None, "dp"), P(None, "dp", None), P(None, "dp", None),
            P(None, "dp", None), P(None, None, "dp"), P(None, "dp"), P(None, "dp"), P(None, "dp", None), P(),
        ),
        check_vma=False,
    )
```

```python
import functools

import jax
import jax.numpy as jnp
from jax import lax
from jax.experimental import pallas as pl
from jax.experimental.pallas import tpu as pltpu
from jax.sharding import PartitionSpec as P

EPSILON = 1e-05
HIGH = lax.Precision.HIGH
MESH = pl.DeviceIdType.MESH
LANES = 128
F32 = jnp.float32


def mm(left, right, contract=((1,), (0,))):
    return lax.dot_general(left, right, (contract, ((), ())), precision=HIGH, preferred_element_type=F32)


NN = ((1,), (0,))
NT = ((1,), (1,))
TN = ((0,), (0,))


def split(value):
    high = value.astype(jnp.bfloat16)
    return high, (value - high.astype(F32)).astype(jnp.bfloat16)


def split3(value):
    first = value.astype(jnp.bfloat16)
    rest = value - first.astype(F32)
    second = rest.astype(jnp.bfloat16)
    third = (rest - second.astype(F32)).astype(jnp.bfloat16)
    return first, second, third


def exact(select, value, contract=((1,), (0,))):
    total = None
    for part in split3(value):
        term = lax.dot_general(select, part, (contract, ((), ())), preferred_element_type=F32)
        total = term if total is None else total + term
    return total


def exact_right(value, select, contract=((1,), (0,))):
    total = None
    for part in split3(value):
        term = lax.dot_general(part, select, (contract, ((), ())), preferred_element_type=F32)
        total = term if total is None else total + term
    return total


def iota(shape, axis):
    return lax.broadcasted_iota(jnp.int32, shape, axis)


def head_matrix(heads_padded, width, head_size, start=0):
    head = iota((heads_padded, width), 0)
    channel = iota((heads_padded, width), 1) + start
    inside = jnp.logical_and(channel >= head * head_size, channel < (head + 1) * head_size)
    return jnp.where(inside, 1.0, 0.0).astype(jnp.bfloat16)


def tri(size):
    return jnp.where(iota((size, size), 0) >= iota((size, size), 1), 1.0, 0.0)


def sigmoid(v):
    return jax.nn.sigmoid(v)


def softplus(v):
    return jnp.maximum(v, 0.0) + jnp.log1p(jnp.exp(-jnp.abs(v)))


def tiles(count, body):
    lax.fori_loop(0, count, lambda i, c: (body(i), c)[1], 0)


def lanes(i, width):
    return pl.ds(pl.multiple_of(i * width, width), width)


class Place:
    def __init__(self, dp_count, seq_count):
        self.n_dp, self.n_seq = dp_count, seq_count
        self.dp = lax.axis_index("dp")
        self.seq = lax.axis_index("seq")
        self.core = self.seq % 2
        self.z = self.seq // 2
        self.sib = self.z * 2 + (1 - self.core)
        self.parity = self.z % 2
        self.pair = (self.z + 1 - 2 * self.parity) * 2 + self.core
        y, x = self.dp // 2, self.dp % 2
        self.dpx = 2 * y + (1 - x)
        self.dpy = 2 * (1 - y) + x
        self.dpd = 2 * (1 - y) + (1 - x)


def remote(src, dst, send, recv, dp, seq):
    return pltpu.make_async_remote_copy(
        src_ref=src, dst_ref=dst, send_sem=send, recv_sem=recv, device_id=(dp, seq), device_id_type=MESH
    )


def entry_barrier(place):
    barrier = pltpu.get_barrier_semaphore()

    def greet(dp, seq):
        pl.semaphore_signal(barrier, inc=1, device_id=(dp, seq), device_id_type=MESH)

    for step in range(1, place.n_dp):
        greet((place.dp + step) % place.n_dp, place.seq)
    greet(place.dp, place.sib)
    greet(place.dp, place.pair)

    @pl.when(jnp.logical_and(place.core == 1, place.seq < place.n_seq - 1))
    def _():
        greet(place.dp, place.seq + 1)

    @pl.when(jnp.logical_and(place.core == 0, place.seq > 0))
    def _():
        greet(place.dp, place.seq - 1)

    outer = jnp.logical_or(place.seq == 0, place.seq == place.n_seq - 1)

    @pl.when(outer)
    def _():
        pl.semaphore_wait(barrier, place.n_dp + 1)

    @pl.when(jnp.logical_not(outer))
    def _():
        pl.semaphore_wait(barrier, place.n_dp + 2)


def full_barrier(place):
    barrier = pltpu.get_barrier_semaphore()
    for step in range(1, place.n_dp):
        peer = (place.dp + step) % place.n_dp
        pl.semaphore_signal(barrier, inc=1, device_id=(peer, place.seq), device_id_type=MESH)
    for step in range(1, place.n_seq):
        peer = (place.seq + step) % place.n_seq
        pl.semaphore_signal(barrier, inc=1, device_id=(place.dp, peer), device_id_type=MESH)
    pl.semaphore_wait(barrier, place.n_dp + place.n_seq - 2)


class Gather:
    def __init__(self, place, own, dest, stride, row_of, columns, half, sems, index):
        self.p, self.own, self.dest = place, own, dest
        self.stride, self.row_of, self.columns = stride, row_of, columns
        self.send, self.recv = sems
        self.index = index
        self.half = half
        self.third = half // 3
        self.wide = place.n_dp == 4 and half % 24 == 0 and place.n_seq % 4 == 0

    def at(self, owner, core, offset, count):
        start = owner * self.stride + self.row_of(core) + offset
        return self.dest.at[pl.ds(pl.multiple_of(start, 8), count), self.columns]

    def copy(self, kind, src, dst, dp, seq):
        return remote(src, dst, self.send.at[self.index, kind], self.recv.at[self.index, kind], dp, seq)

    def own_part(self, offset, count):
        start = self.row_of(self.p.core) + offset
        return self.own.at[pl.ds(pl.multiple_of(start, 8), count), self.columns]

    def get(self, kind):
        p, t = self.p, self.third
        if not self.wide:
            if kind < p.n_dp:
                peer = (p.dp + kind) % p.n_dp
                return self.copy(
                    kind, self.own_part(0, self.half), self.at(p.dp, p.core, 0, self.half), peer, p.seq
                )
            owner = (p.dp + 2 * p.n_dp - 1 - kind) % p.n_dp
            part = self.at(owner, p.core, 0, self.half)
            return self.copy(kind, part, part, p.dp, p.sib)
        first = p.parity * t
        only = 2 * t * p.parity
        miss = 2 * t * (1 - p.parity)
        if kind < 2:
            return self.copy(
                kind, self.own_part(first, 2 * t), self.at(p.dp, p.core, first, 2 * t),
                p.dpx if kind == 0 else p.dpy, p.seq,
            )
        owner, offset, count, dp, seq = {
            2: (p.dpx, first, t, p.dpy, p.seq),
            3: (p.dpy, first + t, t, p.dpx, p.seq),
            4: (p.dpx, only, t, p.dp, p.pair),
            5: (p.dpy, only, t, p.dp, p.pair),
            6: (p.dpd, only, t, p.dp, p.pair),
            7: (p.dpx, first, 2 * t, p.dp, p.sib),
            8: (p.dpy, first, 2 * t, p.dp, p.sib),
            9: (p.dpd, first, 2 * t, p.dp, p.sib),
            10: (p.dpx, miss, t, p.dp, p.sib),
            11: (p.dpy, miss, t, p.dp, p.sib),
            12: (p.dpd, miss, t, p.dp, p.sib),
        }[kind]
        part = self.at(owner, p.core, offset, count)
        return self.copy(kind, part, part, dp, seq)

    def stage(self, number):
        n = self.p.n_dp
        if not self.wide:
            if number == 0:
                for kind in range(1, n):
                    self.get(kind).start()
            elif number == 1:
                for kind in range(1, n):
                    self.get(kind).wait_recv()
                    self.get(n - 1 + kind).start()
            elif number == 4:
                for kind in range(n, 2 * n - 1):
                    self.get(kind).wait_recv()
            elif number == 5:
                for kind in range(1, 2 * n - 1):
                    self.get(kind).wait_send()
            return
        if number == 0:
            self.get(0).start()
            self.get(1).start()
        elif number == 1:
            self.get(0).wait_recv()
            for kind in (2, 4, 7):
                self.get(kind).start()
            self.get(1).wait_recv()
            for kind in (3, 5, 8):
                self.get(kind).start()
        elif number == 2:
            self.get(2).wait_recv()
            self.get(3).wait_recv()
            for kind in (6, 9):
                self.get(kind).start()
        elif number == 3:
            for kind in (4, 5, 6):
                self.get(kind).wait_recv()
                self.get(kind + 6).start()
        elif number == 4:
            for kind in range(7, 13):
                self.get(kind).wait_recv()
        else:
            for kind in range(13):
                self.get(kind).wait_send()


GATHER_OFFSETS = (0, 2, 4, 6, 7, 9)
PIECE = 384


def kinds_of(n_dp):
    return max(13, 2 * n_dp)


def forward_kernel(n_dp, n_seq, dims, *refs):
    (
        x_hbm, mask_ref, conv_ref, head_ref, wm_own, wg_own, wo_own,
        result_ref, conv_full, xs_out, gate_out, ext_out, step_out, mo_out, sin_out, sout_out, wm_out, wg_out, wo_out,
        WM, WG, WO, xs, gate, ext, step, mo, sin, sout, conv_in, mixed, diag, ldE, dtE, ldT, gm,
        g_send, g_recv, g_local, c_send, c_recv, e_send, e_recv, r_send, r_recv, o_sem,
    ) = refs
    T, D, DI, CW, H, PS, N, K = dims
    layers = 2
    place = Place(n_dp, n_seq)
    h = D // n_dp // 2
    mix_pieces, gate_pieces, across = (CW + LANES) // PIECE, DI // PIECE, D // PIECE
    out_pieces = 2 * across
    per_layer = mix_pieces + gate_pieces + out_pieces
    early = mix_pieces + gate_pieces
    done_at = GATHER_OFFSETS[4]

    def tick(t):
        for number in reversed(range(len(GATHER_OFFSETS))):
            job = t - GATHER_OFFSETS[number]
            layer, q = job // per_layer, job % per_layer
            inside = jnp.logical_and(job >= 0, job < 2 * per_layer)

            def run(own, dest, stride, row_of, column, number=number, job=job, layer=layer):
                piece = Gather(
                    place, own.at[layer], dest.at[layer], stride, row_of, lanes(column, PIECE), h, (g_send, g_recv), job
                )
                piece.stage(number)

            @pl.when(jnp.logical_and(inside, q < mix_pieces))
            def _():
                run(wm_own, WM, 2 * h, lambda core: core * h, q)

            @pl.when(jnp.logical_and(inside, jnp.logical_and(q >= mix_pieces, q < early)))
            def _():
                run(wg_own, WG, 2 * h, lambda core: core * h, q - mix_pieces)

            @pl.when(jnp.logical_and(inside, q >= early))
            def _():
                part = (q - early) // across
                run(wo_own, WO, 4 * h, lambda core: core * 2 * h + part * h, (q - early) % across)

    def own_copy(kind, layer):
        own, dest = ((wm_own, WM), (wg_own, WG), (wo_own, WO))[kind]
        rows = own.shape[1]
        start = pl.multiple_of(place.dp * rows, 8)
        return pltpu.make_async_copy(own.at[layer], dest.at[layer, pl.ds(start, rows)], g_local.at[layer * 3 + kind])

    first_in = pltpu.make_async_copy(x_hbm, xs.at[0], o_sem.at[0])
    first_in.start()
    ext[0, 0:8, :] = jnp.zeros((8, CW), F32)
    ext[1, 0:8, :] = jnp.zeros((8, CW), F32)
    entry_barrier(place)
    tick(0)
    for layer in range(layers):
        for kind in range(3):
            own_copy(kind, layer).start()

    def conv_copy(step_index):
        peer = (place.dp + step_index) % n_dp
        return remote(
            conv_ref, conv_in.at[place.dp], c_send.at[step_index - 1], c_recv.at[step_index - 1], peer, place.seq
        )

    for s in range(1, n_dp):
        conv_copy(s).start()
    conv_in[place.dp] = conv_ref[...]
    first_in.wait()
    tiles(done_at, lambda i: tick(i + 1))
    per_body = mix_pieces + 1 + (H // 2 + gate_pieces) // 3 + across
    ti, tj = iota((T, T), 0), iota((T, T), 1)
    lane_low = iota((T, LANES), 1) < PS
    CHUNK = 256
    chunks = DI // CHUNK

    def saved_copies(layer):
        saved = (
            (gate, gate_out), (ext, ext_out), (step, step_out), (mo, mo_out), (sin, sin_out), (sout, sout_out),
            (WM, wm_out), (WG, wg_out), (WO, wo_out),
        )
        return [
            functools.partial(lambda a, b, k: pltpu.make_async_copy(a.at[layer], b.at[layer], o_sem.at[layer * 9 + k + 1]), a, b, k)
            for k, (a, b) in enumerate(saved)
        ]

    def layer_body(layer, carry):
        x_all = xs[layer]
        inv = lax.rsqrt(jnp.mean(x_all * x_all, axis=-1, keepdims=True) + EPSILON)
        diag[:, 0:D] = x_all * inv
        head = head_ref[layer]
        base = done_at + 1 + layer * per_body
        own_copy(0, layer).wait()

        def project_mix(i):
            ext[layer, 8 : T + 8, lanes(i, PIECE)] = mm(diag[:, 0:D], WM[layer, :, lanes(i, PIECE)])
            tick(base + i)

        tiles(mix_pieces - 1, project_mix)
        last = (mix_pieces - 1) * PIECE
        value = mm(diag[:, 0:D], WM[layer, :, last : last + PIECE])
        ext[layer, 8 : T + 8, last:CW] = value[:, 0 : CW - last]
        raw = value[:, CW - last :]
        edge = remote(
            ext.at[layer, pl.ds(T, 8)], ext.at[layer, pl.ds(0, 8)], e_send.at[layer], e_recv.at[layer],
            place.dp, place.seq + 1,
        )

        @pl.when(place.seq < n_seq - 1)
        def _():
            edge.start()

        step[layer] = raw
        tick(base + mix_pieces - 1)
        saved_copies(layer)[6]().start()
        dt = softplus(raw + head[1:2, :])
        rate = -jnp.exp(head[0:1, :]) * dt
        ld = exact(tri(T).astype(jnp.bfloat16), rate)
        ldT[...] = ld.T

        def expand(i):
            select = head_matrix(LANES, 256, PS, i * 256)
            ldE[:, lanes(i, 256)] = exact_right(ld, select)
            dtE[:, lanes(i, 256)] = exact_right(dt, select)

        tiles(DI // 256, expand)

        @pl.when(layer == 0)
        def _():
            for s in range(1, n_dp):
                conv_copy(s).wait_recv()

            def sum_taps(i):
                at = lanes(i, 256)
                taps = conv_in[0, :, at]
                for s in range(1, n_dp):
                    taps = taps + conv_in[s, :, at]
                conv_full[:, at] = taps

            tiles(CW // 256, sum_taps)

        @pl.when(place.seq > 0)
        def _():
            edge.wait_recv()

        def conv(i):
            at = lanes(i, 256)
            taps = conv_full[pl.ds(pl.multiple_of(layer * 8, 8), 8), at]
            total = taps[K : K + 1, :]
            for k in range(K):
                total = total + taps[k : k + 1, :] * ext[layer, 8 - K + 1 + k : 8 - K + 1 + k + T, at]
            mixed[:, at] = total * sigmoid(total)

        tiles(CW // 256, conv)
        tick(base + mix_pieces)
        b_map = mixed[:, DI : DI + N]
        c_map = mixed[:, DI + N : DI + 2 * N]
        gm[...] = jnp.where(ti >= tj, mm(c_map, b_map, NT), 0.0)

        def local_state(i):
            at = lanes(i, 256)
            l_tile = ldE[:, at]
            weighted = mixed[:, at] * dtE[:, at] * jnp.exp(l_tile[T - 1 : T, :] - l_tile)
            sout[layer, :, at] = mm(b_map, weighted, TN)

        tiles(DI // 256, local_state)

        def relay_copy(chunk):
            at = lanes(chunk, CHUNK)
            return remote(
                sout.at[layer, :, at], sin.at[layer, :, at], r_send.at[layer, chunk], r_recv.at[layer, chunk],
                place.dp, place.seq + 1,
            )

        def relay(chunk):
            at = lanes(chunk, CHUNK)

            @pl.when(place.seq > 0)
            def _():
                relay_copy(chunk).wait_recv()
                total = jnp.exp(ldE[T - 1 : T, at])
                sout[layer, :, at] = sout[layer, :, at] + total * sin[layer, :, at]

            @pl.when(place.seq == 0)
            def _():
                sin[layer, :, at] = jnp.zeros((N, CHUNK), F32)

            @pl.when(place.seq < n_seq - 1)
            def _():
                relay_copy(chunk).start()

        pairs = H // 2

        items = pairs + gate_pieces
        relay_from = place.seq * (items - chunks) // (n_seq - 1)

        def diagonal(i):
            at = lanes(i, LANES)
            scaled = mixed[:, at] * dtE[:, at]
            l_tile = ldE[:, at]
            parts = []
            for side in range(2):
                column = l_tile[:, side * PS : side * PS + 1]
                row = ldT[pl.ds(2 * i + side, 1), :]
                weights = gm[...] * jnp.exp(jnp.minimum(column - row, 0.0))
                parts.append(mm(weights, scaled))
            diag[:, at] = jnp.where(lane_low, parts[0], parts[1])


        def gate_proj(i):
            at = lanes(i, PIECE)
            gate[layer, :, at] = mm(xs[layer] * inv, WG[layer, :, at])

        def work_item(i):
            @pl.when(i < pairs)
            def _():
                diagonal(i)

            @pl.when(i == pairs)
            def _():
                own_copy(1, layer).wait()

            @pl.when(i >= pairs)
            def _():
                gate_proj(i - pairs)

            @pl.when(jnp.logical_and(i >= relay_from, i < relay_from + chunks))
            def _():
                relay(i - relay_from)

            @pl.when(i % 3 == 2)
            def _():
                tick(base + mix_pieces + 1 + i // 3)

        tiles(items, work_item)
        saved_copies(layer)[7]().start()

        def skip_row(i):
            return exact_right(head[2:3, :], head_matrix(LANES, 256, PS, i * 256))

        def off(i):
            at = lanes(i, 256)
            lift = jnp.exp(ldE[:, at])
            out = diag[:, at] + lift * mm(c_map, sin[layer, :, at]) + skip_row(i) * mixed[:, at]
            mo[layer, :, at] = out

        tiles(DI // 256, off)

        def gating(i, squares):
            at = lanes(i, LANES)
            pre = gate[layer, :, at]
            gated = mo[layer, :, at] * (pre * sigmoid(pre))
            diag[:, at] = gated
            return squares + gated * gated

        squares = lax.fori_loop(0, DI // LANES, gating, jnp.zeros((T, LANES), F32))
        inv_out = lax.rsqrt(jnp.sum(squares, axis=-1, keepdims=True) / DI + EPSILON)
        own_copy(2, layer).wait()
        tiles(across, lambda i: tick(base + mix_pieces + 1 + items // 3 + i))

        def project_out(i):
            at = lanes(i, PIECE)
            branch = mm(diag[...] * inv_out, WO[layer, :, at])
            nxt = xs[layer, :, at] + branch
            xs[layer + 1, :, at] = nxt

        tiles(across, project_out)
        for number, copy in enumerate(saved_copies(layer)):
            if number < 6 or number == 8:
                copy().start()
        @pl.when(place.seq < n_seq - 1)
        def _():
            edge.wait_send()
            tiles(chunks, lambda c: relay_copy(c).wait_send())

        return carry

    lax.fori_loop(0, layers, layer_body, 0)
    done = done_at + 1 + layers * per_body
    left = layers * per_layer + GATHER_OFFSETS[5] - done
    if left > 0:
        tiles(left, lambda i: tick(done + i))
    result_ref[...] = xs[layers] * mask_ref[...]
    last = pltpu.make_async_copy(xs.at[1], xs_out, o_sem.at[0])
    last.start()
    for s in range(1, n_dp):
        conv_copy(s).wait_send()
    for layer in range(layers):
        for copy in saved_copies(layer):
            copy().wait()
    last.wait()


def forward(x, mask, conv, head, wm, wg, wo, n_dp, n_seq, dims):
    T, D, DI, CW, H, PS, N, K = dims
    any_spec = pl.BlockSpec(memory_space=pl.ANY)
    vmem = pl.BlockSpec(memory_space=pltpu.VMEM)
    CX = CW + LANES
    kinds = kinds_of(n_dp)
    PIECES = 2 * ((CW + LANES) // PIECE + DI // PIECE + 2 * (D // PIECE))
    sd = lambda *s: jax.ShapeDtypeStruct(s, F32)
    v = lambda *s: pltpu.VMEM(s, F32)
    dma = pltpu.SemaphoreType.DMA
    return pl.pallas_call(
        functools.partial(forward_kernel, n_dp, n_seq, dims),
        out_shape=(
            sd(T, D), sd(16, CW), sd(T, D), sd(2, T, DI), sd(2, T + 8, CW), sd(2, T, LANES), sd(2, T, DI), sd(2, N, DI),
            sd(2, N, DI), sd(2, D, CX), sd(2, D, DI), sd(2, DI, D),
        ),
        in_specs=[any_spec, vmem, vmem, vmem, any_spec, any_spec, any_spec],
        out_specs=(vmem, vmem) + (any_spec,) * 10,
        scratch_shapes=[
            v(2, D, CX), v(2, D, DI), v(2, DI, D), v(3, T, D), v(2, T, DI), v(2, T + 8, CW), v(2, T, LANES),
            v(2, T, DI), v(2, N, DI), v(2, N, DI), v(n_dp, 16, CW), v(T, CW), v(T, DI), v(T, DI), v(T, DI),
            v(LANES, T), v(T, T),
            dma((PIECES, kinds)), dma((PIECES, kinds)), dma((6,)), dma((n_dp - 1,)), dma((n_dp - 1,)), dma((2,)), dma((2,)),
            dma((2, DI // 256)), dma((2, DI // 256)), dma((19,)),
        ],
        compiler_params=pltpu.CompilerParams(
            collective_id=0, has_side_effects=True, vmem_limit_bytes=61 << 20
        ),
        name="forward",
    )(x, mask, conv, head, wm, wg, wo)


def prepare(hidden, lengths, norm_gain, gate_weight, mix_weight, step_weight, conv_kernel, conv_bias, gated_gain,
            out_weight, skip_gain, log_rate, step_bias, n_dp):
    T = hidden.shape[1]
    H = skip_gain.shape[1]
    shard = conv_bias.shape[1]
    CW = shard * n_dp
    position = lax.axis_index("seq") * T + lax.iota(jnp.int32, T)
    mask = (position < lengths[0]).astype(F32)[:, None]
    gain = norm_gain[:, :, None]
    step_pad = jnp.pad(step_weight, ((0, 0), (0, 0), (0, LANES - H)))
    wm = jnp.concatenate([mix_weight, step_pad], axis=2) * gain
    wg = gate_weight * gain
    wo = out_weight * gated_gain[:, :, None]
    head = jnp.pad(jnp.stack([log_rate, step_bias, skip_gain], axis=1), ((0, 0), (0, 5), (0, LANES - H)))
    own = jnp.concatenate([conv_kernel, conv_bias[:, None, :]], axis=1)
    own = jnp.pad(own, ((0, 0), (0, 8 - own.shape[1]), (0, 0))).reshape(16, shard)
    conv = lax.dynamic_update_slice(jnp.zeros((16, CW), F32), own, (0, lax.axis_index("dp") * shard))
    return mask, conv, head, wm, wg, wo
CHUNK_N = 384


class Plan:
    def __init__(self, n_dp, n_seq, dims):
        T, D, DI, CW, H, PS, N, K = dims
        self.n_dp, self.n_seq = n_dp, n_seq
        self.n_z = n_seq // 2
        self.h = D // n_dp // 2
        self.out_jobs = 2 * (D // CHUNK_N)
        self.gate_jobs = DI // CHUNK_N
        self.mix_jobs = (CW + LANES) // CHUNK_N
        self.lead, self.bubbles = 2, 3
        self.per_layer = self.out_jobs + self.gate_jobs + self.mix_jobs
        self.early = self.out_jobs + self.gate_jobs
        self.slots = self.lead + self.per_layer + self.bubbles
        self.blocks = 2 * self.mix_jobs
        self.blocks_per_job = self.h // 8
        self.conv_jobs = -(-self.blocks // self.blocks_per_job)
        self.jobs = 2 * self.per_layer + self.conv_jobs
        self.total_slots = 2 * self.slots + self.conv_jobs
        self.wide = n_dp == 4 and self.n_z == 4 and self.h % 32 == 0
        self.rounds = self.n_z.bit_length() - 1
        self.offsets = (0, 1, 2, 4, 6, 9, 12, 15, 18, 19)
        self.o_ring = self.offsets[4] + 1
        self.f_ring = max(self.offsets) + 1
        self.r_ring = (self.jobs + 1) // 2
        self.s_ring = self.offsets[2] + 1
        self.kinds = 12 if self.wide else n_dp - 1 + self.rounds + 2
        self.sibling_kind = self.kinds - 1

    def job_of(self, slot):
        layer = slot // self.slots
        q = slot % self.slots - self.lead
        early = jnp.logical_and(q >= 0, q < self.early)
        late = q >= self.early + self.bubbles
        inside = jnp.logical_and(slot >= 0, slot < 2 * self.slots)
        valid = jnp.logical_and(inside, jnp.logical_or(early, late))
        job = layer * self.per_layer + q - jnp.where(early, 0, self.bubbles)
        conv = jnp.logical_and(slot >= 2 * self.slots, slot < self.total_slots)
        job = jnp.where(slot >= 2 * self.slots, 2 * self.per_layer + slot - 2 * self.slots, job)
        return jnp.logical_or(valid, conv), job


class Reducer:
    def __init__(self, place, plan, refs, outs):
        self.p, self.plan = place, plan
        self.S, self.O, self.R, self.rx, self.ry, self.r2x, self.r2y, self.z1, self.z2, self.G, self.F, self.send, self.recv, self.loc, self.fin = refs
        self.outs = outs

    def copy(self, job, kind, src, dst, dp, seq):
        return remote(src, dst, self.send.at[job, kind], self.recv.at[job, kind], dp, seq)

    def own(self, job, owner, start, count):
        ring = lax.rem(job, self.plan.o_ring)
        if not isinstance(start, int):
            start = pl.multiple_of(start, 8)
        return self.O.at[ring, owner, pl.ds(start, count)]

    def mine(self, job, start, count):
        return self.own(job, self.p.dp, start, count)

    def summed(self, job, start, count):
        ring = lax.rem(job, self.plan.f_ring)
        if not isinstance(start, int):
            start = pl.multiple_of(start, 8)
        return self.G.at[ring, pl.ds(start, count)]

    def to_sibling(self, job):
        ring = lax.rem(job, self.plan.s_ring)
        kind = self.plan.kinds - 2
        return self.copy(job, kind, self.S.at[ring], self.R.at[job], self.p.dp, self.p.sib)

    def slot(self, job):
        return lax.rem(job, self.plan.r_ring)

    def load(self, job):
        ring = lax.rem(job, self.plan.s_ring)
        return pltpu.make_async_copy(self.R.at[job], self.S.at[ring], self.loc.at[ring])

    def z_peer(self, step):
        return lax.rem(self.p.z + step, self.plan.n_z) * 2 + self.p.core

    def xy(self, job, kind):
        p, half = self.p, self.plan.h // 2
        low, high = (0, half), (half, half)
        return {
            0: lambda: self.copy(job, 0, self.own(job, p.dpx, *low), self.rx.at[self.slot(job), 0], p.dpx, p.seq),
            1: lambda: self.copy(job, 1, self.own(job, p.dpd, *low), self.rx.at[self.slot(job), 1], p.dpx, p.seq),
            2: lambda: self.copy(job, 2, self.own(job, p.dpy, *high), self.ry.at[self.slot(job), 0], p.dpy, p.seq),
            3: lambda: self.copy(job, 3, self.own(job, p.dpd, *high), self.ry.at[self.slot(job), 1], p.dpy, p.seq),
            4: lambda: self.copy(job, 4, self.own(job, p.dpy, *low), self.r2y.at[self.slot(job)], p.dpy, p.seq),
            5: lambda: self.copy(job, 5, self.own(job, p.dpx, *high), self.r2x.at[self.slot(job)], p.dpx, p.seq),
        }[kind]()

    def keep(self):
        return self.p.parity * (self.plan.h // 2)

    def quarter(self):
        return self.keep() + (self.p.z // 2) * (self.plan.h // 4)

    def zed(self, job, kind):
        p, h = self.p, self.plan.h
        if kind == 6:
            return self.copy(job, 6, self.summed(job, (1 - p.parity) * (h // 2), h // 2), self.z1.at[self.slot(job)], p.dp, p.pair)
        if kind == 7:
            start = self.keep() + (1 - p.z // 2) * (h // 4)
            return self.copy(job, 7, self.summed(job, start, h // 4), self.z2.at[self.slot(job)], p.dp, self.z_peer(2))
        if kind == 8:
            part = self.whole(job, self.quarter(), h // 4)
            return self.copy(job, 8, part, part, p.dp, self.z_peer(2))
        part = self.whole(job, self.keep(), h // 2)
        return self.copy(job, 9, part, part, p.dp, p.pair)

    def whole(self, job, start, count):
        ring = lax.rem(job, self.plan.f_ring)
        return self.F.at[ring, pl.ds(pl.multiple_of(start, 8), count)]

    def direct(self, job, step):
        p, h = self.p, self.plan.h
        peer = lax.rem(p.dp + step, p.n_dp)
        return self.copy(job, step - 1, self.own(job, peer, 0, h), self.rx.at[self.slot(job), step - 1], peer, p.seq)

    def butterfly(self, job, rnd):
        p, h = self.p, self.plan.h
        bit = (p.z // (1 << rnd)) % 2
        peer = (p.z + (1 << rnd) - 2 * bit * (1 << rnd)) * 2 + p.core
        kind = p.n_dp - 1 + rnd
        return self.copy(job, kind, self.summed(job, 0, h), self.z1.at[self.slot(job), rnd], p.dp, peer)

    def add(self, dst, src):
        dst[...] = dst[...] + src[...]

    def stage(self, number, job):
        plan, p = self.plan, self.p
        h = plan.h
        half = h // 2
        if number == 0:
            self.to_sibling(job).start()
        elif number == 1:
            copy = self.to_sibling(job)
            copy.wait_recv()
            copy.wait_send()
            self.load(job).start()
        elif number == 2:
            self.load(job).wait()
            ring = lax.rem(job, plan.s_ring)
            o_ring = lax.rem(job, plan.o_ring)

            def add_owner(o):
                self.O[o_ring, o] = self.O[o_ring, o] + self.S[ring, o]

            tiles(plan.n_dp, add_owner)
            if plan.wide:
                for kind in range(4):
                    self.xy(job, kind).start()
            else:
                for step in range(1, plan.n_dp):
                    self.direct(job, step).start()
        elif number == 3:
            if plan.wide:
                for kind in range(4):
                    self.xy(job, kind).wait_recv()
                self.add(self.own(job, p.dpy, 0, half), self.rx.at[self.slot(job), 1])
                self.add(self.own(job, p.dpx, half, half), self.ry.at[self.slot(job), 1])
                self.add(self.mine(job, 0, half), self.rx.at[self.slot(job), 0])
                self.add(self.mine(job, half, half), self.ry.at[self.slot(job), 0])
                self.xy(job, 4).start()
                self.xy(job, 5).start()
            else:
                for step in range(1, plan.n_dp):
                    self.direct(job, step).wait_recv()
                    self.add(self.mine(job, 0, h), self.rx.at[self.slot(job), step - 1])
        elif number == 4:
            if plan.wide:
                self.xy(job, 4).wait_recv()
                self.summed(job, 0, half)[...] = self.mine(job, 0, half)[...] + self.r2y[self.slot(job)]
                self.xy(job, 5).wait_recv()
                self.summed(job, half, half)[...] = self.mine(job, half, half)[...] + self.r2x[self.slot(job)]
                self.zed(job, 6).start()
                for kind in range(6):
                    self.xy(job, kind).wait_send()
            else:
                self.summed(job, 0, h)[...] = self.mine(job, 0, h)[...]
                for step in range(1, plan.n_dp):
                    self.direct(job, step).wait_send()
                if plan.rounds > 0:
                    self.butterfly(job, 0).start()
        elif number == 5:
            if plan.wide:
                self.zed(job, 6).wait_recv()
                self.add(self.summed(job, self.keep(), half), self.z1.at[self.slot(job)])
                self.zed(job, 7).start()
            else:
                self.exchange(job, 0)
        elif number == 6:
            if plan.wide:
                self.zed(job, 7).wait_recv()
                total = self.summed(job, self.quarter(), h // 4)
                self.whole(job, self.quarter(), h // 4)[...] = total[...] + self.z2[self.slot(job)]
                self.zed(job, 8).start()
            else:
                self.exchange(job, 1)
        elif number == 7:
            if plan.wide:
                self.zed(job, 8).wait_recv()
                self.zed(job, 9).start()
        elif number == 8:
            if plan.wide:
                self.zed(job, 9).wait_recv()
            else:
                for rnd in range(2, max(plan.rounds, 3)):
                    self.exchange(job, rnd)
            self.final(job, "start")
        else:
            self.final(job, "wait")
            if plan.wide:
                for kind in range(6, 10):
                    self.zed(job, kind).wait_send()

    def exchange(self, job, rnd):
        if rnd >= self.plan.rounds:
            return
        copy = self.butterfly(job, rnd)
        copy.wait_recv()
        copy.wait_send()
        self.add(self.summed(job, 0, self.plan.h), self.z1.at[self.slot(job), rnd])
        if rnd + 1 < self.plan.rounds:
            self.butterfly(job, rnd + 1).start()

    def final(self, job, what):
        plan, p = self.plan, self.p
        h = plan.h
        gm, gg, go, gc = self.outs
        layer = 1 - job // plan.per_layer
        q = lax.rem(job, plan.per_layer)
        normal = job < 2 * plan.per_layer
        src = self.whole(job, 0, h) if plan.wide else self.summed(job, 0, h)

        def put(core):
            def rows(start):
                return pl.ds(pl.multiple_of(start, 8), h)

            per_row = plan.out_jobs // 2
            return (
                (
                    jnp.logical_and(normal, q < plan.out_jobs),
                    lambda: go.at[layer, rows(core * 2 * h + (q // per_row) * h), lanes(lax.rem(q, per_row), CHUNK_N)],
                ),
                (
                    jnp.logical_and(normal, jnp.logical_and(q >= plan.out_jobs, q < plan.early)),
                    lambda: gg.at[layer, rows(core * h), lanes(q - plan.out_jobs, CHUNK_N)],
                ),
                (
                    jnp.logical_and(normal, q >= plan.early),
                    lambda: gm.at[layer, rows(core * h), lanes(q - plan.early, CHUNK_N)],
                ),
                (jnp.logical_not(normal), lambda: gc.at[job - 2 * plan.per_layer, core]),
            )

        def go_for(make, which):
            local = pltpu.make_async_copy(src, make(), self.fin.at[lax.rem(job, plan.f_ring)])
            away = self.copy(job, plan.sibling_kind, src, make(), p.dp, p.sib)
            if which == "start":
                local.start()
                away.start()
            else:
                local.wait()
                away.wait_send()

        for when, make in put(p.core):
            pl.when(when)(functools.partial(go_for, make, what))
        if what == "wait":
            for when, make in put(1 - p.core):

                def arrived(make=make):
                    self.copy(job, plan.sibling_kind, src, make(), p.dp, p.sib).wait_recv()

                pl.when(when)(arrived)

    def tick(self, t):
        for number in reversed(range(len(self.plan.offsets))):
            valid, job = self.plan.job_of(t - self.plan.offsets[number])

            @pl.when(valid)
            def _():
                self.stage(number, job)


def backward_kernel(n_dp, n_seq, dims, *refs):
    T, D, DI, CW, H, PS, N, K = dims
    plan = Plan(n_dp, n_seq, dims)
    (
        cot_ref, mask_ref, conv_ref, head_ref, x0_hbm, x1_hbm, gate_hbm, ext_hbm, step_hbm, mo_hbm, sin_hbm,
        sout_hbm, wm_hbm, wg_hbm, wo_hbm,
        hg_ref, gm, gg, go, gc, R,
        grad, x, gate, ext, step, mo, sin, sout, wrow, wcol, U, V, mixed, ldE, dtE, ldT, gmT, dgT, PG, raw, nT, gnT,
        NG, dS, dSin, maps, heads, convg, rows,
        S, O, rx, ry, r2x, r2y, z1, z2, G, F, edge_in,
        j_send, j_recv, s_loc, f_loc, l_sem, w_sem, v_sem, e_send, e_recv, r_send, r_recv,
    ) = refs
    place = Place(n_dp, n_seq)
    h = plan.h
    red = Reducer(
        place, plan, (S, O, R, rx, ry, r2x, r2y, z1, z2, G, F, j_send, j_recv, s_loc, f_loc), (gm, gg, go, gc)
    )
    CX = CW + LANES
    CHUNK = 256
    chunks = DI // CHUNK
    pairs = H // 2

    def load_of(layer, k):
        source, target = (
            (mo_hbm, mo), (gate_hbm, gate), (step_hbm, step), (ext_hbm, ext), (sin_hbm, sin), (sout_hbm, sout),
            (wo_hbm, wrow),
        )[k]
        return pltpu.make_async_copy(source.at[layer], target, l_sem.at[k])

    class Load:
        def __init__(self, layer, k):
            self.layer, self.k = layer, k

        def wait(self):
            load_of(self.layer, self.k).wait()

    for k in range(7):
        load_of(1, k).start()

    def load_x(layer_value, action):
        @pl.when(layer_value == 1)
        def _():
            getattr(pltpu.make_async_copy(x1_hbm, x, l_sem.at[7]), action)()

        @pl.when(layer_value == 0)
        def _():
            getattr(pltpu.make_async_copy(x0_hbm, x, l_sem.at[7]), action)()

    grad[...] = cot_ref[...] * mask_ref[...]
    PG[T : T + 8, :] = jnp.zeros((8, CW), F32)
    full_barrier(place)
    ti, tj = iota((T, T), 0), iota((T, T), 1)
    lane_low = iota((T, LANES), 1) < PS

    def produce(job, lhs, stride, offset_of, rhs):
        ring_s = lax.rem(job, plan.s_ring)
        ring_o = lax.rem(job, plan.o_ring)
        for target, buffer, ring in ((1 - place.core, S, ring_s), (place.core, O, ring_o)):
            left = jnp.concatenate(
                [lhs[pl.ds(pl.multiple_of(o * stride + offset_of(target), 8), h), :] for o in range(n_dp)], axis=0
            )
            result = mm(left, rhs)
            for o in range(n_dp):
                buffer[ring, o] = result[o * h : (o + 1) * h]

    def column_stream(hbm, count, layer, body):
        def fetch(i, slot):
            return pltpu.make_async_copy(hbm.at[layer, :, lanes(i, CHUNK_N)], wcol.at[slot], w_sem.at[slot])

        fetch(0, 0).start()
        fetch(1, 1).start()

        def run(i):
            slot = lax.rem(i, 3)
            fetch(i, slot).wait()

            @pl.when(i + 2 < count)
            def _():
                fetch(i + 2, lax.rem(i + 2, 3)).start()

            body(i, slot)

        return run

    def layer_body(li, carry):
        layer = 1 - li
        base = li * plan.slots
        first_job = li * plan.per_layer
        head = head_ref[layer]
        loads = [Load(layer, k) for k in range(7)]
        load_x(layer, "start")

        loads[0].wait()
        loads[1].wait()

        def regate(i, squares):
            at = lanes(i, LANES)
            pre = gate[:, at]
            gated = mo[:, at] * (pre * sigmoid(pre))
            U[:, at] = gated
            return squares + gated * gated

        squares = lax.fori_loop(0, DI // LANES, regate, jnp.zeros((T, LANES), F32))
        inv_out = lax.rsqrt(jnp.sum(squares, axis=-1, keepdims=True) / DI + EPSILON)
        red.tick(base)
        loads[6].wait()

        def back_out(i, sums):
            at = lanes(i, 256)
            q = mm(grad[...], wrow[at, :], NT)
            V[:, at] = q
            gated = U[:, at]
            gnT[at, :] = (gated * inv_out).T
            product = q * gated
            return sums + product[:, 0:LANES] + product[:, LANES:256]

        sums = lax.fori_loop(0, DI // 256, back_out, jnp.zeros((T, LANES), F32))
        pull = jnp.sum(sums, axis=-1, keepdims=True) / DI * (inv_out * inv_out * inv_out)

        red.tick(base + 1)

        @pl.when(li == 0)
        def _():
            load_of(0, 6).start()

        def out_piece(i):
            per_row = plan.out_jobs // 2
            part = i // per_row
            rhs = grad[:, lanes(i % per_row, CHUNK_N)]
            produce(first_job + i, gnT, 4 * h, lambda target: target * 2 * h + part * h, rhs)

        def out_job(i):
            out_piece(i)
            red.tick(base + plan.lead + i)

        def degate(i):
            at = lanes(i, LANES)
            pre = gate[:, at]
            sig = sigmoid(pre)
            gated_grad = inv_out * V[:, at] - U[:, at] * pull
            gate[:, at] = gated_grad * mo[:, at] * (sig * (1.0 + pre * (1.0 - sig)))
            V[:, at] = gated_grad * (pre * sig)

        tiles(DI // LANES, degate)
        out_job(0)
        load_x(layer, "wait")
        inv_in = lax.rsqrt(jnp.mean(x[...] * x[...], axis=-1, keepdims=True) + EPSILON)
        for copy in loads[2:6]:
            copy.wait()
        raw_step = step[...]
        dt = softplus(raw_step + head[1:2, :])
        ld = exact(tri(T).astype(jnp.bfloat16), -jnp.exp(head[0:1, :]) * dt)
        ldT[...] = ld.T

        def expand(i):
            select = head_matrix(LANES, 256, PS, i * 256)
            ldE[:, lanes(i, 256)] = exact_right(ld, select)
            dtE[:, lanes(i, 256)] = exact_right(dt, select)

        tiles(DI // 256, expand)

        def conv_value(at):
            taps = conv_ref[pl.ds(pl.multiple_of(layer * 8, 8), 8), at]
            total = taps[K : K + 1, :]
            for k in range(K):
                total = total + taps[k : k + 1, :] * ext[8 - K + 1 + k : 8 - K + 1 + k + T, at]
            return taps, total

        def conv(i):
            at = lanes(i, 256)
            total = conv_value(at)[1]
            mixed[:, at] = total * sigmoid(total)

        tiles(CW // 256, conv)
        out_job(1)
        b_map = mixed[:, DI : DI + N]
        c_map = mixed[:, DI + N : DI + 2 * N]
        gmT[...] = jnp.where(ti <= tj, mm(b_map, c_map, NT), 0.0)
        dgT[...] = jnp.zeros((T, T), F32)
        maps[...] = jnp.zeros((T, 2 * N), F32)

        def back_state(i):
            at = lanes(i, 256)
            lifted = V[:, at] * jnp.exp(ldE[:, at])
            dSin[:, at] = mm(c_map, lifted, TN)
            maps[:, N:] = maps[:, N:] + mm(lifted, sin[:, at], NT)

        tiles(DI // 256, back_state)

        def relay_copy(chunk):
            at = lanes(chunk, CHUNK)
            return remote(
                dSin.at[:, at], dS.at[li, :, at], r_send.at[li, chunk], r_recv.at[li, chunk], place.dp, place.seq - 1
            )

        def relay(chunk):
            at = lanes(chunk, CHUNK)

            @pl.when(place.seq < n_seq - 1)
            def _():
                relay_copy(chunk).wait_recv()
                dSin[:, at] = dSin[:, at] + jnp.exp(ldE[T - 1 : T, at]) * dS[li, :, at]

            @pl.when(place.seq == n_seq - 1)
            def _():
                dS[li, :, at] = jnp.zeros((N, CHUNK), F32)

            @pl.when(place.seq > 0)
            def _():
                relay_copy(chunk).start()

        items = pairs + plan.gate_jobs
        relay_from = (n_seq - 1 - place.seq) * (items - chunks) // (n_seq - 1)
        nT[...] = (x[...] * inv_in).T
        NG[...] = jnp.zeros((T, D), F32)

        def back_gate(i, slot):
            NG[...] = NG[...] + mm(gate[:, lanes(i, CHUNK_N)], wcol[slot], NT)

        gate_stream = column_stream(wg_hbm, plan.gate_jobs, layer, back_gate)

        def gate_job(i):
            produce(first_job + plan.out_jobs + i, nT, 2 * h, lambda target: target * h, gate[:, lanes(i, CHUNK_N)])

        def diagonal(i):
            at = lanes(i, LANES)
            scaled = mixed[:, at] * dtE[:, at]
            out_grad = V[:, at]
            l_tile = ldE[:, at]
            parts = []
            for side in range(2):
                column = l_tile[:, side * PS : side * PS + 1]
                row = ldT[pl.ds(2 * i + side, 1), :]
                decay = jnp.exp(jnp.minimum(row - column, 0.0))
                own_lanes = lane_low if side == 0 else jnp.logical_not(lane_low)
                pairing = mm(jnp.where(own_lanes, scaled, 0.0), out_grad, NT)
                dgT[...] = dgT[...] + decay * pairing
                parts.append(mm(gmT[...] * decay, out_grad))
            U[:, at] = jnp.where(lane_low, parts[0], parts[1])

        def work_item(i):
            @pl.when(i < pairs)
            def _():
                diagonal(i)

            @pl.when(i >= pairs)
            def _():
                gate_stream(i - pairs)

            @pl.when(jnp.logical_and(i >= relay_from, i < relay_from + chunks))
            def _():
                relay(i - relay_from)

            number = i // 2 + 2

            @pl.when(jnp.logical_and(i % 2 == 1, number < plan.out_jobs))
            def _():
                out_piece(number)

            @pl.when(jnp.logical_and(i % 2 == 1, jnp.logical_and(number >= plan.out_jobs, number < plan.early)))
            def _():
                gate_job(number - plan.out_jobs)

            @pl.when(i % 2 == 1)
            def _():
                red.tick(base + plan.lead + number)

        tiles(items, work_item)
        mix_stream = column_stream(wm_hbm, plan.mix_jobs, layer, lambda i, slot: back_mix(i, slot))
        masked = jnp.where(ti <= tj, dgT[...], 0.0)
        maps[:, 0:N] = mm(masked, c_map)
        maps[:, N:] = maps[:, N:] + mm(masked, b_map, TN)
        heads[...] = jnp.zeros((2, T, LANES), F32)
        rows[...] = jnp.zeros((8, LANES), F32)

        def back_heads(i):
            at = lanes(i, 256)
            select = head_matrix(LANES, 256, PS, i * 256)
            select32 = select.astype(F32)
            l_tile = ldE[:, at]
            heads_in = mixed[:, at]
            dt_tile = dtE[:, at]
            scaled = heads_in * dt_tile
            end_weight = jnp.exp(l_tile[T - 1 : T, :] - l_tile)
            skip = exact_right(head[2:3, :], select)
            out_grad = V[:, at]
            scaled_grad = U[:, at] + end_weight * mm(b_map, dS[li, :, at])
            maps[:, 0:N] = maps[:, 0:N] + mm(scaled * end_weight, dS[li, :, at], NT)
            decay = out_grad * (mo[:, at] - skip * heads_in) - scaled * scaled_grad
            heads[0] = heads[0] + mm(decay, select32, NT)
            heads[1] = heads[1] + mm(scaled_grad * heads_in, select32, NT)
            skip_sum = jnp.sum(out_grad * heads_in, axis=0, keepdims=True)
            end_sum = jnp.sum(dS[li, :, at] * sout[:, at], axis=0, keepdims=True)
            both = jnp.concatenate([skip_sum, end_sum, jnp.zeros((6, 256), F32)], axis=0)
            rows[...] = rows[...] + mm(both, select32, NT)
            U[:, at] = skip * out_grad + scaled_grad * dt_tile

        tiles(DI // 256, back_heads)
        red.tick(base + plan.lead + plan.early + plan.bubbles - 1)
        last_row = iota((T, LANES), 0) == T - 1
        decay_grad = heads[0] + jnp.where(last_row, rows[1:2, :], 0.0)
        rate_grad = exact(tri(T).astype(jnp.bfloat16), decay_grad, TN)
        step_grad = heads[1] - jnp.exp(head[0:1, :]) * rate_grad
        raw[:, CW:CX] = step_grad * sigmoid(raw_step + head[1:2, :])

        def back_conv(i):
            at = lanes(i, 256)
            taps, total = conv_value(at)
            sig = sigmoid(total)
            slope = sig * (1.0 + total * (1.0 - sig))

            def finish(upstream):
                pre = upstream * slope
                PG[0:T, at] = pre
                parts = [
                    jnp.sum(pre * ext[8 - K + 1 + k : 8 - K + 1 + k + T, at], axis=0, keepdims=True) for k in range(K)
                ]
                parts.append(jnp.sum(pre, axis=0, keepdims=True))
                parts.append(jnp.zeros((8 - K - 1, 256), F32))
                convg[li, :, at] = jnp.concatenate(parts, axis=0)

            @pl.when(i < DI // 256)
            def _():
                finish(U[:, lanes(jnp.minimum(i, DI // 256 - 1), 256)])

            @pl.when(i >= DI // 256)
            def _():
                finish(maps[...])

        tiles(CW // 256, back_conv)
        convg[li, :, CW:CX] = jnp.where(iota((8, LANES), 0) == 0, rows[0:1, :], 0.0)

        @pl.when(li == 0)
        def _():
            for k in range(6):
                load_of(0, k).start()

        edge = remote(
            PG.at[pl.ds(0, 8)], edge_in.at[li], e_send.at[li], e_recv.at[li], place.dp, place.seq - 1
        )

        @pl.when(place.seq > 0)
        def _():
            edge.start()

        @pl.when(place.seq < n_seq - 1)
        def _():
            edge.wait_recv()
            PG[T : T + 8, :] = edge_in[li]

        def back_raw(i):
            at = lanes(i, 256)
            taps = conv_ref[pl.ds(pl.multiple_of(layer * 8, 8), 8), at]
            total = taps[K - 1 : K, :] * PG[0:T, at]
            for k in range(K - 1):
                total = total + taps[k : k + 1, :] * PG[K - 1 - k : K - 1 - k + T, at]
            raw[:, at] = total

        tiles(CW // 256, back_raw)

        def mix_job(i):
            produce(first_job + plan.early + i, nT, 2 * h, lambda target: target * h, raw[:, lanes(i, CHUNK_N)])
            red.tick(base + plan.lead + plan.early + plan.bubbles + i)

        def back_mix(i, slot):
            mix_job(i)
            NG[...] = NG[...] + mm(raw[:, lanes(i, CHUNK_N)], wcol[slot], NT)

        tiles(plan.mix_jobs, mix_stream)
        inner = jnp.sum(NG[...] * x[...], axis=-1, keepdims=True) / D
        grad[...] = grad[...] + inv_in * NG[...] - x[...] * (inner * (inv_in * inv_in * inv_in))

        @pl.when(place.seq > 0)
        def _():
            edge.wait_send()
            tiles(chunks, lambda c: relay_copy(c).wait_send())

        return carry

    lax.fori_loop(0, 2, layer_body, 0)
    hg_ref[...] = grad[...]
    base = 2 * plan.slots
    for e in range(plan.conv_jobs):
        job = 2 * plan.per_layer + e
        for block in range(plan.blocks_per_job):
            number = e * plan.blocks_per_job + block
            at = pl.ds(block * 8, 8)
            for o in range(n_dp):
                if number < plan.blocks:
                    li, c = divmod(number, plan.mix_jobs)
                    value = convg[li, :, c * CHUNK_N : (c + 1) * CHUNK_N]
                else:
                    value = jnp.zeros((8, CHUNK_N), F32)
                S[job % plan.s_ring, o, at] = value
                O[job % plan.o_ring, o, at] = value
        red.tick(base + e)
    tiles(max(plan.offsets), lambda i: red.tick(base + plan.conv_jobs + i))


def backward(cot, mask, conv, head, saved, n_dp, n_seq, dims):
    T, D, DI, CW, H, PS, N, K = dims
    plan = Plan(n_dp, n_seq, dims)
    any_spec = pl.BlockSpec(memory_space=pl.ANY)
    vmem = pl.BlockSpec(memory_space=pltpu.VMEM)
    CX = CW + LANES
    h, J, ring = plan.h, plan.jobs, plan.r_ring
    sd = lambda *s: jax.ShapeDtypeStruct(s, F32)
    v = lambda *s: pltpu.VMEM(s, F32)
    dma = pltpu.SemaphoreType.DMA
    if plan.wide:
        received = [v(ring, 2, h // 2, CHUNK_N), v(ring, 2, h // 2, CHUNK_N), v(ring, h // 2, CHUNK_N),
                    v(ring, h // 2, CHUNK_N), v(ring, h // 2, CHUNK_N), v(ring, h // 4, CHUNK_N)]
    else:
        none = v(8, LANES)
        received = [v(ring, n_dp - 1, h, CHUNK_N), none, none, none, v(ring, max(plan.rounds, 1), h, CHUNK_N), none]
    return pl.pallas_call(
        functools.partial(backward_kernel, n_dp, n_seq, dims),
        out_shape=(
            sd(T, D), sd(2, 2 * h, CX), sd(2, 2 * h, DI), sd(2, 4 * h, D), sd(plan.conv_jobs, 2, h, CHUNK_N),
            sd(J, n_dp, h, CHUNK_N),
        ),
        in_specs=[vmem] * 4 + [any_spec] * 11,
        out_specs=(vmem,) + (any_spec,) * 5,
        scratch_shapes=[
            v(T, D), v(T, D), v(T, DI), v(T + 8, CW), v(T, LANES), v(T, DI), v(N, DI), v(N, DI),
            v(DI, D), v(3, D, CHUNK_N), v(T, DI), v(T, DI), v(T, CW), v(T, DI), v(T, DI), v(LANES, T), v(T, T),
            v(T, T), v(T + 8, CW), v(T, CX), v(D, T), v(DI, T), v(T, D), v(2, N, DI), v(N, DI), v(T, 2 * N),
            v(2, T, LANES), v(2, 8, CX), v(8, LANES),
            v(plan.s_ring, n_dp, h, CHUNK_N), v(plan.o_ring, n_dp, h, CHUNK_N), *received,
            v(plan.f_ring, h, CHUNK_N), v(plan.f_ring, h, CHUNK_N) if plan.wide else v(8, LANES), v(2, 8, CW),
            dma((J, plan.kinds + 1)), dma((J, plan.kinds + 1)), dma((plan.s_ring,)), dma((plan.f_ring,)), dma((8,)),
            dma((3,)), dma((2,)), dma((2,)), dma((2,)), dma((2, DI // 256)), dma((2, DI // 256)),
        ],
        compiler_params=pltpu.CompilerParams(
            collective_id=1, has_side_effects=True, vmem_limit_bytes=61 << 20
        ),
        name="backward",
    )(cot, mask, conv, head, *saved)


def on_device(hidden, cotangent, lengths, norm_gain, gate_weight, mix_weight, step_weight, conv_kernel, conv_bias,
              gated_gain, out_weight, skip_gain, log_rate, step_bias):
    n_dp, n_seq = lax.axis_size("dp"), lax.axis_size("seq")
    slots, T, D = hidden.shape
    DI, CW, H, K = gate_weight.shape[2], mix_weight.shape[2], skip_gain.shape[1], conv_kernel.shape[1]
    dims = (T, D, DI, CW, H, DI // H, (CW - DI) // 2, K)
    plan = Plan(n_dp, n_seq, dims)
    mask, conv, head, wm, wg, wo = prepare(
        hidden, lengths, norm_gain, gate_weight, mix_weight, step_weight, conv_kernel, conv_bias, gated_gain,
        out_weight, skip_gain, log_rate, step_bias, n_dp,
    )
    x = hidden[0]
    result, conv_full, *saved = forward(x, mask, conv, head, wm, wg, wo, n_dp, n_seq, dims)
    hidden_grad, gm, gg, go, gc, _ = backward(
        cotangent[0], mask, conv_full, head, (x, *saved), n_dp, n_seq, dims
    )
    gain = norm_gain[:, :, None]
    mix_grad = gm[:, :, :CW]
    step_grad = gm[:, :, CW : CW + H]
    norm_gain_grad = (
        jnp.sum(mix_grad * mix_weight, axis=2)
        + jnp.sum(gg * gate_weight, axis=2)
        + jnp.sum(step_grad * step_weight, axis=2)
    )
    gated_gain_grad = jnp.sum(go * out_weight, axis=2)
    blocks = gc[:, 0].reshape(-1, 8, CHUNK_N)[: plan.blocks]
    blocks = blocks.reshape(2, plan.mix_jobs, 8, CHUNK_N).transpose(0, 2, 1, 3).reshape(2, 8, CW + LANES)[::-1]
    shard = conv_bias.shape[1]
    own = lax.dynamic_slice(blocks, (0, 0, lax.axis_index("dp") * shard), (2, 8, shard))
    skip_grad = blocks[:, 0, CW : CW + H]
    return (
        result[None], hidden_grad[None], norm_gain_grad, gg * gain, mix_grad * gain, step_grad * gain, own[:, :K],
        own[:, K], gated_gain_grad, go * gated_gain[:, :, None], skip_grad,
    )


def solution(mesh):
    return jax.shard_map(
        on_device,
        mesh=mesh,
        in_specs=(
            P("dp", "seq", None), P("dp", "seq", None), P("dp"), P(None, "dp"), P(None, "dp", None),
            P(None, "dp", None), P(None, "dp", None), P(None, None, "dp"), P(None, "dp"), P(None, "dp"),
            P(None, "dp", None), P(), P(), P(),
        ),
        out_specs=(
            P("dp", "seq", None), P("dp", "seq", None), P(None, "dp"), P(None, "dp", None), P(None, "dp", None),
            P(None, "dp", None), P(None, None, "dp"), P(None, "dp"), P(None, "dp"), P(None, "dp", None), P(),
        ),
        check_vma=False,
    )
```

```python
import functools

import jax
import jax.numpy as jnp
from jax import lax
from jax.experimental import pallas as pl
from jax.experimental.pallas import tpu as pltpu
from jax.sharding import PartitionSpec as P

EPSILON = 1e-05
HIGH = lax.Precision.HIGH
MESH = pl.DeviceIdType.MESH
LANES = 128
F32 = jnp.float32


def mm(left, right, contract=((1,), (0,))):
    return lax.dot_general(left, right, (contract, ((), ())), precision=HIGH, preferred_element_type=F32)


NN = ((1,), (0,))
NT = ((1,), (1,))
TN = ((0,), (0,))


def split(value):
    high = value.astype(jnp.bfloat16)
    return high, (value - high.astype(F32)).astype(jnp.bfloat16)


def split3(value):
    first = value.astype(jnp.bfloat16)
    rest = value - first.astype(F32)
    second = rest.astype(jnp.bfloat16)
    third = (rest - second.astype(F32)).astype(jnp.bfloat16)
    return first, second, third


def exact(select, value, contract=((1,), (0,))):
    total = None
    for part in split3(value):
        term = lax.dot_general(select, part, (contract, ((), ())), preferred_element_type=F32)
        total = term if total is None else total + term
    return total


def exact_right(value, select, contract=((1,), (0,))):
    total = None
    for part in split3(value):
        term = lax.dot_general(part, select, (contract, ((), ())), preferred_element_type=F32)
        total = term if total is None else total + term
    return total


def iota(shape, axis):
    return lax.broadcasted_iota(jnp.int32, shape, axis)


def head_matrix(heads_padded, width, head_size, start=0):
    head = iota((heads_padded, width), 0)
    channel = iota((heads_padded, width), 1) + start
    inside = jnp.logical_and(channel >= head * head_size, channel < (head + 1) * head_size)
    return jnp.where(inside, 1.0, 0.0).astype(jnp.bfloat16)


def tri(size):
    return jnp.where(iota((size, size), 0) >= iota((size, size), 1), 1.0, 0.0)


def sigmoid(v):
    return jax.nn.sigmoid(v)


def softplus(v):
    return jnp.maximum(v, 0.0) + jnp.log1p(jnp.exp(-jnp.abs(v)))


def tiles(count, body):
    lax.fori_loop(0, count, lambda i, c: (body(i), c)[1], 0)


def lanes(i, width):
    return pl.ds(pl.multiple_of(i * width, width), width)


class Place:
    def __init__(self, dp_count, seq_count):
        self.n_dp, self.n_seq = dp_count, seq_count
        self.dp = lax.axis_index("dp")
        self.seq = lax.axis_index("seq")
        self.core = self.seq % 2
        self.z = self.seq // 2
        self.sib = self.z * 2 + (1 - self.core)
        self.parity = self.z % 2
        self.pair = (self.z + 1 - 2 * self.parity) * 2 + self.core
        y, x = self.dp // 2, self.dp % 2
        self.dpx = 2 * y + (1 - x)
        self.dpy = 2 * (1 - y) + x
        self.dpd = 2 * (1 - y) + (1 - x)


def remote(src, dst, send, recv, dp, seq):
    return pltpu.make_async_remote_copy(
        src_ref=src, dst_ref=dst, send_sem=send, recv_sem=recv, device_id=(dp, seq), device_id_type=MESH
    )


def entry_barrier(place):
    barrier = pltpu.get_barrier_semaphore()

    def greet(dp, seq):
        pl.semaphore_signal(barrier, inc=1, device_id=(dp, seq), device_id_type=MESH)

    for step in range(1, place.n_dp):
        greet((place.dp + step) % place.n_dp, place.seq)
    greet(place.dp, place.sib)
    greet(place.dp, place.pair)

    @pl.when(jnp.logical_and(place.core == 1, place.seq < place.n_seq - 1))
    def _():
        greet(place.dp, place.seq + 1)

    @pl.when(jnp.logical_and(place.core == 0, place.seq > 0))
    def _():
        greet(place.dp, place.seq - 1)

    outer = jnp.logical_or(place.seq == 0, place.seq == place.n_seq - 1)

    @pl.when(outer)
    def _():
        pl.semaphore_wait(barrier, place.n_dp + 1)

    @pl.when(jnp.logical_not(outer))
    def _():
        pl.semaphore_wait(barrier, place.n_dp + 2)


def full_barrier(place):
    barrier = pltpu.get_barrier_semaphore()
    for step in range(1, place.n_dp):
        peer = (place.dp + step) % place.n_dp
        pl.semaphore_signal(barrier, inc=1, device_id=(peer, place.seq), device_id_type=MESH)
    for step in range(1, place.n_seq):
        peer = (place.seq + step) % place.n_seq
        pl.semaphore_signal(barrier, inc=1, device_id=(place.dp, peer), device_id_type=MESH)
    pl.semaphore_wait(barrier, place.n_dp + place.n_seq - 2)


class Gather:
    def __init__(self, place, dest, stride, row_of, columns, half, sems, index):
        self.p, self.dest = place, dest
        self.stride, self.row_of, self.columns = stride, row_of, columns
        self.send, self.recv = sems
        self.index = index
        self.half = half
        self.third = half // 3
        self.wide = place.n_dp == 4 and half % 24 == 0 and place.n_seq % 4 == 0

    def at(self, owner, core, offset, count):
        start = owner * self.stride + self.row_of(core) + offset
        return self.dest.at[pl.ds(pl.multiple_of(start, 8), count), self.columns]

    def copy(self, kind, src, dst, dp, seq):
        return remote(src, dst, self.send.at[self.index, kind], self.recv.at[self.index, kind], dp, seq)

    def own_part(self, offset, count):
        return self.at(self.p.dp, self.p.core, offset, count)

    def scale(self, gain):
        for core in range(2):
            rows = self.at(self.p.dp, core, 0, self.half)
            start = self.row_of(core)
            if not isinstance(start, int):
                start = pl.multiple_of(start, 8)
            column = gain[pl.ds(start, self.half), :]
            rows[...] = rows[...] * jnp.concatenate([column] * (PIECE // LANES), axis=1)

    def get(self, kind):
        p, t = self.p, self.third
        if not self.wide:
            if kind < p.n_dp:
                peer = (p.dp + kind) % p.n_dp
                return self.copy(
                    kind, self.own_part(0, self.half), self.at(p.dp, p.core, 0, self.half), peer, p.seq
                )
            owner = (p.dp + 2 * p.n_dp - 1 - kind) % p.n_dp
            part = self.at(owner, p.core, 0, self.half)
            return self.copy(kind, part, part, p.dp, p.sib)
        first = p.parity * t
        only = 2 * t * p.parity
        miss = 2 * t * (1 - p.parity)
        if kind < 2:
            return self.copy(
                kind, self.own_part(first, 2 * t), self.at(p.dp, p.core, first, 2 * t),
                p.dpx if kind == 0 else p.dpy, p.seq,
            )
        owner, offset, count, dp, seq = {
            2: (p.dpx, first, t, p.dpy, p.seq),
            3: (p.dpy, first + t, t, p.dpx, p.seq),
            4: (p.dpx, only, t, p.dp, p.pair),
            5: (p.dpy, only, t, p.dp, p.pair),
            6: (p.dpd, only, t, p.dp, p.pair),
            7: (p.dpx, first, 2 * t, p.dp, p.sib),
            8: (p.dpy, first, 2 * t, p.dp, p.sib),
            9: (p.dpd, first, 2 * t, p.dp, p.sib),
            10: (p.dpx, miss, t, p.dp, p.sib),
            11: (p.dpy, miss, t, p.dp, p.sib),
            12: (p.dpd, miss, t, p.dp, p.sib),
        }[kind]
        part = self.at(owner, p.core, offset, count)
        return self.copy(kind, part, part, dp, seq)

    def stage(self, number):
        n = self.p.n_dp
        if not self.wide:
            if number == 0:
                for kind in range(1, n):
                    self.get(kind).start()
            elif number == 1:
                for kind in range(1, n):
                    self.get(kind).wait_recv()
                    self.get(n - 1 + kind).start()
            elif number == 4:
                for kind in range(n, 2 * n - 1):
                    self.get(kind).wait_recv()
            elif number == 5:
                for kind in range(1, 2 * n - 1):
                    self.get(kind).wait_send()
            return
        if number == 0:
            self.get(0).start()
            self.get(1).start()
        elif number == 1:
            self.get(0).wait_recv()
            for kind in (2, 4, 7):
                self.get(kind).start()
            self.get(1).wait_recv()
            for kind in (3, 5, 8):
                self.get(kind).start()
        elif number == 2:
            self.get(2).wait_recv()
            self.get(3).wait_recv()
            for kind in (6, 9):
                self.get(kind).start()
        elif number == 3:
            for kind in (4, 5, 6):
                self.get(kind).wait_recv()
                self.get(kind + 6).start()
        elif number == 4:
            for kind in range(7, 13):
                self.get(kind).wait_recv()
        else:
            for kind in range(13):
                self.get(kind).wait_send()


GATHER_OFFSETS = (0, 2, 4, 6, 7, 9)
PIECE = 384


def kinds_of(n_dp):
    return max(13, 2 * n_dp)


def forward_kernel(n_dp, n_seq, dims, *refs):
    (
        x_hbm, mask_ref, conv_ref, head_ref, norm_ref, gated_ref, wm_own, wg_own, wo_own, ws_own,
        result_ref, conv_full, xs_out, gate_out, ext_out, step_out, mo_out, sin_out, sout_out, wm_out, wg_out, wo_out,
        WM, WG, WO, xs, gate, ext, step, mo, sin, sout, conv_in, mixed, diag, ldE, dtE, ldT, gm,
        g_send, g_recv, g_local, c_send, c_recv, e_send, e_recv, r_send, r_recv, o_sem,
    ) = refs
    T, D, DI, CW, H, PS, N, K = dims
    layers = 2
    place = Place(n_dp, n_seq)
    h = D // n_dp // 2
    mix_pieces, gate_pieces, across = (CW + LANES) // PIECE, DI // PIECE, D // PIECE
    out_pieces = 2 * across
    per_layer = mix_pieces + gate_pieces + out_pieces
    early = mix_pieces + gate_pieces
    done_at = GATHER_OFFSETS[4]

    def tick(t):
        for number in reversed(range(len(GATHER_OFFSETS))):
            job = t - GATHER_OFFSETS[number]
            layer, q = job // per_layer, job % per_layer
            inside = jnp.logical_and(job >= 0, job < 2 * per_layer)

            def run(kind, dest, stride, row_of, column, number=number, job=job, layer=layer):
                piece = Gather(place, dest.at[layer], stride, row_of, lanes(column, PIECE), h, (g_send, g_recv), job)
                if number == 0:
                    first = job == layer * per_layer + (0, mix_pieces, early)[kind]

                    @pl.when(first)
                    def _():
                        own_copy(kind, layer).wait()
                        if kind == 0:
                            own_copy(3, layer).wait()

                    piece.scale((norm_ref, norm_ref, gated_ref)[kind].at[layer])
                piece.stage(number)

            @pl.when(jnp.logical_and(inside, q < mix_pieces))
            def _():
                run(0, WM, 2 * h, lambda core: core * h, q)

            @pl.when(jnp.logical_and(inside, jnp.logical_and(q >= mix_pieces, q < early)))
            def _():
                run(1, WG, 2 * h, lambda core: core * h, q - mix_pieces)

            @pl.when(jnp.logical_and(inside, q >= early))
            def _():
                part = (q - early) // across
                run(2, WO, 4 * h, lambda core: core * 2 * h + part * h, (q - early) % across)

    def own_copy(kind, layer):
        own, dest, start, count = (
            (wm_own, WM, 0, CW), (wg_own, WG, 0, DI), (wo_own, WO, 0, D), (ws_own, WM, CW, LANES)
        )[kind]
        rows = own.shape[1]
        at = pl.ds(pl.multiple_of(place.dp * rows, 8), rows)
        target = dest.at[layer, at, pl.ds(start, count)]
        return pltpu.make_async_copy(own.at[layer], target, g_local.at[layer * 4 + kind])

    for layer in range(layers):
        for kind in (0, 3, 1, 2):
            own_copy(kind, layer).start()
    first_in = pltpu.make_async_copy(x_hbm, xs.at[0], o_sem.at[0])
    first_in.start()
    ext[0, 0:8, :] = jnp.zeros((8, CW), F32)
    ext[1, 0:8, :] = jnp.zeros((8, CW), F32)
    entry_barrier(place)
    tick(0)
    def conv_copy(step_index):
        peer = (place.dp + step_index) % n_dp
        return remote(
            conv_ref, conv_in.at[place.dp], c_send.at[step_index - 1], c_recv.at[step_index - 1], peer, place.seq
        )

    for s in range(1, n_dp):
        conv_copy(s).start()
    conv_in[place.dp] = conv_ref[...]
    first_in.wait()
    tiles(done_at, lambda i: tick(i + 1))
    per_body = mix_pieces + 1 + (H // 2 + gate_pieces) // 3 + across
    ti, tj = iota((T, T), 0), iota((T, T), 1)
    lane_low = iota((T, LANES), 1) < PS
    CHUNK = 256
    chunks = DI // CHUNK

    def saved_copies(layer):
        saved = (
            (gate, gate_out), (ext, ext_out), (step, step_out), (mo, mo_out), (sin, sin_out), (sout, sout_out),
            (WM, wm_out), (WG, wg_out), (WO, wo_out),
        )
        return [
            functools.partial(lambda a, b, k: pltpu.make_async_copy(a.at[layer], b.at[layer], o_sem.at[layer * 9 + k + 1]), a, b, k)
            for k, (a, b) in enumerate(saved)
        ]

    def layer_body(layer, carry):
        x_all = xs[layer]
        inv = lax.rsqrt(jnp.mean(x_all * x_all, axis=-1, keepdims=True) + EPSILON)
        diag[:, 0:D] = x_all * inv
        head = head_ref[layer]
        base = done_at + 1 + layer * per_body
        def project_mix(i):
            ext[layer, 8 : T + 8, lanes(i, PIECE)] = mm(diag[:, 0:D], WM[layer, :, lanes(i, PIECE)])
            tick(base + i)

        tiles(mix_pieces - 1, project_mix)
        last = (mix_pieces - 1) * PIECE
        value = mm(diag[:, 0:D], WM[layer, :, last : last + PIECE])
        ext[layer, 8 : T + 8, last:CW] = value[:, 0 : CW - last]
        raw = value[:, CW - last :]
        edge = remote(
            ext.at[layer, pl.ds(T, 8)], ext.at[layer, pl.ds(0, 8)], e_send.at[layer], e_recv.at[layer],
            place.dp, place.seq + 1,
        )

        @pl.when(place.seq < n_seq - 1)
        def _():
            edge.start()

        step[layer] = raw
        tick(base + mix_pieces - 1)
        saved_copies(layer)[6]().start()
        dt = softplus(raw + head[1:2, :])
        rate = -jnp.exp(head[0:1, :]) * dt
        ld = exact(tri(T).astype(jnp.bfloat16), rate)
        ldT[...] = ld.T

        def expand(i):
            select = head_matrix(LANES, 256, PS, i * 256)
            ldE[:, lanes(i, 256)] = exact_right(ld, select)
            dtE[:, lanes(i, 256)] = exact_right(dt, select)

        tiles(DI // 256, expand)

        @pl.when(layer == 0)
        def _():
            for s in range(1, n_dp):
                conv_copy(s).wait_recv()

            def sum_taps(i):
                at = lanes(i, 256)
                taps = conv_in[0, :, at]
                for s in range(1, n_dp):
                    taps = taps + conv_in[s, :, at]
                conv_full[:, at] = taps

            tiles(CW // 256, sum_taps)

        @pl.when(place.seq > 0)
        def _():
            edge.wait_recv()

        def conv(i):
            at = lanes(i, 256)
            taps = conv_full[pl.ds(pl.multiple_of(layer * 8, 8), 8), at]
            total = taps[K : K + 1, :]
            for k in range(K):
                total = total + taps[k : k + 1, :] * ext[layer, 8 - K + 1 + k : 8 - K + 1 + k + T, at]
            mixed[:, at] = total * sigmoid(total)

        tiles(CW // 256, conv)
        tick(base + mix_pieces)
        b_map = mixed[:, DI : DI + N]
        c_map = mixed[:, DI + N : DI + 2 * N]
        gm[...] = jnp.where(ti >= tj, mm(c_map, b_map, NT), 0.0)

        def local_state(i):
            at = lanes(i, 256)
            l_tile = ldE[:, at]
            weighted = mixed[:, at] * dtE[:, at] * jnp.exp(l_tile[T - 1 : T, :] - l_tile)
            sout[layer, :, at] = mm(b_map, weighted, TN)

        tiles(DI // 256, local_state)

        def relay_copy(chunk):
            at = lanes(chunk, CHUNK)
            return remote(
                sout.at[layer, :, at], sin.at[layer, :, at], r_send.at[layer, chunk], r_recv.at[layer, chunk],
                place.dp, place.seq + 1,
            )

        def relay(chunk):
            at = lanes(chunk, CHUNK)

            @pl.when(place.seq > 0)
            def _():
                relay_copy(chunk).wait_recv()
                total = jnp.exp(ldE[T - 1 : T, at])
                sout[layer, :, at] = sout[layer, :, at] + total * sin[layer, :, at]

            @pl.when(place.seq == 0)
            def _():
                sin[layer, :, at] = jnp.zeros((N, CHUNK), F32)

            @pl.when(place.seq < n_seq - 1)
            def _():
                relay_copy(chunk).start()

        pairs = H // 2

        items = pairs + gate_pieces
        relay_from = place.seq * (items - chunks) // (n_seq - 1)

        def diagonal(i):
            at = lanes(i, LANES)
            scaled = mixed[:, at] * dtE[:, at]
            l_tile = ldE[:, at]
            parts = []
            for side in range(2):
                column = l_tile[:, side * PS : side * PS + 1]
                row = ldT[pl.ds(2 * i + side, 1), :]
                weights = gm[...] * jnp.exp(jnp.minimum(column - row, 0.0))
                parts.append(mm(weights, scaled))
            diag[:, at] = jnp.where(lane_low, parts[0], parts[1])


        def gate_proj(i):
            at = lanes(i, PIECE)
            gate[layer, :, at] = mm(xs[layer] * inv, WG[layer, :, at])

        def work_item(i):
            @pl.when(i < pairs)
            def _():
                diagonal(i)

            @pl.when(i >= pairs)
            def _():
                gate_proj(i - pairs)

            @pl.when(jnp.logical_and(i >= relay_from, i < relay_from + chunks))
            def _():
                relay(i - relay_from)

            @pl.when(i % 3 == 2)
            def _():
                tick(base + mix_pieces + 1 + i // 3)

        tiles(items, work_item)
        saved_copies(layer)[7]().start()

        def skip_row(i):
            return exact_right(head[2:3, :], head_matrix(LANES, 256, PS, i * 256))

        def off(i):
            at = lanes(i, 256)
            lift = jnp.exp(ldE[:, at])
            out = diag[:, at] + lift * mm(c_map, sin[layer, :, at]) + skip_row(i) * mixed[:, at]
            mo[layer, :, at] = out

        tiles(DI // 256, off)

        def gating(i, squares):
            at = lanes(i, LANES)
            pre = gate[layer, :, at]
            gated = mo[layer, :, at] * (pre * sigmoid(pre))
            diag[:, at] = gated
            return squares + gated * gated

        squares = lax.fori_loop(0, DI // LANES, gating, jnp.zeros((T, LANES), F32))
        inv_out = lax.rsqrt(jnp.sum(squares, axis=-1, keepdims=True) / DI + EPSILON)
        tiles(across, lambda i: tick(base + mix_pieces + 1 + items // 3 + i))

        def project_out(i):
            at = lanes(i, PIECE)
            branch = mm(diag[...] * inv_out, WO[layer, :, at])
            nxt = xs[layer, :, at] + branch
            xs[layer + 1, :, at] = nxt

        tiles(across, project_out)
        for number, copy in enumerate(saved_copies(layer)):
            if number < 6 or number == 8:
                copy().start()
        @pl.when(place.seq < n_seq - 1)
        def _():
            edge.wait_send()
            tiles(chunks, lambda c: relay_copy(c).wait_send())

        return carry

    lax.fori_loop(0, layers, layer_body, 0)
    done = done_at + 1 + layers * per_body
    left = layers * per_layer + GATHER_OFFSETS[5] - done
    if left > 0:
        tiles(left, lambda i: tick(done + i))
    result_ref[...] = xs[layers] * mask_ref[...]
    last = pltpu.make_async_copy(xs.at[1], xs_out, o_sem.at[0])
    last.start()
    for s in range(1, n_dp):
        conv_copy(s).wait_send()
    for layer in range(layers):
        for copy in saved_copies(layer):
            copy().wait()
    last.wait()


def forward(x, mask, conv, head, norm, gated, wm, wg, wo, ws, n_dp, n_seq, dims):
    T, D, DI, CW, H, PS, N, K = dims
    any_spec = pl.BlockSpec(memory_space=pl.ANY)
    vmem = pl.BlockSpec(memory_space=pltpu.VMEM)
    CX = CW + LANES
    kinds = kinds_of(n_dp)
    PIECES = 2 * ((CW + LANES) // PIECE + DI // PIECE + 2 * (D // PIECE))
    sd = lambda *s: jax.ShapeDtypeStruct(s, F32)
    v = lambda *s: pltpu.VMEM(s, F32)
    dma = pltpu.SemaphoreType.DMA
    return pl.pallas_call(
        functools.partial(forward_kernel, n_dp, n_seq, dims),
        out_shape=(
            sd(T, D), sd(16, CW), sd(T, D), sd(2, T, DI), sd(2, T + 8, CW), sd(2, T, LANES), sd(2, T, DI), sd(2, N, DI),
            sd(2, N, DI), sd(2, D, CX), sd(2, D, DI), sd(2, DI, D),
        ),
        in_specs=[any_spec] + [vmem] * 5 + [any_spec] * 4,
        out_specs=(vmem, vmem) + (any_spec,) * 10,
        scratch_shapes=[
            v(2, D, CX), v(2, D, DI), v(2, DI, D), v(3, T, D), v(2, T, DI), v(2, T + 8, CW), v(2, T, LANES),
            v(2, T, DI), v(2, N, DI), v(2, N, DI), v(n_dp, 16, CW), v(T, CW), v(T, DI), v(T, DI), v(T, DI),
            v(LANES, T), v(T, T),
            dma((PIECES, kinds)), dma((PIECES, kinds)), dma((8,)), dma((n_dp - 1,)), dma((n_dp - 1,)), dma((2,)), dma((2,)),
            dma((2, DI // 256)), dma((2, DI // 256)), dma((19,)),
        ],
        compiler_params=pltpu.CompilerParams(
            collective_id=0, has_side_effects=True, vmem_limit_bytes=61 << 20
        ),
        name="forward",
    )(x, mask, conv, head, norm, gated, wm, wg, wo, ws)


def prepare(hidden, lengths, norm_gain, gate_weight, mix_weight, step_weight, conv_kernel, conv_bias, gated_gain,
            out_weight, skip_gain, log_rate, step_bias, n_dp):
    T = hidden.shape[1]
    H = skip_gain.shape[1]
    shard = conv_bias.shape[1]
    CW = shard * n_dp
    position = lax.axis_index("seq") * T + lax.iota(jnp.int32, T)
    mask = (position < lengths[0]).astype(F32)[:, None]
    step_pad = jnp.pad(step_weight, ((0, 0), (0, 0), (0, LANES - H)))
    norm = jnp.broadcast_to(norm_gain[:, :, None], norm_gain.shape + (LANES,))
    gated = jnp.broadcast_to(gated_gain[:, :, None], gated_gain.shape + (LANES,))
    head = jnp.pad(jnp.stack([log_rate, step_bias, skip_gain], axis=1), ((0, 0), (0, 5), (0, LANES - H)))
    own = jnp.concatenate([conv_kernel, conv_bias[:, None, :]], axis=1)
    own = jnp.pad(own, ((0, 0), (0, 8 - own.shape[1]), (0, 0))).reshape(16, shard)
    conv = lax.dynamic_update_slice(jnp.zeros((16, CW), F32), own, (0, lax.axis_index("dp") * shard))
    return mask, conv, head, norm, gated, step_pad
CHUNK_N = 384


class Plan:
    def __init__(self, n_dp, n_seq, dims):
        T, D, DI, CW, H, PS, N, K = dims
        self.n_dp, self.n_seq = n_dp, n_seq
        self.n_z = n_seq // 2
        self.h = D // n_dp // 2
        self.out_jobs = 2 * (D // CHUNK_N)
        self.gate_jobs = DI // CHUNK_N
        self.mix_jobs = (CW + LANES) // CHUNK_N
        self.lead, self.bubbles = 2, 3
        self.per_layer = self.out_jobs + self.gate_jobs + self.mix_jobs
        self.early = self.out_jobs + self.gate_jobs
        self.slots = self.lead + self.per_layer + self.bubbles
        self.blocks = 2 * self.mix_jobs
        self.blocks_per_job = self.h // 8
        self.conv_jobs = -(-self.blocks // self.blocks_per_job)
        self.jobs = 2 * self.per_layer + self.conv_jobs
        self.total_slots = 2 * self.slots + self.conv_jobs
        self.wide = n_dp == 4 and self.n_z == 4 and self.h % 32 == 0
        self.rounds = self.n_z.bit_length() - 1
        self.offsets = (0, 1, 1, 4, 6, 8, 10, 12, 15, 16)
        self.o_ring = self.offsets[4] + 1
        self.f_ring = max(self.offsets) + 1
        self.r_ring = self.offsets[4] - self.offsets[2] + 2
        self.z_ring = self.offsets[8] - self.offsets[4] + 1
        self.half_ring = self.offsets[7] - self.offsets[5] + 2
        self.w_ring = self.offsets[8] - self.offsets[7] + 1
        self.s_ring = self.offsets[2] + 1
        self.in_ring = self.offsets[2] + 2
        self.kinds = 12 if self.wide else n_dp - 1 + self.rounds + 2
        self.sibling_kind = self.kinds - 1

    def job_of(self, slot):
        layer = slot // self.slots
        q = slot % self.slots - self.lead
        early = jnp.logical_and(q >= 0, q < self.early)
        late = q >= self.early + self.bubbles
        inside = jnp.logical_and(slot >= 0, slot < 2 * self.slots)
        valid = jnp.logical_and(inside, jnp.logical_or(early, late))
        job = layer * self.per_layer + q - jnp.where(early, 0, self.bubbles)
        conv = jnp.logical_and(slot >= 2 * self.slots, slot < self.total_slots)
        job = jnp.where(slot >= 2 * self.slots, 2 * self.per_layer + slot - 2 * self.slots, job)
        return jnp.logical_or(valid, conv), job


class Reducer:
    def __init__(self, place, plan, refs, outs):
        self.p, self.plan = place, plan
        self.S, self.O, self.R, self.rx, self.ry, self.r2x, self.r2y, self.z1, self.z2, self.G, self.F, self.W, self.gains, self.sums, self.weights, self.send, self.recv, self.loc, self.fin, self.wsem = refs
        self.outs = outs

    def copy(self, job, kind, src, dst, dp, seq):
        return remote(src, dst, self.send.at[job, kind], self.recv.at[job, kind], dp, seq)

    def own(self, job, owner, start, count):
        ring = lax.rem(job, self.plan.o_ring)
        if not isinstance(start, int):
            start = pl.multiple_of(start, 8)
        return self.O.at[ring, owner, pl.ds(start, count)]

    def mine(self, job, start, count):
        return self.own(job, self.p.dp, start, count)

    def summed(self, job, start, count):
        ring = lax.rem(job, self.plan.f_ring)
        if not isinstance(start, int):
            start = pl.multiple_of(start, 8)
        return self.G.at[ring, pl.ds(start, count)]

    def to_sibling(self, job):
        ring = lax.rem(job, self.plan.s_ring)
        kind = self.plan.kinds - 2
        into = lax.rem(job, self.plan.in_ring)
        return self.copy(job, kind, self.S.at[ring], self.R.at[into], self.p.dp, self.p.sib)

    def slot(self, job):
        return lax.rem(job, self.plan.r_ring)

    def z_slot(self, job):
        return lax.rem(job, self.plan.z_ring)

    def half_slot(self, job):
        return lax.rem(job, self.plan.half_ring)

    def xy(self, job, kind):
        p, half = self.p, self.plan.h // 2
        low, high = (0, half), (half, half)
        return {
            0: lambda: self.copy(job, 0, self.own(job, p.dpx, *low), self.rx.at[self.slot(job), 0], p.dpx, p.seq),
            1: lambda: self.copy(job, 1, self.own(job, p.dpd, *low), self.rx.at[self.slot(job), 1], p.dpx, p.seq),
            2: lambda: self.copy(job, 2, self.own(job, p.dpy, *high), self.ry.at[self.slot(job), 0], p.dpy, p.seq),
            3: lambda: self.copy(job, 3, self.own(job, p.dpd, *high), self.ry.at[self.slot(job), 1], p.dpy, p.seq),
            4: lambda: self.copy(job, 4, self.own(job, p.dpy, *low), self.r2y.at[self.slot(job)], p.dpy, p.seq),
            5: lambda: self.copy(job, 5, self.own(job, p.dpx, *high), self.r2x.at[self.slot(job)], p.dpx, p.seq),
        }[kind]()

    def keep(self):
        return (self.p.z - 1) * (self.plan.h // 2)

    def zed(self, job, kind):
        p, h = self.p, self.plan.h
        across = (self.plan.n_z - 1 - p.z) * 2 + p.core
        if kind == 6:
            return self.copy(job, 6, self.summed(job, 0, h), self.z1.at[self.z_slot(job)], p.dp, p.pair)
        if kind == 7:
            start = (2 - p.z) * (h // 2)
            return self.copy(job, 7, self.summed(job, start, h // 2), self.z2.at[self.half_slot(job)], p.dp, across)
        if kind == 8:
            part = self.whole(job, self.keep(), h // 2)
            return self.copy(job, 8, part, part, p.dp, across)
        part = self.whole(job, 0, h)
        return self.copy(job, 9, part, part, p.dp, p.pair)

    def inner(self):
        return jnp.logical_and(self.p.z > 0, self.p.z < self.plan.n_z - 1)

    def whole(self, job, start, count):
        ring = lax.rem(job, self.plan.f_ring)
        if not isinstance(start, int):
            start = pl.multiple_of(start, 8)
        return self.F.at[ring, pl.ds(start, count)]

    def direct(self, job, step):
        p, h = self.p, self.plan.h
        peer = lax.rem(p.dp + step, p.n_dp)
        return self.copy(job, step - 1, self.own(job, peer, 0, h), self.rx.at[self.slot(job), step - 1], peer, p.seq)

    def butterfly(self, job, rnd):
        p, h = self.p, self.plan.h
        bit = (p.z // (1 << rnd)) % 2
        peer = (p.z + (1 << rnd) - 2 * bit * (1 << rnd)) * 2 + p.core
        kind = p.n_dp - 1 + rnd
        return self.copy(job, kind, self.summed(job, 0, h), self.z1.at[self.z_slot(job), rnd], p.dp, peer)

    def add(self, dst, src):
        dst[...] = dst[...] + src[...]

    def stage(self, number, job):
        plan, p = self.plan, self.p
        h = plan.h
        half = h // 2
        if number == 0:
            self.to_sibling(job).start()
        elif number == 1:
            return
        elif number == 2:
            copy = self.to_sibling(job)
            copy.wait_recv()
            copy.wait_send()
            ring = lax.rem(job, plan.in_ring)
            o_ring = lax.rem(job, plan.o_ring)

            def add_owner(o):
                self.O[o_ring, o] = self.O[o_ring, o] + self.R[ring, o]

            tiles(plan.n_dp, add_owner)
            if plan.wide:
                for kind in range(4):
                    self.xy(job, kind).start()
            else:
                for step in range(1, plan.n_dp):
                    self.direct(job, step).start()
        elif number == 3:
            if plan.wide:
                for kind in range(4):
                    self.xy(job, kind).wait_recv()
                self.add(self.own(job, p.dpy, 0, half), self.rx.at[self.slot(job), 1])
                self.add(self.own(job, p.dpx, half, half), self.ry.at[self.slot(job), 1])
                self.add(self.mine(job, 0, half), self.rx.at[self.slot(job), 0])
                self.add(self.mine(job, half, half), self.ry.at[self.slot(job), 0])
                self.xy(job, 4).start()
                self.xy(job, 5).start()
            else:
                for step in range(1, plan.n_dp):
                    self.direct(job, step).wait_recv()
                    self.add(self.mine(job, 0, h), self.rx.at[self.slot(job), step - 1])
        elif number == 4:
            if plan.wide:
                self.xy(job, 4).wait_recv()
                self.summed(job, 0, half)[...] = self.mine(job, 0, half)[...] + self.r2y[self.slot(job)]
                self.xy(job, 5).wait_recv()
                self.summed(job, half, half)[...] = self.mine(job, half, half)[...] + self.r2x[self.slot(job)]

                @pl.when(jnp.logical_not(self.inner()))
                def _():
                    self.zed(job, 6).start()

                for kind in range(6):
                    self.xy(job, kind).wait_send()
            else:
                self.summed(job, 0, h)[...] = self.mine(job, 0, h)[...]
                for step in range(1, plan.n_dp):
                    self.direct(job, step).wait_send()
                if plan.rounds > 0:
                    self.butterfly(job, 0).start()
        elif number == 5:
            if plan.wide:

                @pl.when(self.inner())
                def _():
                    self.zed(job, 6).wait_recv()
                    self.add(self.summed(job, 0, h), self.z1.at[self.z_slot(job)])
                    self.zed(job, 7).start()

            else:
                self.exchange(job, 0)
        elif number == 6:
            if plan.wide:

                @pl.when(self.inner())
                def _():
                    self.zed(job, 7).wait_recv()
                    part = self.summed(job, self.keep(), half)[...] + self.z2[self.half_slot(job)]
                    self.whole(job, self.keep(), half)[...] = part
                    self.zed(job, 8).start()

            else:
                self.exchange(job, 1)
        elif number == 7:
            self.weight(job, "start")
            if plan.wide:

                @pl.when(self.inner())
                def _():
                    self.zed(job, 8).wait_recv()
                    self.zed(job, 9).start()

        elif number == 8:
            if plan.wide:

                @pl.when(self.inner())
                def _():
                    for kind in (7, 8, 9):
                        self.zed(job, kind).wait_send()

                @pl.when(jnp.logical_not(self.inner()))
                def _():
                    self.zed(job, 9).wait_recv()
                    self.zed(job, 6).wait_send()

            else:
                for rnd in range(2, max(plan.rounds, 3)):
                    self.exchange(job, rnd)
            self.scale(job)
            self.final(job, "start")
        else:
            self.final(job, "wait")

    def exchange(self, job, rnd):
        if rnd >= self.plan.rounds:
            return
        copy = self.butterfly(job, rnd)
        copy.wait_recv()
        copy.wait_send()
        self.add(self.summed(job, 0, self.plan.h), self.z1.at[self.z_slot(job), rnd])
        if rnd + 1 < self.plan.rounds:
            self.butterfly(job, rnd + 1).start()

    def kind_of(self, job):
        plan = self.plan
        second = job >= plan.per_layer
        q = job - jnp.where(second, plan.per_layer, 0)
        normal = job < 2 * plan.per_layer
        layer = jnp.where(second, 0, 1)
        is_out = jnp.logical_and(normal, q < plan.out_jobs)
        is_gate = jnp.logical_and(normal, jnp.logical_and(q >= plan.out_jobs, q < plan.early))
        is_mix = jnp.logical_and(normal, q >= plan.early)
        return layer, q, normal, is_out, is_gate, is_mix

    def total(self, job):
        return self.whole(job, 0, self.plan.h) if self.plan.wide else self.summed(job, 0, self.plan.h)

    def weight(self, job, what):
        plan, p = self.plan, self.p
        h = plan.h
        layer, q, normal, is_out, is_gate, is_mix = self.kind_of(job)
        wm, wg, wo = self.weights
        slot = lax.rem(job, plan.w_ring)
        per_row = plan.out_jobs // 2

        def go_for(source, row, column):
            at = (layer, pl.ds(pl.multiple_of(row, 8), h), lanes(column, CHUNK_N))
            copy = pltpu.make_async_copy(source.at[at], self.W.at[slot], self.wsem.at[slot])
            getattr(copy, what)()

        pl.when(is_out)(
            lambda: go_for(wo, p.dp * 4 * h + p.core * 2 * h + (q // per_row) * h, lax.rem(q, per_row))
        )
        pl.when(is_gate)(lambda: go_for(wg, p.dp * 2 * h + p.core * h, q - plan.out_jobs))
        pl.when(is_mix)(lambda: go_for(wm, p.dp * 2 * h + p.core * h, q - plan.early))

    def scale(self, job):
        plan, p = self.plan, self.p
        h = plan.h
        layer, q, normal, is_out, is_gate, is_mix = self.kind_of(job)
        norm, gated = self.gains
        norm_sum, gated_sum = self.sums
        slot = lax.rem(job, plan.w_ring)
        total = self.total(job)
        self.weight(job, "wait")

        def apply(sums, gain):
            value = total[...]
            product = value * self.W[slot]
            lane_sum = product[:, 0:LANES]
            for part in range(1, CHUNK_N // LANES):
                lane_sum = lane_sum + product[:, part * LANES : (part + 1) * LANES]
            sums[...] = sums[...] + lane_sum
            total[...] = value * jnp.concatenate([gain[...]] * (CHUNK_N // LANES), axis=1)

        @pl.when(is_out)
        def _():
            part = q // (plan.out_jobs // 2)
            rows = pl.ds(pl.multiple_of(p.core * 2 * h + part * h, 8), h)
            apply(gated_sum.at[layer, pl.ds(pl.multiple_of(part * h, 8), h)], gated.at[layer, rows])

        @pl.when(jnp.logical_or(is_gate, is_mix))
        def _():
            apply(norm_sum.at[layer], norm.at[layer, pl.ds(pl.multiple_of(p.core * h, 8), h)])

    def final(self, job, what):
        plan, p = self.plan, self.p
        h = plan.h
        gm, gs, gg, go, gc = self.outs
        layer, q, normal, is_out, is_gate, is_mix = self.kind_of(job)
        src = self.total(job)
        per_row = plan.out_jobs // 2
        last = plan.mix_jobs - 1
        edge = gm.shape[2] - last * CHUNK_N
        ring = lax.rem(job, plan.f_ring)
        extra = plan.kinds

        def rows(start):
            return pl.ds(pl.multiple_of(start, 8), h)

        def put(core):
            at = rows(core * h)
            return (
                (is_out, lambda: [(None, go.at[layer, rows(core * 2 * h + (q // per_row) * h), lanes(lax.rem(q, per_row), CHUNK_N)])]),
                (is_gate, lambda: [(None, gg.at[layer, at, lanes(q - plan.out_jobs, CHUNK_N)])]),
                (
                    jnp.logical_and(is_mix, q - plan.early < last),
                    lambda: [(None, gm.at[layer, at, lanes(q - plan.early, CHUNK_N)])],
                ),
                (
                    jnp.logical_and(is_mix, q - plan.early == last),
                    lambda: [
                        ((0, edge), gm.at[layer, at, pl.ds(last * CHUNK_N, edge)]),
                        ((edge, CHUNK_N - edge), gs.at[layer, at]),
                    ],
                ),
                (jnp.logical_not(normal), lambda: [(None, gc.at[job - 2 * plan.per_layer, core])]),
            )

        def go_for(make, which):
            for number, (columns, target) in enumerate(make()):
                part = src if columns is None else src.at[:, pl.ds(*columns)]
                kind = plan.sibling_kind if number == 0 else extra
                local = pltpu.make_async_copy(part, target, self.fin.at[number, ring])
                away = self.copy(job, kind, part, target, p.dp, p.sib)
                if which == "start":
                    local.start()
                    away.start()
                elif which == "wait":
                    local.wait()
                    away.wait_send()
                else:
                    away.wait_recv()

        for when, make in put(p.core):
            pl.when(when)(functools.partial(go_for, make, what))
        if what == "wait":
            for when, make in put(1 - p.core):
                pl.when(when)(functools.partial(go_for, make, "arrived"))

    def tick(self, t):
        for number in reversed(range(len(self.plan.offsets))):
            valid, job = self.plan.job_of(t - self.plan.offsets[number])

            @pl.when(valid)
            def _():
                self.stage(number, job)


def backward_kernel(n_dp, n_seq, dims, *refs):
    T, D, DI, CW, H, PS, N, K = dims
    plan = Plan(n_dp, n_seq, dims)
    (
        cot_ref, mask_ref, conv_ref, head_ref, norm_ref, gated_ref, x0_hbm, x1_hbm, gate_hbm, ext_hbm, step_hbm, mo_hbm, sin_hbm,
        sout_hbm, wm_hbm, wg_hbm, wo_hbm,
        hg_ref, gm, gs, gg, go, gc, norm_out, gated_out,
        grad, x, gate, ext, step, mo, sin, sout, wrow, wcol, U, V, mixed, ldE, dtE, ldT, gmT, dgT, PG, raw, nT, gnT,
        NG, dS, dSin, maps, heads, convg, rows,
        S, R, O, rx, ry, r2x, r2y, z1, z2, G, F, edge_in, W, norm_sum, gated_sum,
        j_send, j_recv, s_loc, f_loc, wt_sem, gain_sem, l_sem, w_sem, v_sem, e_send, e_recv, r_send, r_recv,
    ) = refs
    place = Place(n_dp, n_seq)
    h = plan.h
    red = Reducer(
        place,
        plan,
        (
            S, O, R, rx, ry, r2x, r2y, z1, z2, G, F, W, (norm_ref, gated_ref), (norm_sum, gated_sum),
            (wm_hbm, wg_hbm, wo_hbm), j_send, j_recv, s_loc, f_loc, wt_sem,
        ),
        (gm, gs, gg, go, gc),
    )
    norm_sum[...] = jnp.zeros(norm_sum.shape, F32)
    gated_sum[...] = jnp.zeros(gated_sum.shape, F32)
    CX = CW + LANES
    CHUNK = 256
    chunks = DI // CHUNK
    pairs = H // 2

    def load_of(layer, k):
        source, target = (
            (mo_hbm, mo), (gate_hbm, gate), (step_hbm, step), (ext_hbm, ext), (sin_hbm, sin), (sout_hbm, sout),
            (wo_hbm, wrow),
        )[k]
        return pltpu.make_async_copy(source.at[layer], target, l_sem.at[k])

    class Load:
        def __init__(self, layer, k):
            self.layer, self.k = layer, k

        def wait(self):
            load_of(self.layer, self.k).wait()

    for k in range(7):
        load_of(1, k).start()

    def load_x(layer_value, action):
        @pl.when(layer_value == 1)
        def _():
            getattr(pltpu.make_async_copy(x1_hbm, x, l_sem.at[7]), action)()

        @pl.when(layer_value == 0)
        def _():
            getattr(pltpu.make_async_copy(x0_hbm, x, l_sem.at[7]), action)()

    grad[...] = cot_ref[...] * mask_ref[...]
    PG[T : T + 8, :] = jnp.zeros((8, CW), F32)
    full_barrier(place)
    ti, tj = iota((T, T), 0), iota((T, T), 1)
    lane_low = iota((T, LANES), 1) < PS

    def produce(job, lhs, stride, offset_of, rhs):
        ring_s = lax.rem(job, plan.s_ring)
        ring_o = lax.rem(job, plan.o_ring)
        for target, buffer, ring in ((1 - place.core, S, ring_s), (place.core, O, ring_o)):
            left = jnp.concatenate(
                [lhs[pl.ds(pl.multiple_of(o * stride + offset_of(target), 8), h), :] for o in range(n_dp)], axis=0
            )
            result = mm(left, rhs)
            for o in range(n_dp):
                buffer[ring, o] = result[o * h : (o + 1) * h]

    def column_stream(hbm, count, layer, body):
        def fetch(i, slot):
            return pltpu.make_async_copy(hbm.at[layer, :, lanes(i, CHUNK_N)], wcol.at[slot], w_sem.at[slot])

        fetch(0, 0).start()
        fetch(1, 1).start()

        def run(i):
            slot = lax.rem(i, 3)
            fetch(i, slot).wait()

            @pl.when(i + 2 < count)
            def _():
                fetch(i + 2, lax.rem(i + 2, 3)).start()

            body(i, slot)

        return run

    def layer_body(li, carry):
        layer = 1 - li
        base = li * plan.slots
        first_job = li * plan.per_layer
        head = head_ref[layer]
        loads = [Load(layer, k) for k in range(7)]
        load_x(layer, "start")

        loads[0].wait()
        loads[1].wait()

        def regate(i, squares):
            at = lanes(i, LANES)
            pre = gate[:, at]
            gated = mo[:, at] * (pre * sigmoid(pre))
            U[:, at] = gated
            return squares + gated * gated

        squares = lax.fori_loop(0, DI // LANES, regate, jnp.zeros((T, LANES), F32))
        inv_out = lax.rsqrt(jnp.sum(squares, axis=-1, keepdims=True) / DI + EPSILON)
        red.tick(base)
        loads[6].wait()

        def back_out(i, sums):
            at = lanes(i, 256)
            q = mm(grad[...], wrow[at, :], NT)
            V[:, at] = q
            gated = U[:, at]
            gnT[at, :] = (gated * inv_out).T
            product = q * gated
            return sums + product[:, 0:LANES] + product[:, LANES:256]

        sums = lax.fori_loop(0, DI // 256, back_out, jnp.zeros((T, LANES), F32))
        pull = jnp.sum(sums, axis=-1, keepdims=True) / DI * (inv_out * inv_out * inv_out)

        red.tick(base + 1)

        @pl.when(li == 0)
        def _():
            load_of(0, 6).start()

        def out_piece(i):
            per_row = plan.out_jobs // 2
            part = i // per_row
            rhs = grad[:, lanes(i % per_row, CHUNK_N)]
            produce(first_job + i, gnT, 4 * h, lambda target: target * 2 * h + part * h, rhs)

        def out_job(i):
            out_piece(i)
            red.tick(base + plan.lead + i)

        def degate(i):
            at = lanes(i, LANES)
            pre = gate[:, at]
            sig = sigmoid(pre)
            gated_grad = inv_out * V[:, at] - U[:, at] * pull
            gate[:, at] = gated_grad * mo[:, at] * (sig * (1.0 + pre * (1.0 - sig)))
            V[:, at] = gated_grad * (pre * sig)

        tiles(DI // LANES, degate)
        out_job(0)
        load_x(layer, "wait")
        inv_in = lax.rsqrt(jnp.mean(x[...] * x[...], axis=-1, keepdims=True) + EPSILON)
        for copy in loads[2:6]:
            copy.wait()
        raw_step = step[...]
        dt = softplus(raw_step + head[1:2, :])
        ld = exact(tri(T).astype(jnp.bfloat16), -jnp.exp(head[0:1, :]) * dt)
        ldT[...] = ld.T

        def expand(i):
            select = head_matrix(LANES, 256, PS, i * 256)
            ldE[:, lanes(i, 256)] = exact_right(ld, select)
            dtE[:, lanes(i, 256)] = exact_right(dt, select)

        tiles(DI // 256, expand)

        def conv_value(at):
            taps = conv_ref[pl.ds(pl.multiple_of(layer * 8, 8), 8), at]
            total = taps[K : K + 1, :]
            for k in range(K):
                total = total + taps[k : k + 1, :] * ext[8 - K + 1 + k : 8 - K + 1 + k + T, at]
            return taps, total

        def conv(i):
            at = lanes(i, 256)
            total = conv_value(at)[1]
            mixed[:, at] = total * sigmoid(total)

        tiles(CW // 256, conv)
        out_job(1)
        b_map = mixed[:, DI : DI + N]
        c_map = mixed[:, DI + N : DI + 2 * N]
        gmT[...] = jnp.where(ti <= tj, mm(b_map, c_map, NT), 0.0)
        dgT[...] = jnp.zeros((T, T), F32)
        maps[...] = jnp.zeros((T, 2 * N), F32)

        def back_state(i):
            at = lanes(i, 256)
            lifted = V[:, at] * jnp.exp(ldE[:, at])
            dSin[:, at] = mm(c_map, lifted, TN)
            maps[:, N:] = maps[:, N:] + mm(lifted, sin[:, at], NT)

        tiles(DI // 256, back_state)

        def relay_copy(chunk):
            at = lanes(chunk, CHUNK)
            return remote(
                dSin.at[:, at], dS.at[li, :, at], r_send.at[li, chunk], r_recv.at[li, chunk], place.dp, place.seq - 1
            )

        def relay(chunk):
            at = lanes(chunk, CHUNK)

            @pl.when(place.seq < n_seq - 1)
            def _():
                relay_copy(chunk).wait_recv()
                dSin[:, at] = dSin[:, at] + jnp.exp(ldE[T - 1 : T, at]) * dS[li, :, at]

            @pl.when(place.seq == n_seq - 1)
            def _():
                dS[li, :, at] = jnp.zeros((N, CHUNK), F32)

            @pl.when(place.seq > 0)
            def _():
                relay_copy(chunk).start()

        items = pairs + plan.gate_jobs
        relay_from = (n_seq - 1 - place.seq) * (items - chunks) // (n_seq - 1)
        nT[...] = (x[...] * inv_in).T
        NG[...] = jnp.zeros((T, D), F32)

        def back_gate(i, slot):
            NG[...] = NG[...] + mm(gate[:, lanes(i, CHUNK_N)], wcol[slot], NT)

        gate_stream = column_stream(wg_hbm, plan.gate_jobs, layer, back_gate)

        def gate_job(i):
            produce(first_job + plan.out_jobs + i, nT, 2 * h, lambda target: target * h, gate[:, lanes(i, CHUNK_N)])

        def diagonal(i):
            at = lanes(i, LANES)
            scaled = mixed[:, at] * dtE[:, at]
            out_grad = V[:, at]
            l_tile = ldE[:, at]
            parts = []
            for side in range(2):
                column = l_tile[:, side * PS : side * PS + 1]
                row = ldT[pl.ds(2 * i + side, 1), :]
                decay = jnp.exp(jnp.minimum(row - column, 0.0))
                own_lanes = lane_low if side == 0 else jnp.logical_not(lane_low)
                pairing = mm(jnp.where(own_lanes, scaled, 0.0), out_grad, NT)
                dgT[...] = dgT[...] + decay * pairing
                parts.append(mm(gmT[...] * decay, out_grad))
            U[:, at] = jnp.where(lane_low, parts[0], parts[1])

        def work_item(i):
            @pl.when(i < pairs)
            def _():
                diagonal(i)

            @pl.when(i >= pairs)
            def _():
                gate_stream(i - pairs)

            @pl.when(jnp.logical_and(i >= relay_from, i < relay_from + chunks))
            def _():
                relay(i - relay_from)

            number = i // 2 + 2

            @pl.when(jnp.logical_and(i % 2 == 1, number < plan.out_jobs))
            def _():
                out_piece(number)

            @pl.when(jnp.logical_and(i % 2 == 1, jnp.logical_and(number >= plan.out_jobs, number < plan.early)))
            def _():
                gate_job(number - plan.out_jobs)

            @pl.when(i % 2 == 1)
            def _():
                red.tick(base + plan.lead + number)

        tiles(items, work_item)
        mix_stream = column_stream(wm_hbm, plan.mix_jobs, layer, lambda i, slot: back_mix(i, slot))
        masked = jnp.where(ti <= tj, dgT[...], 0.0)
        maps[:, 0:N] = mm(masked, c_map)
        maps[:, N:] = maps[:, N:] + mm(masked, b_map, TN)
        heads[...] = jnp.zeros((2, T, LANES), F32)
        rows[...] = jnp.zeros((8, LANES), F32)

        groups = DI // CHUNK_N
        late = base + plan.lead + plan.early + plan.bubbles

        def conv_back(at, width, upstream):
            taps, total = conv_value(at)
            sig = sigmoid(total)
            pre = upstream * (sig * (1.0 + total * (1.0 - sig)))
            PG[0:T, at] = pre
            parts = [jnp.sum(pre * ext[8 - K + 1 + k : 8 - K + 1 + k + T, at], axis=0, keepdims=True) for k in range(K)]
            parts.append(jnp.sum(pre, axis=0, keepdims=True))
            parts.append(jnp.zeros((8 - K - 1, width), F32))
            convg[li, :, at] = jnp.concatenate(parts, axis=0)

        def edge_copy(number, at):
            return remote(
                PG.at[pl.ds(0, 8), at], edge_in.at[li, :, at], e_send.at[li, number], e_recv.at[li, number],
                place.dp, place.seq - 1,
            )

        def raw_back(number, at):
            @pl.when(place.seq < n_seq - 1)
            def _():
                edge_copy(number, at).wait_recv()
                PG[T : T + 8, at] = edge_in[li, :, at]

            taps = conv_ref[pl.ds(pl.multiple_of(layer * 8, 8), 8), at]
            total = taps[K - 1 : K, :] * PG[0:T, at]
            for k in range(K - 1):
                total = total + taps[k : k + 1, :] * PG[K - 1 - k : K - 1 - k + T, at]
            raw[:, at] = total

        def mix_piece(number):
            produce(
                first_job + plan.early + number, nT, 2 * h, lambda target: target * h, raw[:, lanes(number, CHUNK_N)]
            )
            red.tick(late + number)
            mix_stream(number)

        def back_mix(i, slot):
            NG[...] = NG[...] + mm(raw[:, lanes(i, CHUNK_N)], wcol[slot], NT)

        def back_group(g):
            at = lanes(g, CHUNK_N)
            select = head_matrix(LANES, CHUNK_N, PS, g * CHUNK_N)
            select32 = select.astype(F32)
            l_tile = ldE[:, at]
            heads_in = mixed[:, at]
            dt_tile = dtE[:, at]
            scaled = heads_in * dt_tile
            end_weight = jnp.exp(l_tile[T - 1 : T, :] - l_tile)
            skip = exact_right(head[2:3, :], select)
            out_grad = V[:, at]
            scaled_grad = U[:, at] + end_weight * mm(b_map, dS[li, :, at])
            maps[:, 0:N] = maps[:, 0:N] + mm(scaled * end_weight, dS[li, :, at], NT)
            decay = out_grad * (mo[:, at] - skip * heads_in) - scaled * scaled_grad
            heads[0] = heads[0] + mm(decay, select32, NT)
            heads[1] = heads[1] + mm(scaled_grad * heads_in, select32, NT)
            skip_sum = jnp.sum(out_grad * heads_in, axis=0, keepdims=True)
            end_sum = jnp.sum(dS[li, :, at] * sout[:, at], axis=0, keepdims=True)
            both = jnp.concatenate([skip_sum, end_sum, jnp.zeros((6, CHUNK_N), F32)], axis=0)
            rows[...] = rows[...] + mm(both, select32, NT)
            conv_back(at, CHUNK_N, skip * out_grad + scaled_grad * dt_tile)

            @pl.when(place.seq > 0)
            def _():
                edge_copy(g, at).start()

            @pl.when(g == 0)
            def _():
                red.tick(late - 1)

            @pl.when(g > 0)
            def _():
                raw_back(g - 1, lanes(g - 1, CHUNK_N))
                mix_piece(g - 1)

        tiles(groups, back_group)
        map_lanes = pl.ds(DI, CW - DI)
        conv_back(map_lanes, CW - DI, maps[...])

        @pl.when(place.seq > 0)
        def _():
            edge_copy(groups, map_lanes).start()

        last_row = iota((T, LANES), 0) == T - 1
        decay_grad = heads[0] + jnp.where(last_row, rows[1:2, :], 0.0)
        rate_grad = exact(tri(T).astype(jnp.bfloat16), decay_grad, TN)
        step_grad = heads[1] - jnp.exp(head[0:1, :]) * rate_grad
        raw[:, CW:CX] = step_grad * sigmoid(raw_step + head[1:2, :])
        convg[li, :, CW:CX] = jnp.where(iota((8, LANES), 0) == 0, rows[0:1, :], 0.0)

        @pl.when(li == 0)
        def _():
            for k in range(6):
                load_of(0, k).start()

        def last_pieces(g):
            @pl.when(g == groups - 1)
            def _():
                raw_back(g, lanes(groups - 1, CHUNK_N))

            @pl.when(g == groups)
            def _():
                raw_back(g, map_lanes)

            mix_piece(g)

        lax.fori_loop(groups - 1, groups + 1, lambda g, c: (last_pieces(g), c)[1], 0)
        inner = jnp.sum(NG[...] * x[...], axis=-1, keepdims=True) / D
        grad[...] = grad[...] + inv_in * NG[...] - x[...] * (inner * (inv_in * inv_in * inv_in))

        @pl.when(place.seq > 0)
        def _():
            tiles(groups, lambda g: edge_copy(g, lanes(g, CHUNK_N)).wait_send())
            edge_copy(groups, map_lanes).wait_send()
            tiles(chunks, lambda c: relay_copy(c).wait_send())

        return carry

    lax.fori_loop(0, 2, layer_body, 0)
    hg_ref[...] = grad[...]
    base = 2 * plan.slots
    for e in range(plan.conv_jobs):
        job = 2 * plan.per_layer + e
        for block in range(plan.blocks_per_job):
            number = e * plan.blocks_per_job + block
            at = pl.ds(block * 8, 8)
            for o in range(n_dp):
                if number < plan.blocks:
                    li, c = divmod(number, plan.mix_jobs)
                    value = convg[li, :, c * CHUNK_N : (c + 1) * CHUNK_N]
                else:
                    value = jnp.zeros((8, CHUNK_N), F32)
                S[job % plan.s_ring, o, at] = value
                O[job % plan.o_ring, o, at] = value
        red.tick(base + e)
    tiles(max(plan.offsets), lambda i: red.tick(base + plan.conv_jobs + i))

    copies = []
    for number, (sums, out) in enumerate(((norm_sum, norm_out), (gated_sum, gated_out))):
        local = pltpu.make_async_copy(sums, out.at[place.core], gain_sem.at[number])
        away = remote(sums, out.at[place.core], gain_sem.at[2 + number], gain_sem.at[4 + number], place.dp, place.sib)
        back = remote(sums, out.at[1 - place.core], gain_sem.at[2 + number], gain_sem.at[4 + number], place.dp, place.sib)
        local.start()
        away.start()
        copies.append((local, away, back))
    for local, away, back in copies:
        local.wait()
        away.wait_send()
        back.wait_recv()


def backward(cot, mask, conv, head, norm, gated, saved, n_dp, n_seq, dims):
    T, D, DI, CW, H, PS, N, K = dims
    plan = Plan(n_dp, n_seq, dims)
    any_spec = pl.BlockSpec(memory_space=pl.ANY)
    vmem = pl.BlockSpec(memory_space=pltpu.VMEM)
    CX = CW + LANES
    h, J, ring = plan.h, plan.jobs, plan.r_ring
    sd = lambda *s: jax.ShapeDtypeStruct(s, F32)
    v = lambda *s: pltpu.VMEM(s, F32)
    dma = pltpu.SemaphoreType.DMA
    if plan.wide:
        received = [v(ring, 2, h // 2, CHUNK_N), v(ring, 2, h // 2, CHUNK_N), v(ring, h // 2, CHUNK_N),
                    v(ring, h // 2, CHUNK_N), v(plan.z_ring, h, CHUNK_N), v(plan.half_ring, h // 2, CHUNK_N)]
    else:
        none = v(8, LANES)
        received = [v(ring, n_dp - 1, h, CHUNK_N), none, none, none, v(plan.z_ring, max(plan.rounds, 1), h, CHUNK_N), none]
    return pl.pallas_call(
        functools.partial(backward_kernel, n_dp, n_seq, dims),
        out_shape=(
            sd(T, D), sd(2, 2 * h, CW), sd(2, 2 * h, LANES), sd(2, 2 * h, DI), sd(2, 4 * h, D),
            sd(plan.conv_jobs, 2, h, CHUNK_N), sd(2, 2, h, LANES), sd(2, 2, 2 * h, LANES),
        ),
        in_specs=[vmem] * 6 + [any_spec] * 11,
        out_specs=(vmem,) + (any_spec,) * 7,
        scratch_shapes=[
            v(T, D), v(T, D), v(T, DI), v(T + 8, CW), v(T, LANES), v(T, DI), v(N, DI), v(N, DI),
            v(DI, D), v(3, D, CHUNK_N), v(T, DI), v(T, DI), v(T, CW), v(T, DI), v(T, DI), v(LANES, T), v(T, T),
            v(T, T), v(T + 8, CW), v(T, CX), v(D, T), v(DI, T), v(T, D), v(2, N, DI), v(N, DI), v(T, 2 * N),
            v(2, T, LANES), v(2, 8, CX), v(8, LANES),
            v(plan.s_ring, n_dp, h, CHUNK_N), v(plan.in_ring, n_dp, h, CHUNK_N), v(plan.o_ring, n_dp, h, CHUNK_N), *received,
            v(plan.f_ring, h, CHUNK_N), v(plan.f_ring, h, CHUNK_N) if plan.wide else v(8, LANES), v(2, 8, CW),
            v(plan.w_ring, h, CHUNK_N), v(2, h, LANES), v(2, 2 * h, LANES),
            dma((J, plan.kinds + 1)), dma((J, plan.kinds + 1)), dma((plan.s_ring,)), dma((2, plan.f_ring)), dma((plan.w_ring,)), dma((6,)), dma((8,)),
            dma((3,)), dma((2,)), dma((2, DI // CHUNK_N + 1)), dma((2, DI // CHUNK_N + 1)), dma((2, DI // 256)), dma((2, DI // 256)),
        ],
        compiler_params=pltpu.CompilerParams(
            collective_id=1, has_side_effects=True, vmem_limit_bytes=61 << 20
        ),
        name="backward",
    )(cot, mask, conv, head, norm, gated, *saved)


def on_device(hidden, cotangent, lengths, norm_gain, gate_weight, mix_weight, step_weight, conv_kernel, conv_bias,
              gated_gain, out_weight, skip_gain, log_rate, step_bias):
    n_dp, n_seq = lax.axis_size("dp"), lax.axis_size("seq")
    slots, T, D = hidden.shape
    DI, CW, H, K = gate_weight.shape[2], mix_weight.shape[2], skip_gain.shape[1], conv_kernel.shape[1]
    dims = (T, D, DI, CW, H, DI // H, (CW - DI) // 2, K)
    plan = Plan(n_dp, n_seq, dims)
    mask, conv, head, norm, gated, step_pad = prepare(
        hidden, lengths, norm_gain, gate_weight, mix_weight, step_weight, conv_kernel, conv_bias, gated_gain,
        out_weight, skip_gain, log_rate, step_bias, n_dp,
    )
    x = hidden[0]
    result, conv_full, *saved = forward(
        x, mask, conv, head, norm, gated, mix_weight, gate_weight, out_weight, step_pad, n_dp, n_seq, dims
    )
    hidden_grad, gm, gs, gg, go, gc, norm_sum, gated_sum = backward(
        cotangent[0], mask, conv_full, head, norm, gated, (x, *saved), n_dp, n_seq, dims
    )
    norm_gain_grad = jnp.sum(norm_sum, axis=-1).transpose(1, 0, 2).reshape(norm_gain.shape) / norm_gain
    gated_gain_grad = jnp.sum(gated_sum, axis=-1).transpose(1, 0, 2).reshape(gated_gain.shape) / gated_gain
    blocks = gc[:, 0].reshape(-1, 8, CHUNK_N)[: plan.blocks]
    blocks = blocks.reshape(2, plan.mix_jobs, 8, CHUNK_N).transpose(0, 2, 1, 3).reshape(2, 8, CW + LANES)[::-1]
    shard = conv_bias.shape[1]
    own = lax.dynamic_slice(blocks, (0, 0, lax.axis_index("dp") * shard), (2, 8, shard))
    skip_grad = blocks[:, 0, CW : CW + H]
    return (
        result[None], hidden_grad[None], norm_gain_grad, gg, gm, gs[:, :, :H], own[:, :K], own[:, K],
        gated_gain_grad, go, skip_grad,
    )


def solution(mesh):
    return jax.shard_map(
        on_device,
        mesh=mesh,
        in_specs=(
            P("dp", "seq", None), P("dp", "seq", None), P("dp"), P(None, "dp"), P(None, "dp", None),
            P(None, "dp", None), P(None, "dp", None), P(None, None, "dp"), P(None, "dp"), P(None, "dp"),
            P(None, "dp", None), P(), P(), P(),
        ),
        out_specs=(
            P("dp", "seq", None), P("dp", "seq", None), P(None, "dp"), P(None, "dp", None), P(None, "dp", None),
            P(None, "dp", None), P(None, None, "dp"), P(None, "dp"), P(None, "dp"), P(None, "dp", None), P(),
        ),
        check_vma=False,
    )
```

```python
import functools

import jax
import jax.numpy as jnp
from jax import lax
from jax.experimental import pallas as pl
from jax.experimental.pallas import tpu as pltpu
from jax.sharding import PartitionSpec as P

EPSILON = 1e-05
HIGH = lax.Precision.HIGH
MESH = pl.DeviceIdType.MESH
LANES = 128
F32 = jnp.float32


def mm(left, right, contract=((1,), (0,))):
    return lax.dot_general(left, right, (contract, ((), ())), precision=HIGH, preferred_element_type=F32)


NN = ((1,), (0,))
NT = ((1,), (1,))
TN = ((0,), (0,))


def split(value):
    high = value.astype(jnp.bfloat16)
    return high, (value - high.astype(F32)).astype(jnp.bfloat16)


def split3(value):
    first = value.astype(jnp.bfloat16)
    rest = value - first.astype(F32)
    second = rest.astype(jnp.bfloat16)
    third = (rest - second.astype(F32)).astype(jnp.bfloat16)
    return first, second, third


def exact(select, value, contract=((1,), (0,))):
    total = None
    for part in split3(value):
        term = lax.dot_general(select, part, (contract, ((), ())), preferred_element_type=F32)
        total = term if total is None else total + term
    return total


def exact_right(value, select, contract=((1,), (0,))):
    total = None
    for part in split3(value):
        term = lax.dot_general(part, select, (contract, ((), ())), preferred_element_type=F32)
        total = term if total is None else total + term
    return total


def iota(shape, axis):
    return lax.broadcasted_iota(jnp.int32, shape, axis)


def head_matrix(heads_padded, width, head_size, start=0):
    head = iota((heads_padded, width), 0)
    channel = iota((heads_padded, width), 1) + start
    inside = jnp.logical_and(channel >= head * head_size, channel < (head + 1) * head_size)
    return jnp.where(inside, 1.0, 0.0).astype(jnp.bfloat16)


def tri(size):
    return jnp.where(iota((size, size), 0) >= iota((size, size), 1), 1.0, 0.0)


def sigmoid(v):
    return jax.nn.sigmoid(v)


def softplus(v):
    return jnp.maximum(v, 0.0) + jnp.log1p(jnp.exp(-jnp.abs(v)))


def tiles(count, body):
    lax.fori_loop(0, count, lambda i, c: (body(i), c)[1], 0)


def lanes(i, width):
    return pl.ds(pl.multiple_of(i * width, width), width)


class Place:
    def __init__(self, dp_count, seq_count):
        self.n_dp, self.n_seq = dp_count, seq_count
        self.dp = lax.axis_index("dp")
        self.seq = lax.axis_index("seq")
        self.core = self.seq % 2
        self.z = self.seq // 2
        self.sib = self.z * 2 + (1 - self.core)
        self.parity = self.z % 2
        self.pair = (self.z + 1 - 2 * self.parity) * 2 + self.core
        y, x = self.dp // 2, self.dp % 2
        self.dpx = 2 * y + (1 - x)
        self.dpy = 2 * (1 - y) + x
        self.dpd = 2 * (1 - y) + (1 - x)


def remote(src, dst, send, recv, dp, seq):
    return pltpu.make_async_remote_copy(
        src_ref=src, dst_ref=dst, send_sem=send, recv_sem=recv, device_id=(dp, seq), device_id_type=MESH
    )


def entry_barrier(place):
    barrier = pltpu.get_barrier_semaphore()

    def greet(dp, seq):
        pl.semaphore_signal(barrier, inc=1, device_id=(dp, seq), device_id_type=MESH)

    for step in range(1, place.n_dp):
        greet((place.dp + step) % place.n_dp, place.seq)
    greet(place.dp, place.sib)
    greet(place.dp, place.pair)

    @pl.when(jnp.logical_and(place.core == 1, place.seq < place.n_seq - 1))
    def _():
        greet(place.dp, place.seq + 1)

    @pl.when(jnp.logical_and(place.core == 0, place.seq > 0))
    def _():
        greet(place.dp, place.seq - 1)

    outer = jnp.logical_or(place.seq == 0, place.seq == place.n_seq - 1)

    @pl.when(outer)
    def _():
        pl.semaphore_wait(barrier, place.n_dp + 1)

    @pl.when(jnp.logical_not(outer))
    def _():
        pl.semaphore_wait(barrier, place.n_dp + 2)


def full_barrier(place):
    barrier = pltpu.get_barrier_semaphore()
    for step in range(1, place.n_dp):
        peer = (place.dp + step) % place.n_dp
        pl.semaphore_signal(barrier, inc=1, device_id=(peer, place.seq), device_id_type=MESH)
    for step in range(1, place.n_seq):
        peer = (place.seq + step) % place.n_seq
        pl.semaphore_signal(barrier, inc=1, device_id=(place.dp, peer), device_id_type=MESH)
    pl.semaphore_wait(barrier, place.n_dp + place.n_seq - 2)


class Gather:
    def __init__(self, place, dest, stride, row_of, columns, half, sems, index):
        self.p, self.dest = place, dest
        self.stride, self.row_of, self.columns = stride, row_of, columns
        self.send, self.recv = sems
        self.index = index
        self.half = half
        self.third = half // 3
        self.wide = place.n_dp == 4 and half % 24 == 0 and place.n_seq % 4 == 0

    def at(self, owner, core, offset, count):
        start = owner * self.stride + self.row_of(core) + offset
        return self.dest.at[pl.ds(pl.multiple_of(start, 8), count), self.columns]

    def copy(self, kind, src, dst, dp, seq):
        return remote(src, dst, self.send.at[self.index, kind], self.recv.at[self.index, kind], dp, seq)

    def own_part(self, offset, count):
        return self.at(self.p.dp, self.p.core, offset, count)

    def scale(self, gain):
        for core in range(2):
            rows = self.at(self.p.dp, core, 0, self.half)
            start = self.row_of(core)
            if not isinstance(start, int):
                start = pl.multiple_of(start, 8)
            column = gain[pl.ds(start, self.half), :]
            rows[...] = rows[...] * jnp.concatenate([column] * (PIECE // LANES), axis=1)

    def get(self, kind):
        p, t = self.p, self.third
        if not self.wide:
            if kind < p.n_dp:
                peer = (p.dp + kind) % p.n_dp
                return self.copy(
                    kind, self.own_part(0, self.half), self.at(p.dp, p.core, 0, self.half), peer, p.seq
                )
            owner = (p.dp + 2 * p.n_dp - 1 - kind) % p.n_dp
            part = self.at(owner, p.core, 0, self.half)
            return self.copy(kind, part, part, p.dp, p.sib)
        first = p.parity * t
        only = 2 * t * p.parity
        miss = 2 * t * (1 - p.parity)
        if kind < 2:
            return self.copy(
                kind, self.own_part(first, 2 * t), self.at(p.dp, p.core, first, 2 * t),
                p.dpx if kind == 0 else p.dpy, p.seq,
            )
        owner, offset, count, dp, seq = {
            2: (p.dpx, first, t, p.dpy, p.seq),
            3: (p.dpy, first + t, t, p.dpx, p.seq),
            4: (p.dpx, only, t, p.dp, p.pair),
            5: (p.dpy, only, t, p.dp, p.pair),
            6: (p.dpd, only, t, p.dp, p.pair),
            7: (p.dpx, first, 2 * t, p.dp, p.sib),
            8: (p.dpy, first, 2 * t, p.dp, p.sib),
            9: (p.dpd, first, 2 * t, p.dp, p.sib),
            10: (p.dpx, miss, t, p.dp, p.sib),
            11: (p.dpy, miss, t, p.dp, p.sib),
            12: (p.dpd, miss, t, p.dp, p.sib),
        }[kind]
        part = self.at(owner, p.core, offset, count)
        return self.copy(kind, part, part, dp, seq)

    def stage(self, number):
        n = self.p.n_dp
        if not self.wide:
            if number == 0:
                for kind in range(1, n):
                    self.get(kind).start()
            elif number == 1:
                for kind in range(1, n):
                    self.get(kind).wait_recv()
                    self.get(n - 1 + kind).start()
            elif number == 4:
                for kind in range(n, 2 * n - 1):
                    self.get(kind).wait_recv()
            elif number == 5:
                for kind in range(1, 2 * n - 1):
                    self.get(kind).wait_send()
            return
        if number == 0:
            self.get(0).start()
            self.get(1).start()
        elif number == 1:
            self.get(0).wait_recv()
            for kind in (2, 4, 7):
                self.get(kind).start()
            self.get(1).wait_recv()
            for kind in (3, 5, 8):
                self.get(kind).start()
        elif number == 2:
            self.get(2).wait_recv()
            self.get(3).wait_recv()
            for kind in (6, 9):
                self.get(kind).start()
        elif number == 3:
            for kind in (4, 5, 6):
                self.get(kind).wait_recv()
                self.get(kind + 6).start()
        elif number == 4:
            for kind in range(7, 13):
                self.get(kind).wait_recv()
        else:
            for kind in range(13):
                self.get(kind).wait_send()


GATHER_OFFSETS = (0, 2, 4, 6, 7, 9)
PIECE = 384


def kinds_of(n_dp):
    return max(13, 2 * n_dp)


def forward_kernel(n_dp, n_seq, dims, *refs):
    (
        x_hbm, mask_ref, conv_ref, head_ref, norm_ref, gated_ref, wm_own, wg_own, wo_own, ws_own,
        result_ref, conv_full, xs_out, gate_out, ext_out, step_out, mo_out, sin_out, sout_out, wm_out, wg_out, wo_out, lde_out, dte_out, mixed_out, ldt_out,
        WM, WG, WO, xs, gate, ext, step, mo, sin, sout, conv_in, mixed, diag, ldE, dtE, ldT, gm,
        g_send, g_recv, g_local, c_send, c_recv, e_send, e_recv, r_send, r_recv, o_sem,
    ) = refs
    T, D, DI, CW, H, PS, N, K = dims
    layers = 2
    place = Place(n_dp, n_seq)
    h = D // n_dp // 2
    mix_pieces, gate_pieces, across = (CW + LANES) // PIECE, DI // PIECE, D // PIECE
    out_pieces = 2 * across
    per_layer = mix_pieces + gate_pieces + out_pieces
    early = mix_pieces + gate_pieces
    done_at = GATHER_OFFSETS[4]

    def tick(t):
        for number in reversed(range(len(GATHER_OFFSETS))):
            job = t - GATHER_OFFSETS[number]
            layer, q = job // per_layer, job % per_layer
            inside = jnp.logical_and(job >= 0, job < 2 * per_layer)

            def run(kind, dest, stride, row_of, column, number=number, job=job, layer=layer):
                piece = Gather(place, dest.at[layer], stride, row_of, lanes(column, PIECE), h, (g_send, g_recv), job)
                if number == 0:
                    first = job == layer * per_layer + (0, mix_pieces, early)[kind]

                    @pl.when(first)
                    def _():
                        own_copy(kind, layer).wait()
                        if kind == 0:
                            own_copy(3, layer).wait()

                    piece.scale((norm_ref, norm_ref, gated_ref)[kind].at[layer])
                piece.stage(number)

            @pl.when(jnp.logical_and(inside, q < mix_pieces))
            def _():
                run(0, WM, 2 * h, lambda core: core * h, q)

            @pl.when(jnp.logical_and(inside, jnp.logical_and(q >= mix_pieces, q < early)))
            def _():
                run(1, WG, 2 * h, lambda core: core * h, q - mix_pieces)

            @pl.when(jnp.logical_and(inside, q >= early))
            def _():
                part = (q - early) // across
                run(2, WO, 4 * h, lambda core: core * 2 * h + part * h, (q - early) % across)

    def own_copy(kind, layer):
        own, dest, start, count = (
            (wm_own, WM, 0, CW), (wg_own, WG, 0, DI), (wo_own, WO, 0, D), (ws_own, WM, CW, LANES)
        )[kind]
        rows = own.shape[1]
        at = pl.ds(pl.multiple_of(place.dp * rows, 8), rows)
        target = dest.at[layer, at, pl.ds(start, count)]
        return pltpu.make_async_copy(own.at[layer], target, g_local.at[layer * 4 + kind])

    for layer in range(layers):
        for kind in (0, 3, 1, 2):
            own_copy(kind, layer).start()
    first_in = pltpu.make_async_copy(x_hbm, xs.at[0], o_sem.at[0])
    first_in.start()
    ext[0, 0:8, :] = jnp.zeros((8, CW), F32)
    ext[1, 0:8, :] = jnp.zeros((8, CW), F32)
    entry_barrier(place)
    tick(0)
    def conv_copy(step_index):
        peer = (place.dp + step_index) % n_dp
        return remote(
            conv_ref, conv_in.at[place.dp], c_send.at[step_index - 1], c_recv.at[step_index - 1], peer, place.seq
        )

    for s in range(1, n_dp):
        conv_copy(s).start()
    conv_in[place.dp] = conv_ref[...]
    first_in.wait()
    tiles(done_at, lambda i: tick(i + 1))
    per_body = mix_pieces + 1 + (H // 2 + gate_pieces) // 3 + across
    ti, tj = iota((T, T), 0), iota((T, T), 1)
    lane_low = iota((T, LANES), 1) < PS
    CHUNK = 256
    chunks = DI // CHUNK

    def saved_copies(layer):
        saved = (
            (gate, gate_out), (ext, ext_out), (step, step_out), (mo, mo_out), (sin, sin_out), (sout, sout_out),
            (WM, wm_out), (WG, wg_out), (WO, wo_out), (ldE, lde_out), (dtE, dte_out), (mixed, mixed_out),
            (ldT, ldt_out),
        )
        return [
            functools.partial(
                lambda a, b, k: pltpu.make_async_copy(a.at[layer] if k < 9 else a, b.at[layer], o_sem.at[layer * 13 + k + 1]),
                a, b, k,
            )
            for k, (a, b) in enumerate(saved)
        ]

    def layer_body(layer, carry):
        x_all = xs[layer]
        inv = lax.rsqrt(jnp.mean(x_all * x_all, axis=-1, keepdims=True) + EPSILON)
        diag[:, 0:D] = x_all * inv
        head = head_ref[layer]
        base = done_at + 1 + layer * per_body
        def project_mix(i):
            ext[layer, 8 : T + 8, lanes(i, PIECE)] = mm(diag[:, 0:D], WM[layer, :, lanes(i, PIECE)])
            tick(base + i)

        tiles(mix_pieces - 1, project_mix)
        last = (mix_pieces - 1) * PIECE
        value = mm(diag[:, 0:D], WM[layer, :, last : last + PIECE])
        ext[layer, 8 : T + 8, last:CW] = value[:, 0 : CW - last]
        raw = value[:, CW - last :]
        edge = remote(
            ext.at[layer, pl.ds(T, 8)], ext.at[layer, pl.ds(0, 8)], e_send.at[layer], e_recv.at[layer],
            place.dp, place.seq + 1,
        )

        @pl.when(place.seq < n_seq - 1)
        def _():
            edge.start()

        step[layer] = raw

        @pl.when(layer > 0)
        def _():
            for copy in saved_copies(0)[9:]:
                copy().wait()

        tick(base + mix_pieces - 1)
        saved_copies(layer)[6]().start()
        dt = softplus(raw + head[1:2, :])
        rate = -jnp.exp(head[0:1, :]) * dt
        ld = exact(tri(T).astype(jnp.bfloat16), rate)
        ldT[...] = ld.T

        def expand(i):
            select = head_matrix(LANES, 256, PS, i * 256)
            ldE[:, lanes(i, 256)] = exact_right(ld, select)
            dtE[:, lanes(i, 256)] = exact_right(dt, select)

        tiles(DI // 256, expand)

        @pl.when(layer == 0)
        def _():
            for s in range(1, n_dp):
                conv_copy(s).wait_recv()

            def sum_taps(i):
                at = lanes(i, 256)
                taps = conv_in[0, :, at]
                for s in range(1, n_dp):
                    taps = taps + conv_in[s, :, at]
                conv_full[:, at] = taps

            tiles(CW // 256, sum_taps)

        @pl.when(place.seq > 0)
        def _():
            edge.wait_recv()

        def conv(i):
            at = lanes(i, 256)
            taps = conv_full[pl.ds(pl.multiple_of(layer * 8, 8), 8), at]
            total = taps[K : K + 1, :]
            for k in range(K):
                total = total + taps[k : k + 1, :] * ext[layer, 8 - K + 1 + k : 8 - K + 1 + k + T, at]
            mixed[:, at] = total * sigmoid(total)

        tiles(CW // 256, conv)
        tick(base + mix_pieces)
        b_map = mixed[:, DI : DI + N]
        c_map = mixed[:, DI + N : DI + 2 * N]
        gm[...] = jnp.where(ti >= tj, mm(c_map, b_map, NT), 0.0)

        def local_state(i):
            at = lanes(i, 256)
            l_tile = ldE[:, at]
            weighted = mixed[:, at] * dtE[:, at] * jnp.exp(l_tile[T - 1 : T, :] - l_tile)
            sout[layer, :, at] = mm(b_map, weighted, TN)

        tiles(DI // 256, local_state)

        for copy in saved_copies(layer)[9:]:
            copy().start()

        def relay_copy(chunk):
            at = lanes(chunk, CHUNK)
            return remote(
                sout.at[layer, :, at], sin.at[layer, :, at], r_send.at[layer, chunk], r_recv.at[layer, chunk],
                place.dp, place.seq + 1,
            )

        def relay(chunk):
            at = lanes(chunk, CHUNK)

            @pl.when(place.seq > 0)
            def _():
                relay_copy(chunk).wait_recv()
                total = jnp.exp(ldE[T - 1 : T, at])
                sout[layer, :, at] = sout[layer, :, at] + total * sin[layer, :, at]

            @pl.when(place.seq == 0)
            def _():
                sin[layer, :, at] = jnp.zeros((N, CHUNK), F32)

            @pl.when(place.seq < n_seq - 1)
            def _():
                relay_copy(chunk).start()

        pairs = H // 2

        items = pairs + gate_pieces
        relay_from = place.seq * (items - chunks) // (n_seq - 1)

        def diagonal(i):
            at = lanes(i, LANES)
            scaled = mixed[:, at] * dtE[:, at]
            l_tile = ldE[:, at]
            parts = []
            for side in range(2):
                column = l_tile[:, side * PS : side * PS + 1]
                row = ldT[pl.ds(2 * i + side, 1), :]
                weights = gm[...] * jnp.exp(jnp.minimum(column - row, 0.0))
                parts.append(mm(weights, scaled))
            diag[:, at] = jnp.where(lane_low, parts[0], parts[1])


        def gate_proj(i):
            at = lanes(i, PIECE)
            gate[layer, :, at] = mm(xs[layer] * inv, WG[layer, :, at])

        def work_item(i):
            @pl.when(i < pairs)
            def _():
                diagonal(i)

            @pl.when(i >= pairs)
            def _():
                gate_proj(i - pairs)

            @pl.when(jnp.logical_and(i >= relay_from, i < relay_from + chunks))
            def _():
                relay(i - relay_from)

            @pl.when(i % 3 == 2)
            def _():
                tick(base + mix_pieces + 1 + i // 3)

        tiles(items, work_item)
        saved_copies(layer)[7]().start()

        def skip_row(i):
            return exact_right(head[2:3, :], head_matrix(LANES, 256, PS, i * 256))

        def off(i):
            at = lanes(i, 256)
            lift = jnp.exp(ldE[:, at])
            out = diag[:, at] + lift * mm(c_map, sin[layer, :, at]) + skip_row(i) * mixed[:, at]
            mo[layer, :, at] = out

        tiles(DI // 256, off)

        def gating(i, squares):
            at = lanes(i, LANES)
            pre = gate[layer, :, at]
            gated = mo[layer, :, at] * (pre * sigmoid(pre))
            diag[:, at] = gated
            return squares + gated * gated

        squares = lax.fori_loop(0, DI // LANES, gating, jnp.zeros((T, LANES), F32))
        inv_out = lax.rsqrt(jnp.sum(squares, axis=-1, keepdims=True) / DI + EPSILON)
        tiles(across, lambda i: tick(base + mix_pieces + 1 + items // 3 + i))

        def project_out(i):
            at = lanes(i, PIECE)
            branch = mm(diag[...] * inv_out, WO[layer, :, at])
            nxt = xs[layer, :, at] + branch
            xs[layer + 1, :, at] = nxt

        tiles(across, project_out)
        for number, copy in enumerate(saved_copies(layer)):
            if number < 6 or number == 8:
                copy().start()
        @pl.when(place.seq < n_seq - 1)
        def _():
            edge.wait_send()
            tiles(chunks, lambda c: relay_copy(c).wait_send())

        return carry

    lax.fori_loop(0, layers, layer_body, 0)
    done = done_at + 1 + layers * per_body
    left = layers * per_layer + GATHER_OFFSETS[5] - done
    if left > 0:
        tiles(left, lambda i: tick(done + i))
    result_ref[...] = xs[layers] * mask_ref[...]
    last = pltpu.make_async_copy(xs.at[1], xs_out, o_sem.at[0])
    last.start()
    for s in range(1, n_dp):
        conv_copy(s).wait_send()
    for layer in range(layers):
        for number, copy in enumerate(saved_copies(layer)):
            if number < 9 or layer == layers - 1:
                copy().wait()
    last.wait()


def forward(x, mask, conv, head, norm, gated, wm, wg, wo, ws, n_dp, n_seq, dims):
    T, D, DI, CW, H, PS, N, K = dims
    any_spec = pl.BlockSpec(memory_space=pl.ANY)
    vmem = pl.BlockSpec(memory_space=pltpu.VMEM)
    CX = CW + LANES
    kinds = kinds_of(n_dp)
    PIECES = 2 * ((CW + LANES) // PIECE + DI // PIECE + 2 * (D // PIECE))
    sd = lambda *s: jax.ShapeDtypeStruct(s, F32)
    v = lambda *s: pltpu.VMEM(s, F32)
    dma = pltpu.SemaphoreType.DMA
    return pl.pallas_call(
        functools.partial(forward_kernel, n_dp, n_seq, dims),
        out_shape=(
            sd(T, D), sd(16, CW), sd(T, D), sd(2, T, DI), sd(2, T + 8, CW), sd(2, T, LANES), sd(2, T, DI), sd(2, N, DI),
            sd(2, N, DI), sd(2, D, CX), sd(2, D, DI), sd(2, DI, D), sd(2, T, DI), sd(2, T, DI), sd(2, T, CW), sd(2, LANES, T),
        ),
        in_specs=[any_spec] + [vmem] * 5 + [any_spec] * 4,
        out_specs=(vmem, vmem) + (any_spec,) * 14,
        scratch_shapes=[
            v(2, D, CX), v(2, D, DI), v(2, DI, D), v(3, T, D), v(2, T, DI), v(2, T + 8, CW), v(2, T, LANES),
            v(2, T, DI), v(2, N, DI), v(2, N, DI), v(n_dp, 16, CW), v(T, CW), v(T, DI), v(T, DI), v(T, DI),
            v(LANES, T), v(T, T),
            dma((PIECES, kinds)), dma((PIECES, kinds)), dma((8,)), dma((n_dp - 1,)), dma((n_dp - 1,)), dma((2,)), dma((2,)),
            dma((2, DI // 256)), dma((2, DI // 256)), dma((27,)),
        ],
        compiler_params=pltpu.CompilerParams(
            collective_id=0, has_side_effects=True, vmem_limit_bytes=61 << 20
        ),
        name="forward",
    )(x, mask, conv, head, norm, gated, wm, wg, wo, ws)


def prepare(hidden, lengths, norm_gain, gate_weight, mix_weight, step_weight, conv_kernel, conv_bias, gated_gain,
            out_weight, skip_gain, log_rate, step_bias, n_dp):
    T = hidden.shape[1]
    H = skip_gain.shape[1]
    shard = conv_bias.shape[1]
    CW = shard * n_dp
    position = lax.axis_index("seq") * T + lax.iota(jnp.int32, T)
    mask = (position < lengths[0]).astype(F32)[:, None]
    step_pad = jnp.pad(step_weight, ((0, 0), (0, 0), (0, LANES - H)))
    norm = jnp.broadcast_to(norm_gain[:, :, None], norm_gain.shape + (LANES,))
    gated = jnp.broadcast_to(gated_gain[:, :, None], gated_gain.shape + (LANES,))
    head = jnp.pad(jnp.stack([log_rate, step_bias, skip_gain], axis=1), ((0, 0), (0, 5), (0, LANES - H)))
    own = jnp.concatenate([conv_kernel, conv_bias[:, None, :]], axis=1)
    own = jnp.pad(own, ((0, 0), (0, 8 - own.shape[1]), (0, 0))).reshape(16, shard)
    conv = lax.dynamic_update_slice(jnp.zeros((16, CW), F32), own, (0, lax.axis_index("dp") * shard))
    return mask, conv, head, norm, gated, step_pad
CHUNK_N = 384


class Plan:
    def __init__(self, n_dp, n_seq, dims):
        T, D, DI, CW, H, PS, N, K = dims
        self.n_dp, self.n_seq = n_dp, n_seq
        self.n_z = n_seq // 2
        self.h = D // n_dp // 2
        self.out_jobs = 2 * (D // CHUNK_N)
        self.gate_jobs = DI // CHUNK_N
        self.mix_jobs = (CW + LANES) // CHUNK_N
        self.lead, self.bubbles = 2, 3
        self.per_layer = self.out_jobs + self.gate_jobs + self.mix_jobs
        self.early = self.out_jobs + self.gate_jobs
        self.slots = self.lead + self.per_layer + self.bubbles
        self.blocks = 2 * self.mix_jobs
        self.blocks_per_job = self.h // 8
        self.conv_jobs = -(-self.blocks // self.blocks_per_job)
        self.jobs = 2 * self.per_layer + self.conv_jobs
        self.total_slots = 2 * self.slots + self.conv_jobs
        self.wide = n_dp == 4 and self.n_z == 4 and self.h % 32 == 0
        self.rounds = self.n_z.bit_length() - 1
        self.offsets = (0, 1, 1, 4, 7, 10, 13, 16, 19, 20)
        self.o_ring = self.offsets[4] + 1
        self.f_ring = max(self.offsets) + 1
        self.r_ring = self.offsets[4] - self.offsets[2] + 2
        self.z_ring = self.offsets[8] - self.offsets[4] + 1
        self.half_ring = self.offsets[7] - self.offsets[5] + 2
        self.w_ring = self.offsets[8] - self.offsets[7] + 1
        self.s_ring = self.offsets[2] + 1
        self.in_ring = self.offsets[2] + 2
        self.kinds = 12 if self.wide else n_dp - 1 + self.rounds + 2
        self.sibling_kind = self.kinds - 1

    def job_of(self, slot):
        layer = slot // self.slots
        q = slot % self.slots - self.lead
        early = jnp.logical_and(q >= 0, q < self.early)
        late = q >= self.early + self.bubbles
        inside = jnp.logical_and(slot >= 0, slot < 2 * self.slots)
        valid = jnp.logical_and(inside, jnp.logical_or(early, late))
        job = layer * self.per_layer + q - jnp.where(early, 0, self.bubbles)
        conv = jnp.logical_and(slot >= 2 * self.slots, slot < self.total_slots)
        job = jnp.where(slot >= 2 * self.slots, 2 * self.per_layer + slot - 2 * self.slots, job)
        return jnp.logical_or(valid, conv), job


class Reducer:
    def __init__(self, place, plan, refs, outs):
        self.p, self.plan = place, plan
        self.S, self.O, self.R, self.rx, self.ry, self.r2x, self.r2y, self.z1, self.z2, self.G, self.F, self.W, self.gains, self.sums, self.weights, self.send, self.recv, self.loc, self.fin, self.wsem = refs
        self.outs = outs

    def copy(self, job, kind, src, dst, dp, seq):
        return remote(src, dst, self.send.at[job, kind], self.recv.at[job, kind], dp, seq)

    def own(self, job, owner, start, count):
        ring = lax.rem(job, self.plan.o_ring)
        if not isinstance(start, int):
            start = pl.multiple_of(start, 8)
        return self.O.at[ring, owner, pl.ds(start, count)]

    def mine(self, job, start, count):
        return self.own(job, self.p.dp, start, count)

    def summed(self, job, start, count):
        ring = lax.rem(job, self.plan.f_ring)
        if not isinstance(start, int):
            start = pl.multiple_of(start, 8)
        return self.G.at[ring, pl.ds(start, count)]

    def to_sibling(self, job):
        ring = lax.rem(job, self.plan.s_ring)
        kind = self.plan.kinds - 2
        into = lax.rem(job, self.plan.in_ring)
        return self.copy(job, kind, self.S.at[ring], self.R.at[into], self.p.dp, self.p.sib)

    def slot(self, job):
        return lax.rem(job, self.plan.r_ring)

    def z_slot(self, job):
        return lax.rem(job, self.plan.z_ring)

    def half_slot(self, job):
        return lax.rem(job, self.plan.half_ring)

    def xy(self, job, kind):
        p, half = self.p, self.plan.h // 2
        low, high = (0, half), (half, half)
        return {
            0: lambda: self.copy(job, 0, self.own(job, p.dpx, *low), self.rx.at[self.slot(job), 0], p.dpx, p.seq),
            1: lambda: self.copy(job, 1, self.own(job, p.dpd, *low), self.rx.at[self.slot(job), 1], p.dpx, p.seq),
            2: lambda: self.copy(job, 2, self.own(job, p.dpy, *high), self.ry.at[self.slot(job), 0], p.dpy, p.seq),
            3: lambda: self.copy(job, 3, self.own(job, p.dpd, *high), self.ry.at[self.slot(job), 1], p.dpy, p.seq),
            4: lambda: self.copy(job, 4, self.own(job, p.dpy, *low), self.r2y.at[self.slot(job)], p.dpy, p.seq),
            5: lambda: self.copy(job, 5, self.own(job, p.dpx, *high), self.r2x.at[self.slot(job)], p.dpx, p.seq),
        }[kind]()

    def keep(self):
        return (self.p.z - 1) * (self.plan.h // 2)

    def zed(self, job, kind):
        p, h = self.p, self.plan.h
        across = (self.plan.n_z - 1 - p.z) * 2 + p.core
        if kind == 6:
            return self.copy(job, 6, self.summed(job, 0, h), self.z1.at[self.z_slot(job)], p.dp, p.pair)
        if kind == 7:
            start = (2 - p.z) * (h // 2)
            return self.copy(job, 7, self.summed(job, start, h // 2), self.z2.at[self.half_slot(job)], p.dp, across)
        if kind == 8:
            part = self.whole(job, self.keep(), h // 2)
            return self.copy(job, 8, part, part, p.dp, across)
        part = self.whole(job, 0, h)
        return self.copy(job, 9, part, part, p.dp, p.pair)

    def inner(self):
        return jnp.logical_and(self.p.z > 0, self.p.z < self.plan.n_z - 1)

    def whole(self, job, start, count):
        ring = lax.rem(job, self.plan.f_ring)
        if not isinstance(start, int):
            start = pl.multiple_of(start, 8)
        return self.F.at[ring, pl.ds(start, count)]

    def direct(self, job, step):
        p, h = self.p, self.plan.h
        peer = lax.rem(p.dp + step, p.n_dp)
        return self.copy(job, step - 1, self.own(job, peer, 0, h), self.rx.at[self.slot(job), step - 1], peer, p.seq)

    def butterfly(self, job, rnd):
        p, h = self.p, self.plan.h
        bit = (p.z // (1 << rnd)) % 2
        peer = (p.z + (1 << rnd) - 2 * bit * (1 << rnd)) * 2 + p.core
        kind = p.n_dp - 1 + rnd
        return self.copy(job, kind, self.summed(job, 0, h), self.z1.at[self.z_slot(job), rnd], p.dp, peer)

    def add(self, dst, src):
        dst[...] = dst[...] + src[...]

    def stage(self, number, job):
        plan, p = self.plan, self.p
        h = plan.h
        half = h // 2
        if number == 0:
            self.to_sibling(job).start()
        elif number == 1:
            return
        elif number == 2:
            copy = self.to_sibling(job)
            copy.wait_recv()
            copy.wait_send()
            ring = lax.rem(job, plan.in_ring)
            o_ring = lax.rem(job, plan.o_ring)

            def add_owner(o):
                self.O[o_ring, o] = self.O[o_ring, o] + self.R[ring, o]

            tiles(plan.n_dp, add_owner)
            if plan.wide:
                for kind in range(4):
                    self.xy(job, kind).start()
            else:
                for step in range(1, plan.n_dp):
                    self.direct(job, step).start()
        elif number == 3:
            if plan.wide:
                for kind in range(4):
                    self.xy(job, kind).wait_recv()
                self.add(self.own(job, p.dpy, 0, half), self.rx.at[self.slot(job), 1])
                self.add(self.own(job, p.dpx, half, half), self.ry.at[self.slot(job), 1])
                self.add(self.mine(job, 0, half), self.rx.at[self.slot(job), 0])
                self.add(self.mine(job, half, half), self.ry.at[self.slot(job), 0])
                self.xy(job, 4).start()
                self.xy(job, 5).start()
            else:
                for step in range(1, plan.n_dp):
                    self.direct(job, step).wait_recv()
                    self.add(self.mine(job, 0, h), self.rx.at[self.slot(job), step - 1])
        elif number == 4:
            if plan.wide:
                self.xy(job, 4).wait_recv()
                self.summed(job, 0, half)[...] = self.mine(job, 0, half)[...] + self.r2y[self.slot(job)]
                self.xy(job, 5).wait_recv()
                self.summed(job, half, half)[...] = self.mine(job, half, half)[...] + self.r2x[self.slot(job)]

                @pl.when(jnp.logical_not(self.inner()))
                def _():
                    self.zed(job, 6).start()

                for kind in range(6):
                    self.xy(job, kind).wait_send()
            else:
                self.summed(job, 0, h)[...] = self.mine(job, 0, h)[...]
                for step in range(1, plan.n_dp):
                    self.direct(job, step).wait_send()
                if plan.rounds > 0:
                    self.butterfly(job, 0).start()
        elif number == 5:
            if plan.wide:

                @pl.when(self.inner())
                def _():
                    self.zed(job, 6).wait_recv()
                    self.add(self.summed(job, 0, h), self.z1.at[self.z_slot(job)])
                    self.zed(job, 7).start()

            else:
                self.exchange(job, 0)
        elif number == 6:
            if plan.wide:

                @pl.when(self.inner())
                def _():
                    self.zed(job, 7).wait_recv()
                    part = self.summed(job, self.keep(), half)[...] + self.z2[self.half_slot(job)]
                    self.whole(job, self.keep(), half)[...] = part
                    self.zed(job, 8).start()

            else:
                self.exchange(job, 1)
        elif number == 7:
            self.weight(job, "start")
            if plan.wide:

                @pl.when(self.inner())
                def _():
                    self.zed(job, 8).wait_recv()
                    self.zed(job, 9).start()

        elif number == 8:
            if plan.wide:

                @pl.when(self.inner())
                def _():
                    for kind in (7, 8, 9):
                        self.zed(job, kind).wait_send()

                @pl.when(jnp.logical_not(self.inner()))
                def _():
                    self.zed(job, 9).wait_recv()
                    self.zed(job, 6).wait_send()

            else:
                for rnd in range(2, max(plan.rounds, 3)):
                    self.exchange(job, rnd)
            self.scale(job)
            self.final(job, "start")
        else:
            self.final(job, "wait")

    def exchange(self, job, rnd):
        if rnd >= self.plan.rounds:
            return
        copy = self.butterfly(job, rnd)
        copy.wait_recv()
        copy.wait_send()
        self.add(self.summed(job, 0, self.plan.h), self.z1.at[self.z_slot(job), rnd])
        if rnd + 1 < self.plan.rounds:
            self.butterfly(job, rnd + 1).start()

    def kind_of(self, job):
        plan = self.plan
        second = job >= plan.per_layer
        q = job - jnp.where(second, plan.per_layer, 0)
        normal = job < 2 * plan.per_layer
        layer = jnp.where(second, 0, 1)
        is_out = jnp.logical_and(normal, q < plan.out_jobs)
        is_gate = jnp.logical_and(normal, jnp.logical_and(q >= plan.out_jobs, q < plan.early))
        is_mix = jnp.logical_and(normal, q >= plan.early)
        return layer, q, normal, is_out, is_gate, is_mix

    def total(self, job):
        return self.whole(job, 0, self.plan.h) if self.plan.wide else self.summed(job, 0, self.plan.h)

    def weight(self, job, what):
        plan, p = self.plan, self.p
        h = plan.h
        layer, q, normal, is_out, is_gate, is_mix = self.kind_of(job)
        wm, wg, wo = self.weights
        slot = lax.rem(job, plan.w_ring)
        per_row = plan.out_jobs // 2

        def go_for(source, row, column):
            at = (layer, pl.ds(pl.multiple_of(row, 8), h), lanes(column, CHUNK_N))
            copy = pltpu.make_async_copy(source.at[at], self.W.at[slot], self.wsem.at[slot])
            getattr(copy, what)()

        pl.when(is_out)(
            lambda: go_for(wo, p.dp * 4 * h + p.core * 2 * h + (q // per_row) * h, lax.rem(q, per_row))
        )
        pl.when(is_gate)(lambda: go_for(wg, p.dp * 2 * h + p.core * h, q - plan.out_jobs))
        pl.when(is_mix)(lambda: go_for(wm, p.dp * 2 * h + p.core * h, q - plan.early))

    def scale(self, job):
        plan, p = self.plan, self.p
        h = plan.h
        layer, q, normal, is_out, is_gate, is_mix = self.kind_of(job)
        norm, gated = self.gains
        norm_sum, gated_sum = self.sums
        slot = lax.rem(job, plan.w_ring)
        total = self.total(job)
        self.weight(job, "wait")

        def apply(sums, gain):
            value = total[...]
            product = value * self.W[slot]
            lane_sum = product[:, 0:LANES]
            for part in range(1, CHUNK_N // LANES):
                lane_sum = lane_sum + product[:, part * LANES : (part + 1) * LANES]
            sums[...] = sums[...] + lane_sum
            total[...] = value * jnp.concatenate([gain[...]] * (CHUNK_N // LANES), axis=1)

        @pl.when(is_out)
        def _():
            part = q // (plan.out_jobs // 2)
            rows = pl.ds(pl.multiple_of(p.core * 2 * h + part * h, 8), h)
            apply(gated_sum.at[layer, pl.ds(pl.multiple_of(part * h, 8), h)], gated.at[layer, rows])

        @pl.when(jnp.logical_or(is_gate, is_mix))
        def _():
            apply(norm_sum.at[layer], norm.at[layer, pl.ds(pl.multiple_of(p.core * h, 8), h)])

    def final(self, job, what):
        plan, p = self.plan, self.p
        h = plan.h
        gm, gs, gg, go, gc = self.outs
        layer, q, normal, is_out, is_gate, is_mix = self.kind_of(job)
        src = self.total(job)
        per_row = plan.out_jobs // 2
        last = plan.mix_jobs - 1
        edge = gm.shape[2] - last * CHUNK_N
        ring = lax.rem(job, plan.f_ring)
        extra = plan.kinds

        def rows(start):
            return pl.ds(pl.multiple_of(start, 8), h)

        def put(core):
            at = rows(core * h)
            return (
                (is_out, lambda: [(None, go.at[layer, rows(core * 2 * h + (q // per_row) * h), lanes(lax.rem(q, per_row), CHUNK_N)])]),
                (is_gate, lambda: [(None, gg.at[layer, at, lanes(q - plan.out_jobs, CHUNK_N)])]),
                (
                    jnp.logical_and(is_mix, q - plan.early < last),
                    lambda: [(None, gm.at[layer, at, lanes(q - plan.early, CHUNK_N)])],
                ),
                (
                    jnp.logical_and(is_mix, q - plan.early == last),
                    lambda: [
                        ((0, edge), gm.at[layer, at, pl.ds(last * CHUNK_N, edge)]),
                        ((edge, CHUNK_N - edge), gs.at[layer, at]),
                    ],
                ),
                (jnp.logical_not(normal), lambda: [(None, gc.at[job - 2 * plan.per_layer, core])]),
            )

        def go_for(make, which):
            for number, (columns, target) in enumerate(make()):
                part = src if columns is None else src.at[:, pl.ds(*columns)]
                kind = plan.sibling_kind if number == 0 else extra
                local = pltpu.make_async_copy(part, target, self.fin.at[number, ring])
                away = self.copy(job, kind, part, target, p.dp, p.sib)
                if which == "start":
                    local.start()
                    away.start()
                elif which == "wait":
                    local.wait()
                    away.wait_send()
                else:
                    away.wait_recv()

        for when, make in put(p.core):
            pl.when(when)(functools.partial(go_for, make, what))
        if what == "wait":
            for when, make in put(1 - p.core):
                pl.when(when)(functools.partial(go_for, make, "arrived"))

    def tick(self, t):
        for number in reversed(range(len(self.plan.offsets))):
            valid, job = self.plan.job_of(t - self.plan.offsets[number])

            @pl.when(valid)
            def _():
                self.stage(number, job)


def backward_kernel(n_dp, n_seq, dims, *refs):
    T, D, DI, CW, H, PS, N, K = dims
    plan = Plan(n_dp, n_seq, dims)
    (
        cot_ref, mask_ref, conv_ref, head_ref, norm_ref, gated_ref, x0_hbm, x1_hbm, gate_hbm, ext_hbm, step_hbm, mo_hbm, sin_hbm,
        sout_hbm, wm_hbm, wg_hbm, wo_hbm, lde_hbm, dte_hbm, mixed_hbm, ldt_hbm,
        hg_ref, gm, gs, gg, go, gc, norm_out, gated_out,
        grad, x, gate, ext, step, mo, sin, sout, wrow, wcol, U, V, mixed, ldE, dtE, ldT, gmT, dgT, PG, raw, nT, gnT,
        NG, dS, dSin, maps, heads, convg, rows,
        S, R, O, rx, ry, r2x, r2y, z1, z2, G, F, edge_in, W, norm_sum, gated_sum,
        j_send, j_recv, s_loc, f_loc, wt_sem, gain_sem, l_sem, w_sem, v_sem, e_send, e_recv, r_send, r_recv,
    ) = refs
    place = Place(n_dp, n_seq)
    h = plan.h
    red = Reducer(
        place,
        plan,
        (
            S, O, R, rx, ry, r2x, r2y, z1, z2, G, F, W, (norm_ref, gated_ref), (norm_sum, gated_sum),
            (wm_hbm, wg_hbm, wo_hbm), j_send, j_recv, s_loc, f_loc, wt_sem,
        ),
        (gm, gs, gg, go, gc),
    )
    norm_sum[...] = jnp.zeros(norm_sum.shape, F32)
    gated_sum[...] = jnp.zeros(gated_sum.shape, F32)
    CX = CW + LANES
    CHUNK = 256
    chunks = DI // CHUNK
    pairs = H // 2

    def load_of(layer, k):
        source, target = (
            (mo_hbm, mo), (gate_hbm, gate), (step_hbm, step), (ext_hbm, ext), (sin_hbm, sin), (sout_hbm, sout),
            (wo_hbm, wrow), (lde_hbm, ldE), (dte_hbm, dtE), (mixed_hbm, mixed), (ldt_hbm, ldT),
        )[k]
        return pltpu.make_async_copy(source.at[layer], target, l_sem.at[k])

    class Load:
        def __init__(self, layer, k):
            self.layer, self.k = layer, k

        def wait(self):
            load_of(self.layer, self.k).wait()

    for k in (1, 0, 6, 7, 8, 9, 10, 2, 3, 4, 5):
        load_of(1, k).start()

    def load_x(layer_value, action):
        @pl.when(layer_value == 1)
        def _():
            getattr(pltpu.make_async_copy(x1_hbm, x, l_sem.at[11]), action)()

        @pl.when(layer_value == 0)
        def _():
            getattr(pltpu.make_async_copy(x0_hbm, x, l_sem.at[11]), action)()

    grad[...] = cot_ref[...] * mask_ref[...]
    PG[T : T + 8, :] = jnp.zeros((8, CW), F32)
    full_barrier(place)
    ti, tj = iota((T, T), 0), iota((T, T), 1)
    lane_low = iota((T, LANES), 1) < PS

    def produce(job, lhs, stride, offset_of, rhs):
        ring_s = lax.rem(job, plan.s_ring)
        ring_o = lax.rem(job, plan.o_ring)
        for target, buffer, ring in ((1 - place.core, S, ring_s), (place.core, O, ring_o)):
            left = jnp.concatenate(
                [lhs[pl.ds(pl.multiple_of(o * stride + offset_of(target), 8), h), :] for o in range(n_dp)], axis=0
            )
            result = mm(left, rhs)
            for o in range(n_dp):
                buffer[ring, o] = result[o * h : (o + 1) * h]

    def column_stream(hbm, count, layer, body):
        def fetch(i, slot):
            return pltpu.make_async_copy(hbm.at[layer, :, lanes(i, CHUNK_N)], wcol.at[slot], w_sem.at[slot])

        fetch(0, 0).start()
        fetch(1, 1).start()

        def run(i):
            slot = lax.rem(i, 3)
            fetch(i, slot).wait()

            @pl.when(i + 2 < count)
            def _():
                fetch(i + 2, lax.rem(i + 2, 3)).start()

            body(i, slot)

        return run

    def layer_body(li, carry):
        layer = 1 - li
        base = li * plan.slots
        first_job = li * plan.per_layer
        head = head_ref[layer]
        loads = [Load(layer, k) for k in range(11)]
        load_x(layer, "start")

        loads[0].wait()
        loads[1].wait()

        def regate(i, squares):
            at = lanes(i, LANES)
            pre = gate[:, at]
            gated = mo[:, at] * (pre * sigmoid(pre))
            U[:, at] = gated
            return squares + gated * gated

        squares = lax.fori_loop(0, DI // LANES, regate, jnp.zeros((T, LANES), F32))
        inv_out = lax.rsqrt(jnp.sum(squares, axis=-1, keepdims=True) / DI + EPSILON)
        red.tick(base)
        loads[6].wait()

        def back_out(i, sums):
            at = lanes(i, 256)
            q = mm(grad[...], wrow[at, :], NT)
            V[:, at] = q
            gated = U[:, at]
            gnT[at, :] = (gated * inv_out).T
            product = q * gated
            return sums + product[:, 0:LANES] + product[:, LANES:256]

        sums = lax.fori_loop(0, DI // 256, back_out, jnp.zeros((T, LANES), F32))
        pull = jnp.sum(sums, axis=-1, keepdims=True) / DI * (inv_out * inv_out * inv_out)

        red.tick(base + 1)

        @pl.when(li == 0)
        def _():
            load_of(0, 6).start()

        def out_piece(i):
            per_row = plan.out_jobs // 2
            part = i // per_row
            rhs = grad[:, lanes(i % per_row, CHUNK_N)]
            produce(first_job + i, gnT, 4 * h, lambda target: target * 2 * h + part * h, rhs)

        def out_job(i):
            out_piece(i)
            red.tick(base + plan.lead + i)

        def degate(i):
            at = lanes(i, LANES)
            pre = gate[:, at]
            sig = sigmoid(pre)
            gated_grad = inv_out * V[:, at] - U[:, at] * pull
            gate[:, at] = gated_grad * mo[:, at] * (sig * (1.0 + pre * (1.0 - sig)))
            V[:, at] = gated_grad * (pre * sig)

        tiles(DI // LANES, degate)
        out_job(0)
        load_x(layer, "wait")
        inv_in = lax.rsqrt(jnp.mean(x[...] * x[...], axis=-1, keepdims=True) + EPSILON)
        for copy in loads[2:6] + loads[7:]:
            copy.wait()
        raw_step = step[...]
        def conv_value(at):
            taps = conv_ref[pl.ds(pl.multiple_of(layer * 8, 8), 8), at]
            total = taps[K : K + 1, :]
            for k in range(K):
                total = total + taps[k : k + 1, :] * ext[8 - K + 1 + k : 8 - K + 1 + k + T, at]
            return taps, total

        out_job(1)
        b_map = mixed[:, DI : DI + N]
        c_map = mixed[:, DI + N : DI + 2 * N]
        gmT[...] = jnp.where(ti <= tj, mm(b_map, c_map, NT), 0.0)
        dgT[...] = jnp.zeros((T, T), F32)
        maps[...] = jnp.zeros((T, 2 * N), F32)

        def back_state(i):
            at = lanes(i, 256)
            lifted = V[:, at] * jnp.exp(ldE[:, at])
            dSin[:, at] = mm(c_map, lifted, TN)
            maps[:, N:] = maps[:, N:] + mm(lifted, sin[:, at], NT)

        tiles(DI // 256, back_state)

        def relay_copy(chunk):
            at = lanes(chunk, CHUNK)
            return remote(
                dSin.at[:, at], dS.at[li, :, at], r_send.at[li, chunk], r_recv.at[li, chunk], place.dp, place.seq - 1
            )

        def relay(chunk):
            at = lanes(chunk, CHUNK)

            @pl.when(place.seq < n_seq - 1)
            def _():
                relay_copy(chunk).wait_recv()
                dSin[:, at] = dSin[:, at] + jnp.exp(ldE[T - 1 : T, at]) * dS[li, :, at]

            @pl.when(place.seq == n_seq - 1)
            def _():
                dS[li, :, at] = jnp.zeros((N, CHUNK), F32)

            @pl.when(place.seq > 0)
            def _():
                relay_copy(chunk).start()

        items = pairs + plan.gate_jobs
        relay_from = (n_seq - 1 - place.seq) * (items - chunks) // (n_seq - 1)
        nT[...] = (x[...] * inv_in).T
        NG[...] = jnp.zeros((T, D), F32)

        def back_gate(i, slot):
            NG[...] = NG[...] + mm(gate[:, lanes(i, CHUNK_N)], wcol[slot], NT)

        gate_stream = column_stream(wg_hbm, plan.gate_jobs, layer, back_gate)

        def gate_job(i):
            produce(first_job + plan.out_jobs + i, nT, 2 * h, lambda target: target * h, gate[:, lanes(i, CHUNK_N)])

        def diagonal(i):
            at = lanes(i, LANES)
            scaled = mixed[:, at] * dtE[:, at]
            out_grad = V[:, at]
            l_tile = ldE[:, at]
            parts = []
            for side in range(2):
                column = l_tile[:, side * PS : side * PS + 1]
                row = ldT[pl.ds(2 * i + side, 1), :]
                decay = jnp.exp(jnp.minimum(row - column, 0.0))
                own_lanes = lane_low if side == 0 else jnp.logical_not(lane_low)
                pairing = mm(jnp.where(own_lanes, scaled, 0.0), out_grad, NT)
                dgT[...] = dgT[...] + decay * pairing
                parts.append(mm(gmT[...] * decay, out_grad))
            U[:, at] = jnp.where(lane_low, parts[0], parts[1])

        def work_item(i):
            @pl.when(i < pairs)
            def _():
                diagonal(i)

            @pl.when(i >= pairs)
            def _():
                gate_stream(i - pairs)

            @pl.when(jnp.logical_and(i >= relay_from, i < relay_from + chunks))
            def _():
                relay(i - relay_from)

            number = i // 2 + 2

            @pl.when(jnp.logical_and(i % 2 == 1, number < plan.out_jobs))
            def _():
                out_piece(number)

            @pl.when(jnp.logical_and(i % 2 == 1, jnp.logical_and(number >= plan.out_jobs, number < plan.early)))
            def _():
                gate_job(number - plan.out_jobs)

            @pl.when(i % 2 == 1)
            def _():
                red.tick(base + plan.lead + number)

        tiles(items, work_item)
        mix_stream = column_stream(wm_hbm, plan.mix_jobs, layer, lambda i, slot: back_mix(i, slot))
        masked = jnp.where(ti <= tj, dgT[...], 0.0)
        maps[:, 0:N] = mm(masked, c_map)
        maps[:, N:] = maps[:, N:] + mm(masked, b_map, TN)
        heads[...] = jnp.zeros((2, T, LANES), F32)
        rows[...] = jnp.zeros((8, LANES), F32)

        groups = DI // CHUNK_N
        late = base + plan.lead + plan.early + plan.bubbles

        def conv_back(at, width, upstream):
            taps, total = conv_value(at)
            sig = sigmoid(total)
            pre = upstream * (sig * (1.0 + total * (1.0 - sig)))
            PG[0:T, at] = pre
            parts = [jnp.sum(pre * ext[8 - K + 1 + k : 8 - K + 1 + k + T, at], axis=0, keepdims=True) for k in range(K)]
            parts.append(jnp.sum(pre, axis=0, keepdims=True))
            parts.append(jnp.zeros((8 - K - 1, width), F32))
            convg[li, :, at] = jnp.concatenate(parts, axis=0)

        def edge_copy(number, at):
            return remote(
                PG.at[pl.ds(0, 8), at], edge_in.at[li, :, at], e_send.at[li, number], e_recv.at[li, number],
                place.dp, place.seq - 1,
            )

        def raw_back(number, at):
            @pl.when(place.seq < n_seq - 1)
            def _():
                edge_copy(number, at).wait_recv()
                PG[T : T + 8, at] = edge_in[li, :, at]

            taps = conv_ref[pl.ds(pl.multiple_of(layer * 8, 8), 8), at]
            total = taps[K - 1 : K, :] * PG[0:T, at]
            for k in range(K - 1):
                total = total + taps[k : k + 1, :] * PG[K - 1 - k : K - 1 - k + T, at]
            raw[:, at] = total

        def mix_piece(number):
            produce(
                first_job + plan.early + number, nT, 2 * h, lambda target: target * h, raw[:, lanes(number, CHUNK_N)]
            )
            red.tick(late + number)
            mix_stream(number)

        def back_mix(i, slot):
            NG[...] = NG[...] + mm(raw[:, lanes(i, CHUNK_N)], wcol[slot], NT)

        def back_group(g):
            at = lanes(g, CHUNK_N)
            select = head_matrix(LANES, CHUNK_N, PS, g * CHUNK_N)
            select32 = select.astype(F32)
            l_tile = ldE[:, at]
            heads_in = mixed[:, at]
            dt_tile = dtE[:, at]
            scaled = heads_in * dt_tile
            end_weight = jnp.exp(l_tile[T - 1 : T, :] - l_tile)
            skip = exact_right(head[2:3, :], select)
            out_grad = V[:, at]
            scaled_grad = U[:, at] + end_weight * mm(b_map, dS[li, :, at])
            maps[:, 0:N] = maps[:, 0:N] + mm(scaled * end_weight, dS[li, :, at], NT)
            decay = out_grad * (mo[:, at] - skip * heads_in) - scaled * scaled_grad
            heads[0] = heads[0] + mm(decay, select32, NT)
            heads[1] = heads[1] + mm(scaled_grad * heads_in, select32, NT)
            skip_sum = jnp.sum(out_grad * heads_in, axis=0, keepdims=True)
            end_sum = jnp.sum(dS[li, :, at] * sout[:, at], axis=0, keepdims=True)
            both = jnp.concatenate([skip_sum, end_sum, jnp.zeros((6, CHUNK_N), F32)], axis=0)
            rows[...] = rows[...] + mm(both, select32, NT)
            conv_back(at, CHUNK_N, skip * out_grad + scaled_grad * dt_tile)

            @pl.when(place.seq > 0)
            def _():
                edge_copy(g, at).start()

            @pl.when(g == 0)
            def _():
                red.tick(late - 1)

            @pl.when(g > 0)
            def _():
                raw_back(g - 1, lanes(g - 1, CHUNK_N))
                mix_piece(g - 1)

        tiles(groups, back_group)
        map_lanes = pl.ds(DI, CW - DI)
        conv_back(map_lanes, CW - DI, maps[...])

        @pl.when(place.seq > 0)
        def _():
            edge_copy(groups, map_lanes).start()

        last_row = iota((T, LANES), 0) == T - 1
        decay_grad = heads[0] + jnp.where(last_row, rows[1:2, :], 0.0)
        rate_grad = exact(tri(T).astype(jnp.bfloat16), decay_grad, TN)
        step_grad = heads[1] - jnp.exp(head[0:1, :]) * rate_grad
        raw[:, CW:CX] = step_grad * sigmoid(raw_step + head[1:2, :])
        convg[li, :, CW:CX] = jnp.where(iota((8, LANES), 0) == 0, rows[0:1, :], 0.0)

        @pl.when(li == 0)
        def _():
            for k in (1, 0, 7, 8, 9, 10, 2, 3, 4, 5):
                load_of(0, k).start()

        def last_pieces(g):
            @pl.when(g == groups - 1)
            def _():
                raw_back(g, lanes(groups - 1, CHUNK_N))

            @pl.when(g == groups)
            def _():
                raw_back(g, map_lanes)

            mix_piece(g)

        lax.fori_loop(groups - 1, groups + 1, lambda g, c: (last_pieces(g), c)[1], 0)
        inner = jnp.sum(NG[...] * x[...], axis=-1, keepdims=True) / D
        grad[...] = grad[...] + inv_in * NG[...] - x[...] * (inner * (inv_in * inv_in * inv_in))

        @pl.when(place.seq > 0)
        def _():
            tiles(groups, lambda g: edge_copy(g, lanes(g, CHUNK_N)).wait_send())
            edge_copy(groups, map_lanes).wait_send()
            tiles(chunks, lambda c: relay_copy(c).wait_send())

        return carry

    lax.fori_loop(0, 2, layer_body, 0)
    hg_ref[...] = grad[...]
    base = 2 * plan.slots
    for e in range(plan.conv_jobs):
        job = 2 * plan.per_layer + e
        for block in range(plan.blocks_per_job):
            number = e * plan.blocks_per_job + block
            at = pl.ds(block * 8, 8)
            for o in range(n_dp):
                if number < plan.blocks:
                    li, c = divmod(number, plan.mix_jobs)
                    value = convg[li, :, c * CHUNK_N : (c + 1) * CHUNK_N]
                else:
                    value = jnp.zeros((8, CHUNK_N), F32)
                S[job % plan.s_ring, o, at] = value
                O[job % plan.o_ring, o, at] = value
        red.tick(base + e)
    tiles(max(plan.offsets), lambda i: red.tick(base + plan.conv_jobs + i))

    copies = []
    for number, (sums, out) in enumerate(((norm_sum, norm_out), (gated_sum, gated_out))):
        local = pltpu.make_async_copy(sums, out.at[place.core], gain_sem.at[number])
        away = remote(sums, out.at[place.core], gain_sem.at[2 + number], gain_sem.at[4 + number], place.dp, place.sib)
        back = remote(sums, out.at[1 - place.core], gain_sem.at[2 + number], gain_sem.at[4 + number], place.dp, place.sib)
        local.start()
        away.start()
        copies.append((local, away, back))
    for local, away, back in copies:
        local.wait()
        away.wait_send()
        back.wait_recv()


def backward(cot, mask, conv, head, norm, gated, saved, n_dp, n_seq, dims):
    T, D, DI, CW, H, PS, N, K = dims
    plan = Plan(n_dp, n_seq, dims)
    any_spec = pl.BlockSpec(memory_space=pl.ANY)
    vmem = pl.BlockSpec(memory_space=pltpu.VMEM)
    CX = CW + LANES
    h, J, ring = plan.h, plan.jobs, plan.r_ring
    sd = lambda *s: jax.ShapeDtypeStruct(s, F32)
    v = lambda *s: pltpu.VMEM(s, F32)
    dma = pltpu.SemaphoreType.DMA
    if plan.wide:
        received = [v(ring, 2, h // 2, CHUNK_N), v(ring, 2, h // 2, CHUNK_N), v(ring, h // 2, CHUNK_N),
                    v(ring, h // 2, CHUNK_N), v(plan.z_ring, h, CHUNK_N), v(plan.half_ring, h // 2, CHUNK_N)]
    else:
        none = v(8, LANES)
        received = [v(ring, n_dp - 1, h, CHUNK_N), none, none, none, v(plan.z_ring, max(plan.rounds, 1), h, CHUNK_N), none]
    return pl.pallas_call(
        functools.partial(backward_kernel, n_dp, n_seq, dims),
        out_shape=(
            sd(T, D), sd(2, 2 * h, CW), sd(2, 2 * h, LANES), sd(2, 2 * h, DI), sd(2, 4 * h, D),
            sd(plan.conv_jobs, 2, h, CHUNK_N), sd(2, 2, h, LANES), sd(2, 2, 2 * h, LANES),
        ),
        in_specs=[vmem] * 6 + [any_spec] * 15,
        out_specs=(vmem,) + (any_spec,) * 7,
        scratch_shapes=[
            v(T, D), v(T, D), v(T, DI), v(T + 8, CW), v(T, LANES), v(T, DI), v(N, DI), v(N, DI),
            v(DI, D), v(3, D, CHUNK_N), v(T, DI), v(T, DI), v(T, CW), v(T, DI), v(T, DI), v(LANES, T), v(T, T),
            v(T, T), v(T + 8, CW), v(T, CX), v(D, T), v(DI, T), v(T, D), v(2, N, DI), v(N, DI), v(T, 2 * N),
            v(2, T, LANES), v(2, 8, CX), v(8, LANES),
            v(plan.s_ring, n_dp, h, CHUNK_N), v(plan.in_ring, n_dp, h, CHUNK_N), v(plan.o_ring, n_dp, h, CHUNK_N), *received,
            v(plan.f_ring, h, CHUNK_N), v(plan.f_ring, h, CHUNK_N) if plan.wide else v(8, LANES), v(2, 8, CW),
            v(plan.w_ring, h, CHUNK_N), v(2, h, LANES), v(2, 2 * h, LANES),
            dma((J, plan.kinds + 1)), dma((J, plan.kinds + 1)), dma((plan.s_ring,)), dma((2, plan.f_ring)), dma((plan.w_ring,)), dma((6,)), dma((12,)),
            dma((3,)), dma((2,)), dma((2, DI // CHUNK_N + 1)), dma((2, DI // CHUNK_N + 1)), dma((2, DI // 256)), dma((2, DI // 256)),
        ],
        compiler_params=pltpu.CompilerParams(
            collective_id=1, has_side_effects=True, vmem_limit_bytes=61 << 20
        ),
        name="backward",
    )(cot, mask, conv, head, norm, gated, *saved)


def on_device(hidden, cotangent, lengths, norm_gain, gate_weight, mix_weight, step_weight, conv_kernel, conv_bias,
              gated_gain, out_weight, skip_gain, log_rate, step_bias):
    n_dp, n_seq = lax.axis_size("dp"), lax.axis_size("seq")
    slots, T, D = hidden.shape
    DI, CW, H, K = gate_weight.shape[2], mix_weight.shape[2], skip_gain.shape[1], conv_kernel.shape[1]
    dims = (T, D, DI, CW, H, DI // H, (CW - DI) // 2, K)
    plan = Plan(n_dp, n_seq, dims)
    mask, conv, head, norm, gated, step_pad = prepare(
        hidden, lengths, norm_gain, gate_weight, mix_weight, step_weight, conv_kernel, conv_bias, gated_gain,
        out_weight, skip_gain, log_rate, step_bias, n_dp,
    )
    x = hidden[0]
    result, conv_full, *saved = forward(
        x, mask, conv, head, norm, gated, mix_weight, gate_weight, out_weight, step_pad, n_dp, n_seq, dims
    )
    hidden_grad, gm, gs, gg, go, gc, norm_sum, gated_sum = backward(
        cotangent[0], mask, conv_full, head, norm, gated, (x, *saved), n_dp, n_seq, dims
    )
    norm_gain_grad = jnp.sum(norm_sum, axis=-1).transpose(1, 0, 2).reshape(norm_gain.shape) / norm_gain
    gated_gain_grad = jnp.sum(gated_sum, axis=-1).transpose(1, 0, 2).reshape(gated_gain.shape) / gated_gain
    blocks = gc[:, 0].reshape(-1, 8, CHUNK_N)[: plan.blocks]
    blocks = blocks.reshape(2, plan.mix_jobs, 8, CHUNK_N).transpose(0, 2, 1, 3).reshape(2, 8, CW + LANES)[::-1]
    shard = conv_bias.shape[1]
    own = lax.dynamic_slice(blocks, (0, 0, lax.axis_index("dp") * shard), (2, 8, shard))
    skip_grad = blocks[:, 0, CW : CW + H]
    return (
        result[None], hidden_grad[None], norm_gain_grad, gg, gm, gs[:, :, :H], own[:, :K], own[:, K],
        gated_gain_grad, go, skip_grad,
    )


def solution(mesh):
    return jax.shard_map(
        on_device,
        mesh=mesh,
        in_specs=(
            P("dp", "seq", None), P("dp", "seq", None), P("dp"), P(None, "dp"), P(None, "dp", None),
            P(None, "dp", None), P(None, "dp", None), P(None, None, "dp"), P(None, "dp"), P(None, "dp"),
            P(None, "dp", None), P(), P(), P(),
        ),
        out_specs=(
            P("dp", "seq", None), P("dp", "seq", None), P(None, "dp"), P(None, "dp", None), P(None, "dp", None),
            P(None, "dp", None), P(None, None, "dp"), P(None, "dp"), P(None, "dp"), P(None, "dp", None), P(),
        ),
        check_vma=False,
    )
```
